32 devices in a mesh: groups: 2 (over y), expert: 16 (over z, x, core).
Axes of the slice: x: 2, y: 2, z: 4, core: 2. Of those that a mesh axis runs over, the one named last changes fastest.
Arguments:
- activations: bfloat16 [2, 512, 2048], P(None, ('groups', 'expert')), parts along dimension 1, may hold values from -6 to 6
- pick_weight: float32 [2, 512, 1], P(None, ('groups', 'expert')), parts along dimension 1, may hold values from 0.2 to 1
- expert_ids: int32 [2, 512, 1], P(None, ('groups', 'expert')), parts along dimension 1, may hold values from 0 to 7, as said below
- replica: int32 [2, 512, 1], P(None, ('groups', 'expert')), parts along dimension 1, may hold values from 0 to 4, as said below
- old_home: int32 [8], replicated, may hold values from 0 to 7, each once
- new_expert: int32 [32], P('groups'), parts along dimension 0, may hold values from 0 to 7, as said below
- gate_panel: bfloat16 [16, 2048, 384], P('expert'), may hold values from -0.125 to 0.125
- up_panel: bfloat16 [16, 2048, 384], P('expert'), may hold values from -0.125 to 0.125
- down_panel: bfloat16 [16, 2048, 384], P('expert'), may hold values from -0.21875 to 0.21875
Outputs:
- layer_output: bfloat16 [2, 512, 2048], P(None, ('groups', 'expert')), parts along dimension 1
- slot_load: int32 [32], P(('groups', 'expert')), parts along dimension 0
The draws below stay inside these ranges and needn't reach their ends.
There are 2 independent parts, one for each index of `groups`. The reference program is written for one: setup_inputs(seed, part) draws one part's arguments, and reference() takes and returns one part's arrays. A program takes and returns all parts, laid end to end along the dimension named above; an argument that names none is the same for every part. Nothing has to cross between parts.
Inputs may be any that keep to these rules, and one draw needn't show every extreme that they name: `new_expert`: every expert is held by 1 or 5 slots. `expert_ids`: the 1 expert that a token names are different. replica[s, t, k] is below the number of slots that new_expert gives to expert_ids[s, t, k]. The picks of the 16 tokens of one device in one batch that land on one slot number at most 2, and in each batch some slot receives exactly 2 from every device.
All inputs are finite; a program needn't handle non-finite values.
Results may differ from the reference program's by a relative error of at most 0.0057.
Values may be sent and summed in bfloat16 or wider, within the bound.
No kernel may reach another device: no remote copies, remote signals or barrier semaphores. Data moves between devices by JAX's collectives and lax.ppermute only.
A program may use at most 128 MiB of HBM per device.

```python
import math
from functools import partial
import jax
import jax.numpy as jnp
from jax import lax

D = 2048
FF = 768
HALF = 384
STEPS = 2
TOK_DEV = 16
REPL = 5
SLOTS = 16
EXPERTS = 8
HOT = 2
TOP = 1
CAP = 2
TOKENS = 256


def route_block(key, steady, hot_flags):
    keys = jax.random.split(key, 5)
    shuffled = jax.random.permutation(keys[0], EXPERTS).astype(jnp.int32)
    labels = jnp.arange(EXPERTS, dtype=jnp.int32)
    sort_key = jnp.where(shuffled == steady, -1, labels)
    order = shuffled[jnp.argsort(sort_key, stable=True)]
    hot_length = jax.random.randint(keys[1], (EXPERTS,), REPL * CAP - REPL + 1, REPL * CAP + 1, dtype=jnp.int32)
    cold_length = jax.random.randint(keys[2], (EXPERTS,), 1, CAP + 1, dtype=jnp.int32)
    length = jnp.where(hot_flags, hot_length, cold_length)
    length = jnp.where(labels == steady, CAP, length)
    spans = length[order]
    ends = jnp.cumsum(spans).astype(jnp.int32)
    starts = ends - spans
    places = jnp.arange(TOK_DEV * TOP, dtype=jnp.int32)
    which = jnp.sum((ends[None, :] <= places[:, None]).astype(jnp.int32), axis=1)
    chosen = order[which]
    offset = places - starts[which]
    turn = jax.random.randint(keys[3], (EXPERTS,), 0, REPL, dtype=jnp.int32)
    copy_rank = jnp.where(hot_flags[chosen], (offset + turn[chosen]) % REPL, 0).astype(jnp.int32)
    picked_ids = chosen.reshape(TOP, TOK_DEV).T
    picked_ranks = copy_rank.reshape(TOP, TOK_DEV).T
    token_order = jax.random.permutation(keys[4], TOK_DEV)
    return (picked_ids[token_order], picked_ranks[token_order])


def plan(key):
    keys = jax.random.split(jax.random.fold_in(key, 4242), 3)
    shuffled = jax.random.permutation(keys[0], EXPERTS).astype(jnp.int32)
    listed = jnp.concatenate([shuffled] + [shuffled[:HOT]] * (REPL - 1))
    new_expert = listed[jax.random.permutation(keys[1], SLOTS)].astype(jnp.int32)
    labels = jnp.arange(EXPERTS, dtype=jnp.int32)
    hot_flags = jnp.any(labels[:, None] == shuffled[None, :HOT], axis=1)
    steady = shuffled[HOT]
    block_keys = jax.random.split(keys[2], STEPS * SLOTS)
    picked_ids, picked_ranks = jax.vmap(partial(route_block, steady=steady, hot_flags=hot_flags))(block_keys)
    return (new_expert, picked_ids.reshape(STEPS, TOKENS, TOP).astype(jnp.int32), picked_ranks.reshape(STEPS, TOKENS, TOP).astype(jnp.int32))


def draw_new_expert(key, part):
    return plan(key)[0]


def draw_expert_ids(key, part):
    return plan(key)[1]


def draw_replica(key, part):
    return plan(key)[2]


def steps_of(rng, extent, cuts, smallest, top_value):
    def one(dim, shards_of):
        heights = jax.random.uniform(jax.random.fold_in(jax.random.fold_in(rng, 6), dim), (shards_of,), jnp.float32, smallest / len(cuts), top_value / len(cuts))
        return jnp.repeat(jnp.exp(heights), extent[dim] // shards_of).reshape((-1,) + (1,) * (len(extent) - dim - 1))

    gain = one(*cuts[0])
    for cut in cuts[1:]:
        gain = gain * one(*cut)
    return gain


def normal_values(stream_key, shape, width, bound, cuts=(), kind=jnp.bfloat16):
    array = jax.random.normal(stream_key, shape, jnp.float32) * width
    if len(cuts) > 0:
        array = steps_of(stream_key, shape, cuts, -0.22, 0.18) * array
    return jnp.clip(array, min=-bound, max=bound).astype(kind)


def setup_inputs(seed: int = 0, part: int = 0) -> dict:
    key_list = jax.random.split(jax.random.key(seed), 10)
    part_keys = jax.random.split(jax.random.fold_in(key_list[9], part), 10)
    return {
        "activations": normal_values(part_keys[0], (STEPS, TOKENS, D), 1.0, 6.0, ((1, 16),)),
        "pick_weight": jnp.clip(jnp.exp(math.log(1.0) - 1.609438 * jax.random.uniform(part_keys[1], (STEPS, TOKENS, TOP), jnp.float32) ** steps_of(part_keys[1], (STEPS, TOKENS, TOP), ((1, 16),), -0.2, 0.2)), 0.2, 1.0),
        "expert_ids": draw_expert_ids(jax.random.fold_in(jax.random.fold_in(key_list[9], part), 71), part),
        "replica": draw_replica(jax.random.fold_in(jax.random.fold_in(key_list[9], part), 71), part),
        "old_home": jax.random.permutation(key_list[4], EXPERTS).astype(jnp.int32),
        "new_expert": draw_new_expert(jax.random.fold_in(jax.random.fold_in(key_list[9], part), 71), part),
        "gate_panel": normal_values(key_list[6], (SLOTS, D, HALF), D ** -0.5, 0.125, ((0, 16),)),
        "up_panel": normal_values(key_list[7], (SLOTS, D, HALF), D ** -0.5, 0.125, ((0, 16),)),
        "down_panel": normal_values(key_list[8], (SLOTS, D, HALF), FF ** -0.5, 0.21875, ((0, 16),)),
    }


def expert_weights(panel, old_home, expert):
    home = lax.dynamic_index_in_dim(old_home, expert, 0, keepdims=False)
    both = lax.dynamic_slice_in_dim(panel, (2 * home).astype(jnp.int32), 2, 0)
    return jnp.concatenate((both[0], both[1]), axis=1)


def one_batch(tokens, weights, ids, old_home, gate_panel, up_panel, down_panel):
    block = 128
    count, picks_each = ids.shape
    picks = count * picks_each
    flat_ids = ids.reshape(picks).astype(jnp.int32)
    labels = jnp.arange(EXPERTS, dtype=jnp.int32)
    counts = jnp.sum((flat_ids[:, None] == labels[None, :]).astype(jnp.int32), axis=0).astype(jnp.int32)
    starts = (jnp.cumsum(counts) - counts).astype(jnp.int32)
    blocks_of = ((counts + block - 1) // block).astype(jnp.int32)
    block_end = jnp.cumsum(blocks_of).astype(jnp.int32)
    padded_start = ((block_end - blocks_of) * block).astype(jnp.int32)
    order = jnp.argsort(flat_ids, stable=True).astype(jnp.int32)
    sorted_ids = flat_ids[order]
    rank = (jnp.arange(picks, dtype=jnp.int32) - starts[sorted_ids]).astype(jnp.int32)
    padded_pos = (padded_start[sorted_ids] + rank).astype(jnp.int32)
    total_blocks = (picks + block - 1) // block + EXPERTS
    pad_pick = jnp.full((total_blocks * block,), -1, jnp.int32).at[padded_pos].set(order)
    block_ids = jnp.arange(total_blocks, dtype=jnp.int32)
    reached = (block_ids[:, None] >= block_end[None, :]).astype(jnp.int32)
    block_expert = jnp.minimum(jnp.sum(reached, axis=1), EXPERTS - 1).astype(jnp.int32)

    def run(index):
        expert = block_expert[index]
        members = lax.dynamic_slice_in_dim(pad_pick, (index * block).astype(jnp.int32), block)
        valid = members >= 0
        token_index = jnp.where(valid, members // picks_each, 0).astype(jnp.int32)
        picked = tokens[token_index]
        gate_full = expert_weights(gate_panel, old_home, expert)
        up_full = expert_weights(up_panel, old_home, expert)
        down_full = expert_weights(down_panel, old_home, expert)
        gate = jnp.dot(picked, gate_full, preferred_element_type=jnp.float32)
        up = jnp.dot(picked, up_full, preferred_element_type=jnp.float32)
        hidden = (jax.nn.silu(gate) * up).astype(jnp.bfloat16)
        result = jnp.dot(hidden, down_full.T, preferred_element_type=jnp.float32).astype(jnp.bfloat16)
        return jnp.where(valid[:, None], result, jnp.zeros((), result.dtype))

    results = lax.map(run, block_ids)
    pick_pos = jnp.zeros((picks,), jnp.int32).at[order].set(padded_pos)
    per_pick = results.reshape(-1, tokens.shape[1])[pick_pos].reshape(count, picks_each, -1)
    total = jnp.sum(weights[:, :, None] * per_pick.astype(jnp.float32), axis=1)
    return total.astype(jnp.bfloat16)


def slot_counts(ids, replica, new_expert):
    slots = new_expert.shape[0]
    positions = jnp.arange(slots, dtype=jnp.int32)
    same = new_expert[:, None] == new_expert[None, :]
    ranks = jnp.sum((same & (positions[None, :] < positions[:, None])).astype(jnp.int32), axis=1)
    flat_ids = ids.reshape(-1)
    flat_rep = replica.reshape(-1)
    match = (new_expert[None, :] == flat_ids[:, None]) & (ranks[None, :] == flat_rep[:, None])
    return jnp.sum(match.astype(jnp.int32), axis=0).astype(jnp.int32)


def reference(activations, pick_weight, expert_ids, replica, old_home, new_expert, gate_panel, up_panel, down_panel):
    outputs = []
    slot_load = jnp.zeros((new_expert.shape[0],), jnp.int32)
    for batch in range(STEPS):
        outputs.append(one_batch(activations[batch], pick_weight[batch], expert_ids[batch], old_home, gate_panel, up_panel, down_panel))
        slot_load = slot_load + slot_counts(expert_ids[batch], replica[batch], new_expert)
    return jnp.stack(outputs, axis=0), slot_load.astype(jnp.int32)
```

```python
import jax
import jax.numpy as jnp
from jax import lax
from jax.sharding import PartitionSpec as P

LANES = 128


def slot_rank(new_expert, me):
    positions = jnp.arange(new_expert.shape[0], dtype=jnp.int32)
    mine = jnp.sum(jnp.where(positions == me, new_expert, 0))
    rank = jnp.sum(((new_expert == mine) & (positions < me)).astype(jnp.int32))
    return mine, rank


def per_device(
    activations,
    pick_weight,
    expert_ids,
    replica,
    old_home,
    new_expert,
    gate_panel,
    up_panel,
    down_panel,
):
    me = lax.axis_index("expert")
    batches, tokens, width = activations.shape
    top = expert_ids.shape[2]
    rows = batches * tokens
    x = activations.reshape(rows, width)
    picks = jnp.concatenate([expert_ids.reshape(rows, top), replica.reshape(rows, top)], axis=1)
    weights = pick_weight.reshape(rows, top)
    picks_all = lax.all_gather(picks, "expert", axis=0, tiled=True)
    weights_all = lax.all_gather(weights, "expert", axis=0, tiled=True)
    x_all = lax.all_gather(x, "expert", axis=0, tiled=True)
    ids_all = picks_all[:, :top]
    rep_all = picks_all[:, top:]
    mine, rank = slot_rank(new_expert, me)
    load = jnp.sum(((ids_all == mine) & (rep_all == rank)).astype(jnp.int32))
    labels = jnp.arange(old_home.shape[0], dtype=jnp.int32)
    held = jnp.sum(jnp.where(old_home == me // 2, labels, 0))
    scale = jnp.sum(jnp.where(ids_all == held, weights_all, 0.0), axis=1, keepdims=True)
    gate = jnp.dot(x_all, gate_panel[0], preferred_element_type=jnp.float32)
    up = jnp.dot(x_all, up_panel[0], preferred_element_type=jnp.float32)
    hidden = (jax.nn.silu(gate) * up).astype(jnp.bfloat16)
    part = lax.dot_general(
        hidden, down_panel[0], (((1,), (1,)), ((), ())), preferred_element_type=jnp.float32
    )
    part = (part * scale).astype(jnp.bfloat16)
    total = lax.psum_scatter(part, "expert", scatter_dimension=0, tiled=True)
    return total.reshape(batches, tokens, width), load.reshape(1)


def solution(mesh):
    return jax.shard_map(
        per_device,
        mesh=mesh,
        in_specs=(
            P(None, ("groups", "expert"), None),
            P(None, ("groups", "expert"), None),
            P(None, ("groups", "expert"), None),
            P(None, ("groups", "expert"), None),
            P(),
            P("groups"),
            P("expert", None, None),
            P("expert", None, None),
            P("expert", None, None),
        ),
        out_specs=(P(None, ("groups", "expert"), None), P(("groups", "expert"))),
        check_vma=False,
    )
```

```python
import functools

import jax
import jax.numpy as jnp
from jax import lax
from jax.experimental import pallas as pl
from jax.experimental.pallas import tpu as pltpu
from jax.sharding import PartitionSpec as P

CAP = 2
REPL = 5
LANES = 128
SQUARE = 4
VMEM = pltpu.VMEM
SMEM = pltpu.SMEM


def slot_rank(new_expert, me):
    positions = jnp.arange(new_expert.shape[0], dtype=jnp.int32)
    mine = jnp.sum(jnp.where(positions == me, new_expert, 0))
    rank = jnp.sum(((new_expert == mine) & (positions < me)).astype(jnp.int32))
    return mine, rank


def gathered(
    activations,
    pick_weight,
    expert_ids,
    replica,
    old_home,
    new_expert,
    gate_panel,
    up_panel,
    down_panel,
):
    me = lax.axis_index("expert")
    batches, tokens, width = activations.shape
    top = expert_ids.shape[2]
    rows = batches * tokens
    x = activations.reshape(rows, width)
    picks = jnp.concatenate([expert_ids.reshape(rows, top), replica.reshape(rows, top)], axis=1)
    weights = pick_weight.reshape(rows, top)
    picks_all = lax.all_gather(picks, "expert", axis=0, tiled=True)
    weights_all = lax.all_gather(weights, "expert", axis=0, tiled=True)
    x_all = lax.all_gather(x, "expert", axis=0, tiled=True)
    ids_all = picks_all[:, :top]
    rep_all = picks_all[:, top:]
    mine, rank = slot_rank(new_expert, me)
    load = jnp.sum(((ids_all == mine) & (rep_all == rank)).astype(jnp.int32))
    labels = jnp.arange(old_home.shape[0], dtype=jnp.int32)
    held = jnp.sum(jnp.where(old_home == me // 2, labels, 0))
    scale = jnp.sum(jnp.where(ids_all == held, weights_all, 0.0), axis=1, keepdims=True)
    gate = jnp.dot(x_all, gate_panel[0], preferred_element_type=jnp.float32)
    up = jnp.dot(x_all, up_panel[0], preferred_element_type=jnp.float32)
    hidden = (jax.nn.silu(gate) * up).astype(jnp.bfloat16)
    part = lax.dot_general(
        hidden, down_panel[0], (((1,), (1,)), ((), ())), preferred_element_type=jnp.float32
    )
    part = (part * scale).astype(jnp.bfloat16)
    total = lax.psum_scatter(part, "expert", scatter_dimension=0, tiled=True)
    return total.reshape(batches, tokens, width), load.reshape(1)


def steps(index, size, count):
    whole = jnp.zeros_like(index)
    for step in range(1, count):
        whole = whole + (index >= step * size).astype(jnp.int32)
    return whole


def pick_kernel(cap, home_ref, new_ref, x_ref, far_ref, picks_ref, far_picks_ref, *outs):
    blocks, sel_ref = outs[:SQUARE], outs[SQUARE]
    batches, tokens = picks_ref.shape[0] // 2, picks_ref.shape[1]
    groups = 2 * batches
    count = groups * tokens
    high = groups * cap
    chip = lax.axis_index("expert") // 2
    slots = new_ref.shape[0]

    spread = (
        lax.broadcasted_iota(jnp.int32, (tokens, count), 1)
        - tokens * steps(lax.broadcasted_iota(jnp.int32, (tokens, count), 1), tokens, groups)
        == lax.broadcasted_iota(jnp.int32, (tokens, count), 0)
    ).astype(jnp.float32)
    lane = lax.broadcasted_iota(jnp.int32, (groups, count), 1)
    own_lane = steps(lane, tokens, groups) == lax.broadcasted_iota(jnp.int32, (groups, count), 0)

    def row_of(near, far):
        both = jnp.concatenate([near, far], axis=0).astype(jnp.float32)
        wide = jnp.dot(both, spread, preferred_element_type=jnp.float32)
        return jnp.sum(jnp.where(own_lane, wide, 0.0), axis=0, keepdims=True).astype(jnp.int32)

    ids = row_of(picks_ref[:batches, :], far_picks_ref[:batches, :])
    reps = row_of(picks_ref[batches:, :], far_picks_ref[batches:, :])
    target = jnp.zeros_like(ids)
    for expert in range(home_ref.shape[0]):
        target = jnp.where(ids == expert, home_ref[expert], target)

    sub = lax.broadcasted_iota(jnp.int32, (8, count), 0)
    inside = (target == (sub ^ chip)) & (sub < SQUARE)
    before_from = lax.broadcasted_iota(jnp.int32, (count, count), 0)
    before_to = lax.broadcasted_iota(jnp.int32, (count, count), 1)
    before = (before_from < before_to) & (
        steps(before_from, tokens, groups) == steps(before_to, tokens, groups)
    )
    earlier = jnp.dot(
        inside.astype(jnp.bfloat16),
        before.astype(jnp.bfloat16),
        preferred_element_type=jnp.float32,
    )
    position = jnp.sum(jnp.where(inside, earlier, 0.0), axis=0, keepdims=True).astype(jnp.int32)

    row = lax.broadcasted_iota(jnp.int32, (SQUARE * high, count), 0)
    peer = steps(row, high, SQUARE)
    left = row - high * peer
    group = steps(left, cap, groups)
    left = left - cap * group
    col = lax.broadcasted_iota(jnp.int32, (SQUARE * high, count), 1)
    sel = (
        (target == (peer ^ chip)) & (position == left) & (group == steps(col, tokens, groups))
    ).astype(jnp.bfloat16)
    sel_ref[...] = sel
    x = jnp.concatenate([x_ref[...], far_ref[...]], axis=0)
    width = x.shape[1]
    meta_lane = lax.broadcasted_iota(jnp.int32, (high, LANES), 1)
    for q in range(SQUARE):
        part = jnp.dot(
            sel[q * high : (q + 1) * high], x, preferred_element_type=jnp.float32
        ).astype(jnp.bfloat16)
        blocks[q][:, :width] = part
        meta = jnp.zeros((high, LANES), jnp.float32)
        for core in range(2):
            slot = 2 * (chip ^ q) + core
            mine = new_ref[slot]
            rank = jnp.int32(0)
            for other in range(slots):
                hit = (new_ref[other] == mine) & (slot > other)
                rank = rank + hit.astype(jnp.int32)
            load = jnp.sum(((ids == mine) & (reps == rank)).astype(jnp.float32), axis=1, keepdims=True)
            meta = jnp.where(meta_lane == core, load, meta)
        blocks[q][:, width:] = meta.astype(jnp.bfloat16)


def pick_rows(cap, home, new, x, far, picks, far_picks):
    batches, tokens = picks.shape[0] // 2, picks.shape[1]
    high = 2 * batches * cap
    width = x.shape[1]
    block = jax.ShapeDtypeStruct((high, width + LANES), jnp.bfloat16)
    sel = jax.ShapeDtypeStruct((SQUARE * high, 2 * batches * tokens), jnp.bfloat16)
    return pl.pallas_call(
        functools.partial(pick_kernel, cap),
        out_shape=[block] * SQUARE + [sel],
        in_specs=[pl.BlockSpec(memory_space=SMEM)] * 2 + [pl.BlockSpec(memory_space=VMEM)] * 4,
        out_specs=[pl.BlockSpec(memory_space=VMEM)] * (SQUARE + 1),
        cost_estimate=pl.CostEstimate(
            flops=2 * SQUARE * high * 2 * batches * tokens * width,
            bytes_accessed=4 * SQUARE * high * width,
            transcendentals=0,
        ),
    )(home, new, x, far, picks, far_picks)


def expert_kernel(depth_steps, *refs):
    blocks = refs[:SQUARE]
    gates, ups, downs = refs[SQUARE : SQUARE + 2], refs[SQUARE + 2 : SQUARE + 4], refs[SQUARE + 4 : SQUARE + 6]
    outs = refs[SQUARE + 6 : SQUARE + 6 + SQUARE]
    load_ref = refs[2 * SQUARE + 6]
    sums, hidden = refs[2 * SQUARE + 7 :]
    step = pl.program_id(0)
    high = blocks[0].shape[0]
    deep = gates[0].shape[1]
    wide = downs[0].shape[1]

    @pl.when(step < depth_steps)
    def _():
        x = jnp.concatenate(
            [block[:, pl.ds(pl.multiple_of(step * deep, deep), deep)] for block in blocks], axis=0
        )
        for index, panel in enumerate((*gates, *ups)):
            part = jnp.dot(x, panel[0], preferred_element_type=jnp.float32)

            @pl.when(step == 0)
            def _():
                sums[index] = part

            @pl.when(step > 0)
            def _():
                sums[index] += part

    @pl.when(step == depth_steps)
    def _():
        for half in range(2):
            gate = sums[half]
            value = gate / (1.0 + jnp.exp(-gate)) * sums[2 + half]
            hidden[half] = value.astype(jnp.bfloat16)
        total = jnp.zeros((8, LANES), jnp.float32)
        for block in blocks:
            total = total + block[:8, block.shape[1] - LANES :].astype(jnp.float32)
        load_ref[...] = total.astype(jnp.int32)

    @pl.when(step >= depth_steps)
    def _():
        contract = (((1,), (1,)), ((), ()))
        total = sum(
            lax.dot_general(
                hidden[half], downs[half][0], contract, preferred_element_type=jnp.float32
            )
            for half in range(2)
        ).astype(jnp.bfloat16)
        at = pl.ds(pl.multiple_of((step - depth_steps) * wide, wide), wide)
        for q in range(SQUARE):
            outs[q][:, at] = total[q * high : (q + 1) * high]


def run_expert(blocks, panels, far_panels):
    high = blocks[0].shape[0]
    width, half = panels[0].shape[1], panels[0].shape[2]
    cut = 4
    piece = width // cut
    rows = SQUARE * high
    whole = pl.BlockSpec((high, width + LANES), lambda i: (0, 0))
    front = pl.BlockSpec((1, piece, half), lambda i: (0, jnp.minimum(i, cut - 1), 0))
    back = pl.BlockSpec((1, piece, half), lambda i: (0, jnp.maximum(i - cut, 0), 0))
    return pl.pallas_call(
        functools.partial(expert_kernel, cut),
        grid=(2 * cut,),
        out_shape=[jax.ShapeDtypeStruct((high, width), jnp.bfloat16)] * SQUARE
        + [jax.ShapeDtypeStruct((8, LANES), jnp.int32)],
        in_specs=[whole] * SQUARE + [front] * 4 + [back] * 2,
        out_specs=[pl.BlockSpec((high, width), lambda i: (0, 0))] * SQUARE
        + [pl.BlockSpec((8, LANES), lambda i: (0, 0))],
        scratch_shapes=[
            VMEM((4, rows, half), jnp.float32),
            VMEM((2, rows, half), jnp.bfloat16),
        ],
        cost_estimate=pl.CostEstimate(
            flops=2 * rows * width * half * 6,
            bytes_accessed=6 * 2 * width * half + 4 * rows * width,
            transcendentals=2 * rows * half,
        ),
    )(
        *blocks,
        panels[0],
        far_panels[0],
        panels[1],
        far_panels[1],
        panels[2],
        far_panels[2],
    )


def merge_kernel(sel_ref, *refs):
    blocks, (own_ref, far_ref) = refs[:SQUARE], refs[SQUARE:]
    y = jnp.concatenate([block[...] for block in blocks], axis=0)
    total = lax.dot_general(
        sel_ref[...], y, (((0,), (0,)), ((), ())), preferred_element_type=jnp.float32
    ).astype(jnp.bfloat16)
    rows = own_ref.shape[0]
    own_ref[...] = total[:rows]
    far_ref[...] = total[rows:]


def merge_rows(sel, blocks):
    count = sel.shape[1]
    width = blocks[0].shape[1]
    return pl.pallas_call(
        merge_kernel,
        out_shape=[jax.ShapeDtypeStruct((count // 2, width), jnp.bfloat16)] * 2,
        in_specs=[pl.BlockSpec(memory_space=VMEM)] * (SQUARE + 1),
        out_specs=[pl.BlockSpec(memory_space=VMEM)] * 2,
        cost_estimate=pl.CostEstimate(
            flops=2 * sel.shape[0] * count * width,
            bytes_accessed=2 * (sel.shape[0] + count) * width,
            transcendentals=0,
        ),
    )(sel, *blocks)


def swapped(size, bits):
    return [(index, index ^ bits) for index in range(size)]


def dispatched(
    activations,
    pick_weight,
    expert_ids,
    replica,
    old_home,
    new_expert,
    gate_panel,
    up_panel,
    down_panel,
):
    size = lax.axis_size("expert")
    batches, tokens, width = activations.shape
    rows = batches * tokens
    cap = min(CAP * REPL, tokens)

    def swap(value, bits):
        return lax.ppermute(value, "expert", swapped(size, bits))

    x = activations.reshape(rows, width)
    picks = jnp.concatenate(
        [expert_ids.reshape(batches, tokens), replica.reshape(batches, tokens)], axis=0
    )
    distant = 2 * SQUARE
    x_far = swap(x, distant)
    picks_far = swap(picks, distant)
    panels = (gate_panel, up_panel, down_panel)
    panels_far = [swap(panel, 1) for panel in panels]
    *blocks, sel = pick_rows(cap, old_home, new_expert, x, x_far, picks, picks_far)
    order = (3, 2, 1)
    arrived = {0: blocks[0]}
    for q in order:
        arrived[q] = swap(blocks[q], 2 * q)
    *results, load = run_expert([arrived[q] for q in range(SQUARE)], panels, panels_far)
    returned = {0: results[0]}
    for q in order:
        returned[q] = swap(results[q], 2 * q)
    own, far = merge_rows(sel, [returned[q] for q in range(SQUARE)])
    back = swap(far, distant)
    total = (own.astype(jnp.float32) + back.astype(jnp.float32)).reshape(batches, tokens, width)
    output = (pick_weight * total).astype(jnp.bfloat16)
    core = lax.axis_index("expert") % 2
    both = load[:1] + swap(load, 1)[:1]
    place = lax.broadcasted_iota(jnp.int32, both.shape, 1)
    return output, jnp.sum(jnp.where(place == core, both, 0), axis=1)


def solution(mesh):
    chips = mesh.shape["expert"] // 2

    def per_device(*args):
        if chips == 2 * SQUARE and args[2].shape[2] == 1:
            return dispatched(*args)
        return gathered(*args)

    return jax.shard_map(
        per_device,
        mesh=mesh,
        in_specs=(
            P(None, ("groups", "expert"), None),
            P(None, ("groups", "expert"), None),
            P(None, ("groups", "expert"), None),
            P(None, ("groups", "expert"), None),
            P(),
            P("groups"),
            P("expert", None, None),
            P("expert", None, None),
            P("expert", None, None),
        ),
        out_specs=(P(None, ("groups", "expert"), None), P(("groups", "expert"))),
        check_vma=False,
    )
```

```python
import functools

import jax
import jax.numpy as jnp
from jax import lax
from jax.experimental import pallas as pl
from jax.experimental.pallas import tpu as pltpu
from jax.sharding import PartitionSpec as P

CAP = 2
REPL = 5
LANES = 128
SQUARE = 4
SMALL = 4 << 20
LARGE = 20 << 20
VMEM = pltpu.VMEM
SMEM = pltpu.SMEM


def slot_rank(new_expert, me):
    positions = jnp.arange(new_expert.shape[0], dtype=jnp.int32)
    mine = jnp.sum(jnp.where(positions == me, new_expert, 0))
    rank = jnp.sum(((new_expert == mine) & (positions < me)).astype(jnp.int32))
    return mine, rank


def gathered(
    activations,
    pick_weight,
    expert_ids,
    replica,
    old_home,
    new_expert,
    gate_panel,
    up_panel,
    down_panel,
):
    me = lax.axis_index("expert")
    batches, tokens, width = activations.shape
    top = expert_ids.shape[2]
    rows = batches * tokens
    x = activations.reshape(rows, width)
    picks = jnp.concatenate([expert_ids.reshape(rows, top), replica.reshape(rows, top)], axis=1)
    weights = pick_weight.reshape(rows, top)
    picks_all = lax.all_gather(picks, "expert", axis=0, tiled=True)
    weights_all = lax.all_gather(weights, "expert", axis=0, tiled=True)
    x_all = lax.all_gather(x, "expert", axis=0, tiled=True)
    ids_all = picks_all[:, :top]
    rep_all = picks_all[:, top:]
    mine, rank = slot_rank(new_expert, me)
    load = jnp.sum(((ids_all == mine) & (rep_all == rank)).astype(jnp.int32))
    labels = jnp.arange(old_home.shape[0], dtype=jnp.int32)
    held = jnp.sum(jnp.where(old_home == me // 2, labels, 0))
    scale = jnp.sum(jnp.where(ids_all == held, weights_all, 0.0), axis=1, keepdims=True)
    gate = jnp.dot(x_all, gate_panel[0], preferred_element_type=jnp.float32)
    up = jnp.dot(x_all, up_panel[0], preferred_element_type=jnp.float32)
    hidden = (jax.nn.silu(gate) * up).astype(jnp.bfloat16)
    part = lax.dot_general(
        hidden, down_panel[0], (((1,), (1,)), ((), ())), preferred_element_type=jnp.float32
    )
    part = (part * scale).astype(jnp.bfloat16)
    total = lax.psum_scatter(part, "expert", scatter_dimension=0, tiled=True)
    return total.reshape(batches, tokens, width), load.reshape(1)


def steps(index, size, count):
    whole = jnp.zeros_like(index)
    for step in range(1, count):
        whole = whole + (index >= step * size).astype(jnp.int32)
    return whole


def block_rows(batches, cap):
    return -(-(batches * cap + 1) // 8) * 8


def pick_kernel(cap, home_ref, new_ref, x_ref, picks_ref, *outs):
    blocks, sel_ref = outs[:SQUARE], outs[SQUARE]
    batches, tokens = picks_ref.shape[0] // 3, picks_ref.shape[1]
    count = batches * tokens
    high = block_rows(batches, cap)
    chip = lax.axis_index("expert") // 2
    slots = new_ref.shape[0]

    def batch_of(index):
        return steps(index, tokens, batches)

    col = lax.broadcasted_iota(jnp.int32, (tokens, count), 1)
    spread = col - tokens * batch_of(col) == lax.broadcasted_iota(jnp.int32, (tokens, count), 0)
    spread = spread.astype(jnp.float32)
    own_lane = batch_of(lax.broadcasted_iota(jnp.int32, (batches, count), 1))
    own_lane = own_lane == lax.broadcasted_iota(jnp.int32, (batches, count), 0)

    def row_of(values):
        wide = jnp.dot(values, spread, preferred_element_type=jnp.float32)
        return jnp.sum(jnp.where(own_lane, wide, 0.0), axis=0, keepdims=True).astype(jnp.int32)

    ids = row_of(picks_ref[:batches, :])
    reps = row_of(picks_ref[batches : 2 * batches, :])
    target = jnp.zeros_like(ids)
    for expert in range(home_ref.shape[0]):
        target = jnp.where(ids == expert, home_ref[expert], target)

    sub = lax.broadcasted_iota(jnp.int32, (8, count), 0)
    inside = (target == (sub ^ chip)) & (sub < SQUARE)
    before_from = lax.broadcasted_iota(jnp.int32, (count, count), 0)
    before_to = lax.broadcasted_iota(jnp.int32, (count, count), 1)
    before = (before_from < before_to) & (batch_of(before_from) == batch_of(before_to))
    earlier = jnp.dot(
        inside.astype(jnp.bfloat16),
        before.astype(jnp.bfloat16),
        preferred_element_type=jnp.float32,
    )
    position = jnp.sum(jnp.where(inside, earlier, 0.0), axis=0, keepdims=True).astype(jnp.int32)

    row = lax.broadcasted_iota(jnp.int32, (SQUARE * high, count), 0)
    peer = steps(row, high, SQUARE)
    left = row - high * peer
    group = steps(left, cap, batches + 1)
    left = left - cap * group
    lane = batch_of(lax.broadcasted_iota(jnp.int32, (SQUARE * high, count), 1))
    sel = ((target == (peer ^ chip)) & (position == left) & (group == lane)).astype(jnp.bfloat16)
    sel_ref[...] = sel
    x = x_ref[...]
    meta_row = lax.broadcasted_iota(jnp.int32, (high, LANES), 0) == batches * cap
    meta_lane = lax.broadcasted_iota(jnp.int32, (high, LANES), 1)
    for q in range(SQUARE):
        part = jnp.dot(sel[q * high : (q + 1) * high], x, preferred_element_type=jnp.float32)
        meta = jnp.zeros((high, LANES), jnp.float32)
        for core in range(2):
            slot = 2 * (chip ^ q) + core
            mine = new_ref[slot]
            rank = jnp.int32(0)
            for other in range(slots):
                hit = (new_ref[other] == mine) & (slot > other)
                rank = rank + hit.astype(jnp.int32)
            hits = ((ids == mine) & (reps == rank)).astype(jnp.float32)
            load = jnp.sum(hits, axis=1, keepdims=True)
            meta = jnp.where(meta_row & (meta_lane == core), load, meta)
        blocks[q][...] = part.astype(jnp.bfloat16)
        blocks[q][:, :LANES] = (part[:, :LANES] + meta).astype(jnp.bfloat16)


def pick_rows(cap, home, new, x, picks):
    batches, tokens = picks.shape[0] // 3, picks.shape[1]
    high = block_rows(batches, cap)
    count, width = x.shape
    block = jax.ShapeDtypeStruct((high, width), jnp.bfloat16)
    sel = jax.ShapeDtypeStruct((SQUARE * high, count), jnp.bfloat16)
    return pl.pallas_call(
        functools.partial(pick_kernel, cap),
        out_shape=[block] * SQUARE + [sel],
        in_specs=[pl.BlockSpec(memory_space=SMEM)] * 2 + [pl.BlockSpec(memory_space=VMEM)] * 2,
        out_specs=[pl.BlockSpec(memory_space=VMEM)] * (SQUARE + 1),
        cost_estimate=pl.CostEstimate(
            flops=2 * SQUARE * high * count * width,
            bytes_accessed=4 * SQUARE * high * width,
            transcendentals=0,
        ),
        compiler_params=pltpu.CompilerParams(vmem_limit_bytes=SMALL),
    )(home, new, x, picks)


def expert_kernel(meta, *refs):
    blocks, refs = refs[:SQUARE], refs[SQUARE:]
    gates, ups, downs, prior_ref = refs[:2], refs[2:4], refs[4:6], refs[6]
    outs, load_ref = refs[7 : 7 + SQUARE], refs[7 + SQUARE]
    high = blocks[0].shape[0]
    x = jnp.concatenate([block[...] for block in blocks], axis=0)
    contract = (((1,), (1,)), ((), ()))
    total = None
    for half in range(2):
        gate = jnp.dot(x, gates[half][0], preferred_element_type=jnp.float32)
        up = jnp.dot(x, ups[half][0], preferred_element_type=jnp.float32)
        hidden = (gate / (1.0 + jnp.exp(-gate)) * up).astype(jnp.bfloat16)
        part = lax.dot_general(
            hidden, downs[half][0], contract, preferred_element_type=jnp.float32
        )
        total = part if half == 0 else total + part
    total = total.astype(jnp.bfloat16)
    for q in range(SQUARE):
        outs[q][...] = total[q * high : (q + 1) * high]
    load = prior_ref[...]
    start = meta - meta % 8
    for block in blocks:
        load = load + block[start : start + 8, :LANES].astype(jnp.int32)
    load_ref[...] = load


def run_expert(meta, blocks, panels, far_panels, prior):
    high, width = blocks[0].shape
    half = panels[0].shape[2]
    rows = SQUARE * high
    return pl.pallas_call(
        functools.partial(expert_kernel, meta),
        out_shape=[jax.ShapeDtypeStruct((high, width), jnp.bfloat16)] * SQUARE
        + [jax.ShapeDtypeStruct(prior.shape, jnp.int32)],
        in_specs=[pl.BlockSpec(memory_space=VMEM)] * (SQUARE + 7),
        out_specs=[pl.BlockSpec(memory_space=VMEM)] * (SQUARE + 1),
        cost_estimate=pl.CostEstimate(
            flops=2 * rows * width * half * 6,
            bytes_accessed=6 * 2 * width * half + 4 * rows * width,
            transcendentals=2 * rows * half,
        ),
        compiler_params=pltpu.CompilerParams(vmem_limit_bytes=LARGE),
    )(
        *blocks,
        panels[0],
        far_panels[0],
        panels[1],
        far_panels[1],
        panels[2],
        far_panels[2],
        prior,
    )


def merged(sel_ref, picks_ref, blocks):
    batches, tokens = picks_ref.shape[0] // 3, picks_ref.shape[1]
    count = sel_ref.shape[1]
    y = jnp.concatenate([block[...] for block in blocks], axis=0)
    total = lax.dot_general(
        sel_ref[...], y, (((0,), (0,)), ((), ())), preferred_element_type=jnp.float32
    )
    lane = lax.broadcasted_iota(jnp.int32, (tokens, tokens), 0)
    same = lane == lax.broadcasted_iota(jnp.int32, (tokens, tokens), 1)
    scales = [
        jnp.sum(
            jnp.where(same, picks_ref[2 * batches + batch : 2 * batches + batch + 1, :], 0.0),
            axis=1,
            keepdims=True,
        )
        for batch in range(batches)
    ]
    return (total * jnp.concatenate(scales, axis=0)).astype(jnp.bfloat16)


def merge_far_kernel(sel_ref, picks_ref, *refs):
    refs[SQUARE][...] = merged(sel_ref, picks_ref, refs[:SQUARE])


def merge_own_kernel(meta, sel_ref, picks_ref, load_ref, load_far_ref, *refs):
    refs[SQUARE][...] = merged(sel_ref, picks_ref, refs[:SQUARE])
    core = lax.axis_index("expert") % 2
    both = load_ref[...] + load_far_ref[...]
    row = lax.broadcasted_iota(jnp.int32, both.shape, 0)
    lane = lax.broadcasted_iota(jnp.int32, both.shape, 1)
    refs[SQUARE + 1][0] = jnp.sum(jnp.where((row == meta % 8) & (lane == core), both, 0))


def merge_rows(kernel, sel, picks, loads, blocks):
    count = sel.shape[1]
    width = blocks[0].shape[1]
    shapes = [jax.ShapeDtypeStruct((count, width), jnp.bfloat16)]
    specs = [pl.BlockSpec(memory_space=VMEM)]
    if loads:
        shapes.append(jax.ShapeDtypeStruct((1,), jnp.int32))
        specs.append(pl.BlockSpec(memory_space=SMEM))
    return pl.pallas_call(
        kernel,
        out_shape=shapes,
        in_specs=[pl.BlockSpec(memory_space=VMEM)] * (SQUARE + 2 + len(loads)),
        out_specs=specs,
        cost_estimate=pl.CostEstimate(
            flops=2 * sel.shape[0] * count * width,
            bytes_accessed=2 * (sel.shape[0] + count) * width,
            transcendentals=0,
        ),
        compiler_params=pltpu.CompilerParams(vmem_limit_bytes=SMALL),
    )(sel, picks, *loads, *blocks)


def swapped(size, bits):
    return [(index, index ^ bits) for index in range(size)]


def dispatched(
    activations,
    pick_weight,
    expert_ids,
    replica,
    old_home,
    new_expert,
    gate_panel,
    up_panel,
    down_panel,
):
    size = lax.axis_size("expert")
    batches, tokens, width = activations.shape
    rows = batches * tokens
    cap = min(CAP * REPL, tokens)
    meta = batches * cap
    order = (3, 2, 1)

    def swap(value, bits):
        return lax.ppermute(value, "expert", swapped(size, bits))

    def around(blocks):
        moved = {0: blocks[0]}
        for q in order:
            moved[q] = swap(blocks[q], 2 * q)
        return [moved[q] for q in range(SQUARE)]

    x = activations.reshape(rows, width)
    picks = jnp.concatenate(
        [
            expert_ids.reshape(batches, tokens).astype(jnp.float32),
            replica.reshape(batches, tokens).astype(jnp.float32),
            pick_weight.reshape(batches, tokens),
        ],
        axis=0,
    )
    distant = 2 * SQUARE
    picks_far = swap(picks, distant)
    x_far = swap(x, distant)
    panels = (gate_panel, up_panel, down_panel)
    panels_far = [swap(panel, 1) for panel in panels]
    *blocks, sel = pick_rows(cap, old_home, new_expert, x, picks)
    blocks = around(blocks)
    *blocks_far, sel_far = pick_rows(cap, old_home, new_expert, x_far, picks_far)
    blocks_far = around(blocks_far)
    prior = jnp.zeros((8, LANES), jnp.int32)
    *results, load = run_expert(meta, blocks, panels, panels_far, prior)
    *results_far, load = run_expert(meta, blocks_far, panels, panels_far, load)
    load_far = swap(load, 1)
    results_far = around(results_far)
    results = around(results)
    (far,) = merge_rows(merge_far_kernel, sel_far, picks_far, (), results_far)
    back = swap(far, distant)
    own, slot_load = merge_rows(
        functools.partial(merge_own_kernel, meta), sel, picks, (load, load_far), results
    )
    return (own + back).reshape(batches, tokens, width), slot_load


def solution(mesh):
    chips = mesh.shape["expert"] // 2

    def per_device(*args):
        if chips == 2 * SQUARE and args[2].shape[2] == 1:
            return dispatched(*args)
        return gathered(*args)

    return jax.shard_map(
        per_device,
        mesh=mesh,
        in_specs=(
            P(None, ("groups", "expert"), None),
            P(None, ("groups", "expert"), None),
            P(None, ("groups", "expert"), None),
            P(None, ("groups", "expert"), None),
            P(),
            P("groups"),
            P("expert", None, None),
            P("expert", None, None),
            P("expert", None, None),
        ),
        out_specs=(P(None, ("groups", "expert"), None), P(("groups", "expert"))),
        check_vma=False,
    )
```

```python
import functools

import jax
import jax.numpy as jnp
from jax import lax
from jax.experimental import pallas as pl
from jax.experimental.pallas import tpu as pltpu
from jax.sharding import PartitionSpec as P


CAP = 2
REPL = 5
LANES = 128
SQUARE = 4
SMALL = 4 << 20
LARGE = 20 << 20
VMEM = pltpu.VMEM
SMEM = pltpu.SMEM
HBM = pltpu.MemorySpace.HBM
FETCH = 16 << 20


def slot_rank(new_expert, me):
    positions = jnp.arange(new_expert.shape[0], dtype=jnp.int32)
    mine = jnp.sum(jnp.where(positions == me, new_expert, 0))
    rank = jnp.sum(((new_expert == mine) & (positions < me)).astype(jnp.int32))
    return mine, rank


def gathered(
    activations,
    pick_weight,
    expert_ids,
    replica,
    old_home,
    new_expert,
    gate_panel,
    up_panel,
    down_panel,
):
    me = lax.axis_index("expert")
    batches, tokens, width = activations.shape
    top = expert_ids.shape[2]
    rows = batches * tokens
    x = activations.reshape(rows, width)
    picks = jnp.concatenate([expert_ids.reshape(rows, top), replica.reshape(rows, top)], axis=1)
    weights = pick_weight.reshape(rows, top)
    picks_all = lax.all_gather(picks, "expert", axis=0, tiled=True)
    weights_all = lax.all_gather(weights, "expert", axis=0, tiled=True)
    x_all = lax.all_gather(x, "expert", axis=0, tiled=True)
    ids_all = picks_all[:, :top]
    rep_all = picks_all[:, top:]
    mine, rank = slot_rank(new_expert, me)
    load = jnp.sum(((ids_all == mine) & (rep_all == rank)).astype(jnp.int32))
    labels = jnp.arange(old_home.shape[0], dtype=jnp.int32)
    held = jnp.sum(jnp.where(old_home == me // 2, labels, 0))
    scale = jnp.sum(jnp.where(ids_all == held, weights_all, 0.0), axis=1, keepdims=True)
    gate = jnp.dot(x_all, gate_panel[0], preferred_element_type=jnp.float32)
    up = jnp.dot(x_all, up_panel[0], preferred_element_type=jnp.float32)
    hidden = (jax.nn.silu(gate) * up).astype(jnp.bfloat16)
    part = lax.dot_general(
        hidden, down_panel[0], (((1,), (1,)), ((), ())), preferred_element_type=jnp.float32
    )
    part = (part * scale).astype(jnp.bfloat16)
    total = lax.psum_scatter(part, "expert", scatter_dimension=0, tiled=True)
    return total.reshape(batches, tokens, width), load.reshape(1)


def steps(index, size, count):
    whole = jnp.zeros_like(index)
    for step in range(1, count):
        whole = whole + (index >= step * size).astype(jnp.int32)
    return whole


def block_rows(batches, cap):
    return -(-(batches * cap + 1) // 8) * 8


def pick(cap, table, picks, x, blocks, sel_ref, experts):
    batches, tokens = picks.shape[0] // 2, picks.shape[1]
    count = batches * tokens
    high = block_rows(batches, cap)
    chip = lax.axis_index("expert") // 2

    def batch_of(index):
        return steps(index, tokens, batches)

    col = lax.broadcasted_iota(jnp.int32, (tokens, count), 1)
    spread = col - tokens * batch_of(col) == lax.broadcasted_iota(jnp.int32, (tokens, count), 0)
    spread = spread.astype(jnp.float32)
    own_lane = batch_of(lax.broadcasted_iota(jnp.int32, (batches, count), 1))
    own_lane = own_lane == lax.broadcasted_iota(jnp.int32, (batches, count), 0)

    def row_of(values):
        wide = jnp.dot(values.astype(jnp.float32), spread, preferred_element_type=jnp.float32)
        return jnp.sum(jnp.where(own_lane, wide, 0.0), axis=0, keepdims=True).astype(jnp.int32)

    ids = row_of(picks[:batches, :])
    reps = row_of(picks[batches:, :])
    target = jnp.zeros_like(ids)
    for expert in range(experts):
        target = jnp.where(ids == expert, table[0:1, expert : expert + 1], target)

    sub = lax.broadcasted_iota(jnp.int32, (8, count), 0)
    inside = (target == (sub ^ chip)) & (sub < SQUARE)
    before_from = lax.broadcasted_iota(jnp.int32, (count, count), 0)
    before_to = lax.broadcasted_iota(jnp.int32, (count, count), 1)
    before = (before_from < before_to) & (batch_of(before_from) == batch_of(before_to))
    earlier = jnp.dot(
        inside.astype(jnp.bfloat16),
        before.astype(jnp.bfloat16),
        preferred_element_type=jnp.float32,
    )
    position = jnp.sum(jnp.where(inside, earlier, 0.0), axis=0, keepdims=True).astype(jnp.int32)

    row = lax.broadcasted_iota(jnp.int32, (SQUARE * high, count), 0)
    peer = steps(row, high, SQUARE)
    left = row - high * peer
    group = steps(left, cap, batches + 1)
    left = left - cap * group
    lane = batch_of(lax.broadcasted_iota(jnp.int32, (SQUARE * high, count), 1))
    sel = ((target == (peer ^ chip)) & (position == left) & (group == lane)).astype(jnp.bfloat16)
    sel_ref[...] = sel
    meta_row = lax.broadcasted_iota(jnp.int32, (high, LANES), 0) == batches * cap
    meta_lane = lax.broadcasted_iota(jnp.int32, (high, LANES), 1)
    x = x()
    for q in range(SQUARE):
        part = jnp.dot(sel[q * high : (q + 1) * high], x, preferred_element_type=jnp.float32)
        meta = jnp.zeros((high, LANES), jnp.float32)
        for core in range(2):
            at = 2 * q + core
            hits = (ids == table[1:2, at : at + 1]) & (reps == table[2:3, at : at + 1])
            load = jnp.sum(hits.astype(jnp.float32), axis=1, keepdims=True)
            meta = jnp.where(meta_row & (meta_lane == core), load, meta)
        blocks[q][...] = part.astype(jnp.bfloat16)
        blocks[q][:, :LANES] = (part[:, :LANES] + meta).astype(jnp.bfloat16)


def pick_own_kernel(cap, home_hbm, new_hbm, x_hbm, picks_ref, *refs):
    blocks, sel_ref, table_ref = refs[:SQUARE], refs[SQUARE], refs[SQUARE + 1]
    home_ref, new_ref, x_ref, sem = refs[SQUARE + 2 :]
    copies = [
        pltpu.make_async_copy(source, target, sem.at[index])
        for index, (source, target) in enumerate(
            ((home_hbm, home_ref), (new_hbm, new_ref), (x_hbm, x_ref))
        )
    ]
    for copy in copies:
        copy.start()
    chip = lax.axis_index("expert") // 2
    slots = new_ref.shape[0]
    experts = home_ref.shape[0]
    copies[0].wait()
    copies[1].wait()
    row = lax.broadcasted_iota(jnp.int32, table_ref.shape, 0)
    lane = lax.broadcasted_iota(jnp.int32, table_ref.shape, 1)
    table = jnp.zeros(table_ref.shape, jnp.int32)
    for expert in range(experts):
        table = jnp.where((row == 0) & (lane == expert), home_ref[expert], table)
    for at in range(2 * SQUARE):
        slot = 2 * (chip ^ (at // 2)) + at % 2
        mine = new_ref[slot]
        rank = jnp.int32(0)
        for other in range(slots):
            rank = rank + ((new_ref[other] == mine) & (slot > other)).astype(jnp.int32)
        table = jnp.where((row == 1) & (lane == at), mine, table)
        table = jnp.where((row == 2) & (lane == at), rank, table)
    table_ref[...] = table

    def rows():
        copies[2].wait()
        return x_ref[...]

    pick(cap, table, picks_ref[...], rows, blocks, sel_ref, experts)


def pick_far_kernel(cap, experts, table_ref, x_ref, picks_ref, *refs):
    blocks, sel_ref = refs[:SQUARE], refs[SQUARE]
    pick(cap, table_ref[...], picks_ref[...], lambda: x_ref[...], blocks, sel_ref, experts)


def pick_shapes(cap, x, picks):
    batches = picks.shape[0] // 2
    high = block_rows(batches, cap)
    count, width = x.shape
    block = jax.ShapeDtypeStruct((high, width), jnp.bfloat16)
    sel = jax.ShapeDtypeStruct((SQUARE * high, count), jnp.bfloat16)
    cost = pl.CostEstimate(
        flops=2 * SQUARE * high * count * width, bytes_accessed=FETCH, transcendentals=0
    )
    return [block] * SQUARE + [sel], cost


def pick_own(cap, home, new, x, picks):
    shapes, cost = pick_shapes(cap, x, picks)
    return pl.pallas_call(
        functools.partial(pick_own_kernel, cap),
        out_shape=shapes + [jax.ShapeDtypeStruct((8, LANES), jnp.int32)],
        in_specs=[pl.BlockSpec(memory_space=HBM)] * 3 + [pl.BlockSpec(memory_space=VMEM)],
        out_specs=[pl.BlockSpec(memory_space=VMEM)] * (SQUARE + 2),
        scratch_shapes=[
            SMEM(home.shape, jnp.int32),
            SMEM(new.shape, jnp.int32),
            VMEM(x.shape, x.dtype),
            pltpu.SemaphoreType.DMA((3,)),
        ],
        cost_estimate=cost,
        compiler_params=pltpu.CompilerParams(vmem_limit_bytes=SMALL),
    )(home, new, x, picks)


def pick_far(cap, experts, table, x, picks):
    shapes, cost = pick_shapes(cap, x, picks)
    return pl.pallas_call(
        functools.partial(pick_far_kernel, cap, experts),
        out_shape=shapes,
        in_specs=[pl.BlockSpec(memory_space=VMEM)] * 3,
        out_specs=[pl.BlockSpec(memory_space=VMEM)] * (SQUARE + 1),
        cost_estimate=cost,
        compiler_params=pltpu.CompilerParams(vmem_limit_bytes=SMALL),
    )(table, x, picks)


def expert_kernel(meta, *refs):
    blocks, refs = refs[:SQUARE], refs[SQUARE:]
    gates, ups, downs, prior_ref = refs[:2], refs[2:4], refs[4:6], refs[6]
    outs, load_ref = refs[7 : 7 + SQUARE], refs[7 + SQUARE]
    high = blocks[0].shape[0]
    x = jnp.concatenate([block[...] for block in blocks], axis=0)
    contract = (((1,), (1,)), ((), ()))
    total = None
    for half in range(2):
        gate = jnp.dot(x, gates[half][0], preferred_element_type=jnp.float32)
        up = jnp.dot(x, ups[half][0], preferred_element_type=jnp.float32)
        hidden = (gate / (1.0 + jnp.exp(-gate)) * up).astype(jnp.bfloat16)
        part = lax.dot_general(
            hidden, downs[half][0], contract, preferred_element_type=jnp.float32
        )
        total = part if half == 0 else total + part
    total = total.astype(jnp.bfloat16)
    for q in range(SQUARE):
        outs[q][...] = total[q * high : (q + 1) * high]
    load = prior_ref[...]
    start = meta - meta % 8
    for block in blocks:
        load = load + block[start : start + 8, :LANES].astype(jnp.int32)
    load_ref[...] = load


def run_expert(meta, blocks, panels, far_panels, prior):
    high, width = blocks[0].shape
    half = panels[0].shape[2]
    rows = SQUARE * high
    return pl.pallas_call(
        functools.partial(expert_kernel, meta),
        out_shape=[jax.ShapeDtypeStruct((high, width), jnp.bfloat16)] * SQUARE
        + [jax.ShapeDtypeStruct(prior.shape, jnp.int32)],
        in_specs=[pl.BlockSpec(memory_space=VMEM)] * (SQUARE + 7),
        out_specs=[pl.BlockSpec(memory_space=VMEM)] * (SQUARE + 1),
        cost_estimate=pl.CostEstimate(
            flops=2 * rows * width * half * 6,
            bytes_accessed=6 * 2 * width * half + 4 * rows * width,
            transcendentals=2 * rows * half,
        ),
        compiler_params=pltpu.CompilerParams(vmem_limit_bytes=LARGE),
    )(
        *blocks,
        panels[0],
        far_panels[0],
        panels[1],
        far_panels[1],
        panels[2],
        far_panels[2],
        prior,
    )


def chosen(sel_ref, blocks):
    y = jnp.concatenate([block[...] for block in blocks], axis=0)
    return lax.dot_general(
        sel_ref[...], y, (((0,), (0,)), ((), ())), preferred_element_type=jnp.float32
    )


def merge_kernel(sel_ref, *refs):
    refs[SQUARE][...] = chosen(sel_ref, refs[:SQUARE]).astype(jnp.bfloat16)


def final_kernel(meta, sel_ref, weight_ref, back_ref, load_ref, load_far_ref, *refs):
    out_ref, slot_ref = refs[SQUARE], refs[SQUARE + 1]
    core = lax.axis_index("expert") % 2
    both = load_ref[...] + load_far_ref[...]
    row = lax.broadcasted_iota(jnp.int32, both.shape, 0)
    lane = lax.broadcasted_iota(jnp.int32, both.shape, 1)
    slot_ref[0] = jnp.sum(jnp.where((row == meta % 8) & (lane == core), both, 0))
    batches, tokens = weight_ref.shape
    total = chosen(sel_ref, refs[:SQUARE]) + back_ref[...].astype(jnp.float32)
    lane = lax.broadcasted_iota(jnp.int32, (tokens, tokens), 0)
    same = lane == lax.broadcasted_iota(jnp.int32, (tokens, tokens), 1)
    scale = jnp.concatenate(
        [
            jnp.sum(
                jnp.where(same, weight_ref[batch : batch + 1, :], 0.0), axis=1, keepdims=True
            )
            for batch in range(batches)
        ],
        axis=0,
    )
    out_ref[...] = (total * scale).astype(jnp.bfloat16)


def merge_rows(kernel, sel, others, blocks, loads):
    count = sel.shape[1]
    width = blocks[0].shape[1]
    shapes = [jax.ShapeDtypeStruct((count, width), jnp.bfloat16)]
    specs = [pl.BlockSpec(memory_space=VMEM)]
    if loads:
        shapes.append(jax.ShapeDtypeStruct((1,), jnp.int32))
        specs.append(pl.BlockSpec(memory_space=SMEM))
    return pl.pallas_call(
        kernel,
        out_shape=shapes,
        in_specs=[pl.BlockSpec(memory_space=VMEM)] * (SQUARE + 1 + len(others)),
        out_specs=specs,
        cost_estimate=pl.CostEstimate(
            flops=2 * sel.shape[0] * count * width,
            bytes_accessed=2 * (sel.shape[0] + count) * width,
            transcendentals=0,
        ),
        compiler_params=pltpu.CompilerParams(vmem_limit_bytes=SMALL),
    )(sel, *others, *blocks)


def swapped(size, bits):
    return [(index, index ^ bits) for index in range(size)]


def dispatched(
    activations,
    pick_weight,
    expert_ids,
    replica,
    old_home,
    new_expert,
    gate_panel,
    up_panel,
    down_panel,
):
    size = lax.axis_size("expert")
    batches, tokens, width = activations.shape
    rows = batches * tokens
    cap = min(CAP * REPL, tokens)
    meta = batches * cap
    distant = 2 * SQUARE

    def swap(value, bits):
        return lax.ppermute(value, "expert", swapped(size, bits))

    def around(blocks):
        return [blocks[0]] + [swap(blocks[q], 2 * q) for q in range(1, SQUARE)]

    x = activations.reshape(rows, width)
    x_far = swap(x, distant)
    picks = jnp.concatenate(
        [expert_ids.reshape(batches, tokens), replica.reshape(batches, tokens)], axis=0
    )
    picks_far = swap(picks, distant)
    panels = (gate_panel, up_panel, down_panel)
    panels_far = [swap(panel, 1) for panel in panels]
    *blocks, sel, table = pick_own(cap, old_home, new_expert, x, picks)
    blocks = around(blocks)
    *blocks_far, sel_far = pick_far(cap, old_home.shape[0], table, x_far, picks_far)
    blocks_far = around(blocks_far)
    prior = jnp.zeros((8, LANES), jnp.int32)
    *results, load = run_expert(meta, blocks, panels, panels_far, prior)
    *results_far, load = run_expert(meta, blocks_far, panels, panels_far, load)
    results_far = around(results_far)
    results = around(results)
    load_far = swap(load, 1)
    (far,) = merge_rows(merge_kernel, sel_far, (), results_far, False)
    back = swap(far, distant)
    weight = pick_weight.reshape(batches, tokens)
    output, slot_load = merge_rows(
        functools.partial(final_kernel, meta),
        sel,
        (weight, back, load, load_far),
        results,
        True,
    )
    return output.reshape(batches, tokens, width), slot_load


def solution(mesh):
    chips = mesh.shape["expert"] // 2

    def per_device(*args):
        if direct(args):
            return dispatched(*args)
        return gathered(*args)

    def direct(args):
        return chips == 2 * SQUARE and args[2].shape[2] == 1

    return jax.shard_map(
        per_device,
        mesh=mesh,
        in_specs=(
            P(None, ("groups", "expert"), None),
            P(None, ("groups", "expert"), None),
            P(None, ("groups", "expert"), None),
            P(None, ("groups", "expert"), None),
            P(),
            P("groups"),
            P("expert", None, None),
            P("expert", None, None),
            P("expert", None, None),
        ),
        out_specs=(P(None, ("groups", "expert"), None), P(("groups", "expert"))),
        check_vma=False,
    )
```

```python
import functools

import jax
import jax.numpy as jnp
from jax import lax
from jax.experimental import pallas as pl
from jax.experimental.pallas import tpu as pltpu
from jax.sharding import PartitionSpec as P


CAP = 2
REPL = 5
LANES = 128
SQUARE = 4
SMALL = 4 << 20
LARGE = 20 << 20
VMEM = pltpu.VMEM
SMEM = pltpu.SMEM
HBM = pltpu.MemorySpace.HBM


def slot_rank(new_expert, me):
    positions = jnp.arange(new_expert.shape[0], dtype=jnp.int32)
    mine = jnp.sum(jnp.where(positions == me, new_expert, 0))
    rank = jnp.sum(((new_expert == mine) & (positions < me)).astype(jnp.int32))
    return mine, rank


def gathered(
    activations,
    pick_weight,
    expert_ids,
    replica,
    old_home,
    new_expert,
    gate_panel,
    up_panel,
    down_panel,
):
    me = lax.axis_index("expert")
    batches, tokens, width = activations.shape
    top = expert_ids.shape[2]
    rows = batches * tokens
    x = activations.reshape(rows, width)
    picks = jnp.concatenate([expert_ids.reshape(rows, top), replica.reshape(rows, top)], axis=1)
    weights = pick_weight.reshape(rows, top)
    picks_all = lax.all_gather(picks, "expert", axis=0, tiled=True)
    weights_all = lax.all_gather(weights, "expert", axis=0, tiled=True)
    x_all = lax.all_gather(x, "expert", axis=0, tiled=True)
    ids_all = picks_all[:, :top]
    rep_all = picks_all[:, top:]
    mine, rank = slot_rank(new_expert, me)
    load = jnp.sum(((ids_all == mine) & (rep_all == rank)).astype(jnp.int32))
    labels = jnp.arange(old_home.shape[0], dtype=jnp.int32)
    held = jnp.sum(jnp.where(old_home == me // 2, labels, 0))
    scale = jnp.sum(jnp.where(ids_all == held, weights_all, 0.0), axis=1, keepdims=True)
    gate = jnp.dot(x_all, gate_panel[0], preferred_element_type=jnp.float32)
    up = jnp.dot(x_all, up_panel[0], preferred_element_type=jnp.float32)
    hidden = (jax.nn.silu(gate) * up).astype(jnp.bfloat16)
    part = lax.dot_general(
        hidden, down_panel[0], (((1,), (1,)), ((), ())), preferred_element_type=jnp.float32
    )
    part = (part * scale).astype(jnp.bfloat16)
    total = lax.psum_scatter(part, "expert", scatter_dimension=0, tiled=True)
    return total.reshape(batches, tokens, width), load.reshape(1)


def steps(index, size, count):
    whole = jnp.zeros_like(index)
    for step in range(1, count):
        whole = whole + (index >= step * size).astype(jnp.int32)
    return whole


def block_rows(batches, cap):
    return -(-(batches * cap + 1) // 8) * 8


def pick(cap, table, picks, x, blocks, sel_ref, experts):
    batches, tokens = picks.shape[0] // 2, picks.shape[1]
    count = batches * tokens
    high = block_rows(batches, cap)
    chip = lax.axis_index("expert") // 2

    def batch_of(index):
        return steps(index, tokens, batches)

    col = lax.broadcasted_iota(jnp.int32, (tokens, count), 1)
    spread = col - tokens * batch_of(col) == lax.broadcasted_iota(jnp.int32, (tokens, count), 0)
    spread = spread.astype(jnp.float32)
    own_lane = batch_of(lax.broadcasted_iota(jnp.int32, (batches, count), 1))
    own_lane = own_lane == lax.broadcasted_iota(jnp.int32, (batches, count), 0)

    def row_of(values):
        wide = jnp.dot(values.astype(jnp.float32), spread, preferred_element_type=jnp.float32)
        return jnp.sum(jnp.where(own_lane, wide, 0.0), axis=0, keepdims=True).astype(jnp.int32)

    ids = row_of(picks[:batches, :])
    reps = row_of(picks[batches:, :])
    target = jnp.zeros_like(ids)
    for expert in range(experts):
        target = jnp.where(ids == expert, table[0:1, expert : expert + 1], target)

    sub = lax.broadcasted_iota(jnp.int32, (8, count), 0)
    inside = (target == (sub ^ chip)) & (sub < SQUARE)
    before_from = lax.broadcasted_iota(jnp.int32, (count, count), 0)
    before_to = lax.broadcasted_iota(jnp.int32, (count, count), 1)
    before = (before_from < before_to) & (batch_of(before_from) == batch_of(before_to))
    earlier = jnp.dot(
        inside.astype(jnp.bfloat16),
        before.astype(jnp.bfloat16),
        preferred_element_type=jnp.float32,
    )
    position = jnp.sum(jnp.where(inside, earlier, 0.0), axis=0, keepdims=True).astype(jnp.int32)

    row = lax.broadcasted_iota(jnp.int32, (SQUARE * high, count), 0)
    peer = steps(row, high, SQUARE)
    left = row - high * peer
    group = steps(left, cap, batches + 1)
    left = left - cap * group
    lane = batch_of(lax.broadcasted_iota(jnp.int32, (SQUARE * high, count), 1))
    sel = ((target == (peer ^ chip)) & (position == left) & (group == lane)).astype(jnp.bfloat16)
    sel_ref[...] = sel
    meta_row = lax.broadcasted_iota(jnp.int32, (high, LANES), 0) == batches * cap
    meta_lane = lax.broadcasted_iota(jnp.int32, (high, LANES), 1)
    x = x()
    for q in range(SQUARE):
        part = jnp.dot(sel[q * high : (q + 1) * high], x, preferred_element_type=jnp.float32)
        meta = jnp.zeros((high, LANES), jnp.float32)
        for core in range(2):
            at = 2 * q + core
            hits = (ids == table[1:2, at : at + 1]) & (reps == table[2:3, at : at + 1])
            load = jnp.sum(hits.astype(jnp.float32), axis=1, keepdims=True)
            meta = jnp.where(meta_row & (meta_lane == core), load, meta)
        blocks[q][...] = part.astype(jnp.bfloat16)
        blocks[q][:, :LANES] = (part[:, :LANES] + meta).astype(jnp.bfloat16)


def pick_own_kernel(cap, home_hbm, new_hbm, x_hbm, picks_ref, *refs):
    blocks, sel_ref, table_ref = refs[:SQUARE], refs[SQUARE], refs[SQUARE + 1]
    home_ref, new_ref, x_ref, sem = refs[SQUARE + 2 :]
    copies = [
        pltpu.make_async_copy(source, target, sem.at[index])
        for index, (source, target) in enumerate(
            ((home_hbm, home_ref), (new_hbm, new_ref), (x_hbm, x_ref))
        )
    ]
    for copy in copies:
        copy.start()
    chip = lax.axis_index("expert") // 2
    slots = new_ref.shape[0]
    experts = home_ref.shape[0]
    copies[0].wait()
    copies[1].wait()
    row = lax.broadcasted_iota(jnp.int32, table_ref.shape, 0)
    lane = lax.broadcasted_iota(jnp.int32, table_ref.shape, 1)
    table = jnp.zeros(table_ref.shape, jnp.int32)
    for expert in range(experts):
        table = jnp.where((row == 0) & (lane == expert), home_ref[expert], table)
    for at in range(2 * SQUARE):
        slot = 2 * (chip ^ (at // 2)) + at % 2
        mine = new_ref[slot]
        rank = jnp.int32(0)
        for other in range(slots):
            rank = rank + ((new_ref[other] == mine) & (slot > other)).astype(jnp.int32)
        table = jnp.where((row == 1) & (lane == at), mine, table)
        table = jnp.where((row == 2) & (lane == at), rank, table)
    table_ref[...] = table

    def rows():
        copies[2].wait()
        return x_ref[...]

    pick(cap, table, picks_ref[...], rows, blocks, sel_ref, experts)


def pick_far_kernel(cap, experts, table_ref, x_ref, picks_ref, *refs):
    blocks, sel_ref = refs[:SQUARE], refs[SQUARE]
    pick(cap, table_ref[...], picks_ref[...], lambda: x_ref[...], blocks, sel_ref, experts)


def pick_shapes(cap, x, picks):
    batches = picks.shape[0] // 2
    high = block_rows(batches, cap)
    count, width = x.shape
    block = jax.ShapeDtypeStruct((high, width), jnp.bfloat16)
    sel = jax.ShapeDtypeStruct((SQUARE * high, count), jnp.bfloat16)
    cost = pl.CostEstimate(
        flops=2 * SQUARE * high * count * width,
        bytes_accessed=4 * SQUARE * high * width,
        transcendentals=0,
    )
    return [block] * SQUARE + [sel], cost


def pick_own(cap, home, new, x, picks):
    shapes, cost = pick_shapes(cap, x, picks)
    return pl.pallas_call(
        functools.partial(pick_own_kernel, cap),
        out_shape=shapes + [jax.ShapeDtypeStruct((8, LANES), jnp.int32)],
        in_specs=[pl.BlockSpec(memory_space=HBM)] * 3 + [pl.BlockSpec(memory_space=VMEM)],
        out_specs=[pl.BlockSpec(memory_space=VMEM)] * (SQUARE + 2),
        scratch_shapes=[
            SMEM(home.shape, jnp.int32),
            SMEM(new.shape, jnp.int32),
            VMEM(x.shape, x.dtype),
            pltpu.SemaphoreType.DMA((3,)),
        ],
        cost_estimate=cost,
        compiler_params=pltpu.CompilerParams(vmem_limit_bytes=SMALL),
    )(*(pltpu.with_memory_space_constraint(value, HBM) for value in (home, new, x)), picks)


def pick_far(cap, experts, table, x, picks):
    shapes, cost = pick_shapes(cap, x, picks)
    return pl.pallas_call(
        functools.partial(pick_far_kernel, cap, experts),
        out_shape=shapes,
        in_specs=[pl.BlockSpec(memory_space=VMEM)] * 3,
        out_specs=[pl.BlockSpec(memory_space=VMEM)] * (SQUARE + 1),
        cost_estimate=cost,
        compiler_params=pltpu.CompilerParams(vmem_limit_bytes=SMALL),
    )(table, x, picks)


def expert_kernel(meta, count, *refs):
    blocks, refs = refs[:count], refs[count:]
    panels_hbm, panels_far, refs = refs[:3], refs[3:6], refs[6:]
    outs, load_ref, panels, sem = refs[:count], refs[count], refs[count + 1 : count + 4], refs[count + 4]
    copies = [
        pltpu.make_async_copy(source, target, sem.at[index])
        for index, (source, target) in enumerate(zip(panels_hbm, panels))
    ]
    for copy in copies:
        copy.start()
    high = blocks[0].shape[0]
    x = jnp.concatenate([block[...] for block in blocks], axis=0)
    contract = (((1,), (1,)), ((), ()))
    start = meta - meta % 8
    load = jnp.zeros(load_ref.shape, jnp.float32)
    for block in blocks:
        load = load + block[start : start + 8, :LANES].astype(jnp.float32)
    load_ref[...] = load.astype(jnp.int32)

    def half(gate_ref, up_ref, down_ref, ready):
        ready(0)
        ready(1)
        gate = jnp.dot(x, gate_ref[0], preferred_element_type=jnp.float32)
        up = jnp.dot(x, up_ref[0], preferred_element_type=jnp.float32)
        hidden = (gate / (1.0 + jnp.exp(-gate)) * up).astype(jnp.bfloat16)
        ready(2)
        return lax.dot_general(hidden, down_ref[0], contract, preferred_element_type=jnp.float32)

    total = half(*panels_far, lambda index: None)
    total = total + half(*panels, lambda index: copies[index].wait())
    total = total.astype(jnp.bfloat16)
    for q in range(count):
        outs[q][...] = total[q * high : (q + 1) * high]


def run_expert(meta, blocks, panels, panels_far):
    high, width = blocks[0].shape
    half = panels[0].shape[2]
    count = len(blocks)
    rows = count * high
    held = [pltpu.with_memory_space_constraint(panel, HBM) for panel in panels]
    return pl.pallas_call(
        functools.partial(expert_kernel, meta, count),
        out_shape=[jax.ShapeDtypeStruct((high, width), jnp.bfloat16)] * count
        + [jax.ShapeDtypeStruct((8, LANES), jnp.int32)],
        in_specs=[pl.BlockSpec(memory_space=VMEM)] * count
        + [pl.BlockSpec(memory_space=HBM)] * 3
        + [pl.BlockSpec(memory_space=VMEM)] * 3,
        out_specs=[pl.BlockSpec(memory_space=VMEM)] * (count + 1),
        scratch_shapes=[VMEM(panel.shape, panel.dtype) for panel in panels]
        + [pltpu.SemaphoreType.DMA((3,))],
        cost_estimate=pl.CostEstimate(
            flops=2 * rows * width * half * 6,
            bytes_accessed=6 * 2 * width * half + 4 * rows * width,
            transcendentals=2 * rows * half,
        ),
        compiler_params=pltpu.CompilerParams(vmem_limit_bytes=LARGE),
    )(*blocks, *held, *panels_far)


def chosen(sel_ref, blocks):
    y = jnp.concatenate([block[...] for block in blocks], axis=0)
    return lax.dot_general(
        sel_ref[...], y, (((0,), (0,)), ((), ())), preferred_element_type=jnp.float32
    )


def merge_kernel(sel_ref, *refs):
    refs[SQUARE][...] = chosen(sel_ref, refs[:SQUARE]).astype(jnp.bfloat16)


def final_kernel(meta, sel_ref, weight_ref, back_ref, load_ref, load_far_ref, *refs):
    out_ref, slot_ref = refs[SQUARE], refs[SQUARE + 1]
    core = lax.axis_index("expert") % 2
    both = load_ref[...] + load_far_ref[...]
    row = lax.broadcasted_iota(jnp.int32, both.shape, 0)
    lane = lax.broadcasted_iota(jnp.int32, both.shape, 1)
    slot_ref[0] = jnp.sum(jnp.where((row == meta % 8) & (lane == core), both, 0))
    batches, tokens = weight_ref.shape
    total = chosen(sel_ref, refs[:SQUARE]) + back_ref[...].astype(jnp.float32)
    lane = lax.broadcasted_iota(jnp.int32, (tokens, tokens), 0)
    same = lane == lax.broadcasted_iota(jnp.int32, (tokens, tokens), 1)
    scale = jnp.concatenate(
        [
            jnp.sum(
                jnp.where(same, weight_ref[batch : batch + 1, :], 0.0), axis=1, keepdims=True
            )
            for batch in range(batches)
        ],
        axis=0,
    )
    out_ref[...] = (total * scale).astype(jnp.bfloat16)


def merge_rows(kernel, sel, others, blocks, loads):
    count = sel.shape[1]
    width = blocks[0].shape[1]
    shapes = [jax.ShapeDtypeStruct((count, width), jnp.bfloat16)]
    specs = [pl.BlockSpec(memory_space=VMEM)]
    if loads:
        shapes.append(jax.ShapeDtypeStruct((1,), jnp.int32))
        specs.append(pl.BlockSpec(memory_space=SMEM))
    return pl.pallas_call(
        kernel,
        out_shape=shapes,
        in_specs=[pl.BlockSpec(memory_space=VMEM)] * (SQUARE + 1 + len(others)),
        out_specs=specs,
        cost_estimate=pl.CostEstimate(
            flops=2 * sel.shape[0] * count * width,
            bytes_accessed=2 * (sel.shape[0] + count) * width,
            transcendentals=0,
        ),
        compiler_params=pltpu.CompilerParams(vmem_limit_bytes=SMALL),
    )(sel, *others, *blocks)


def swapped(size, bits):
    return [(index, index ^ bits) for index in range(size)]


def dispatched(
    activations,
    pick_weight,
    expert_ids,
    replica,
    old_home,
    new_expert,
    gate_panel,
    up_panel,
    down_panel,
):
    size = lax.axis_size("expert")
    batches, tokens, width = activations.shape
    rows = batches * tokens
    cap = min(CAP * REPL, tokens)
    meta = batches * cap
    distant = 2 * SQUARE

    def swap(value, bits):
        return lax.ppermute(value, "expert", swapped(size, bits))

    def around(blocks):
        return [blocks[0]] + [swap(blocks[q], 2 * q) for q in range(1, SQUARE)]

    x = activations.reshape(rows, width)
    x_far = swap(x, distant)
    picks = jnp.concatenate(
        [expert_ids.reshape(batches, tokens), replica.reshape(batches, tokens)], axis=0
    )
    picks_far = swap(picks, distant)
    panels = (gate_panel, up_panel, down_panel)
    panels_far = [swap(panel, 1) for panel in panels]
    *blocks, sel, table = pick_own(cap, old_home, new_expert, x, picks)
    blocks = around(blocks)
    *blocks_far, sel_far = pick_far(cap, old_home.shape[0], table, x_far, picks_far)
    blocks_far = around(blocks_far)
    *results, load = run_expert(meta, blocks + blocks_far, panels, panels_far)
    results, results_far = results[:SQUARE], results[SQUARE:]
    results_far = around(results_far)
    results = around(results)
    load_far = swap(load, 1)
    (far,) = merge_rows(merge_kernel, sel_far, (), results_far, False)
    back = swap(far, distant)
    weight = pick_weight.reshape(batches, tokens)
    output, slot_load = merge_rows(
        functools.partial(final_kernel, meta),
        sel,
        (weight, back, load, load_far),
        results,
        True,
    )
    return output.reshape(batches, tokens, width), slot_load


def solution(mesh):
    chips = mesh.shape["expert"] // 2

    def per_device(*args):
        if direct(args):
            return dispatched(*args)
        return gathered(*args)

    def direct(args):
        return chips == 2 * SQUARE and args[2].shape[2] == 1

    return jax.shard_map(
        per_device,
        mesh=mesh,
        in_specs=(
            P(None, ("groups", "expert"), None),
            P(None, ("groups", "expert"), None),
            P(None, ("groups", "expert"), None),
            P(None, ("groups", "expert"), None),
            P(),
            P("groups"),
            P("expert", None, None),
            P("expert", None, None),
            P("expert", None, None),
        ),
        out_specs=(P(None, ("groups", "expert"), None), P(("groups", "expert"))),
        check_vma=False,
    )
```

```python
import functools

import jax
import jax.numpy as jnp
from jax import lax
from jax.experimental import pallas as pl
from jax.experimental.pallas import tpu as pltpu
from jax.sharding import PartitionSpec as P


CAP = 2
REPL = 5
LANES = 128
SQUARE = 4
SMALL = 4 << 20
LARGE = 20 << 20
VMEM = pltpu.VMEM
SMEM = pltpu.SMEM
HBM = pltpu.MemorySpace.HBM


def slot_rank(new_expert, me):
    positions = jnp.arange(new_expert.shape[0], dtype=jnp.int32)
    mine = jnp.sum(jnp.where(positions == me, new_expert, 0))
    rank = jnp.sum(((new_expert == mine) & (positions < me)).astype(jnp.int32))
    return mine, rank


def gathered(
    activations,
    pick_weight,
    expert_ids,
    replica,
    old_home,
    new_expert,
    gate_panel,
    up_panel,
    down_panel,
):
    me = lax.axis_index("expert")
    batches, tokens, width = activations.shape
    top = expert_ids.shape[2]
    rows = batches * tokens
    x = activations.reshape(rows, width)
    picks = jnp.concatenate([expert_ids.reshape(rows, top), replica.reshape(rows, top)], axis=1)
    weights = pick_weight.reshape(rows, top)
    picks_all = lax.all_gather(picks, "expert", axis=0, tiled=True)
    weights_all = lax.all_gather(weights, "expert", axis=0, tiled=True)
    x_all = lax.all_gather(x, "expert", axis=0, tiled=True)
    ids_all = picks_all[:, :top]
    rep_all = picks_all[:, top:]
    mine, rank = slot_rank(new_expert, me)
    load = jnp.sum(((ids_all == mine) & (rep_all == rank)).astype(jnp.int32))
    labels = jnp.arange(old_home.shape[0], dtype=jnp.int32)
    held = jnp.sum(jnp.where(old_home == me // 2, labels, 0))
    scale = jnp.sum(jnp.where(ids_all == held, weights_all, 0.0), axis=1, keepdims=True)
    gate = jnp.dot(x_all, gate_panel[0], preferred_element_type=jnp.float32)
    up = jnp.dot(x_all, up_panel[0], preferred_element_type=jnp.float32)
    hidden = (jax.nn.silu(gate) * up).astype(jnp.bfloat16)
    part = lax.dot_general(
        hidden, down_panel[0], (((1,), (1,)), ((), ())), preferred_element_type=jnp.float32
    )
    part = (part * scale).astype(jnp.bfloat16)
    total = lax.psum_scatter(part, "expert", scatter_dimension=0, tiled=True)
    return total.reshape(batches, tokens, width), load.reshape(1)


def steps(index, size, count):
    whole = jnp.zeros_like(index)
    for step in range(1, count):
        whole = whole + (index >= step * size).astype(jnp.int32)
    return whole


def block_rows(batches, cap):
    return -(-(batches * cap + 1) // 8) * 8


def pick(cap, table, picks, x, blocks, sel_ref, experts):
    batches, tokens = picks.shape[0] // 2, picks.shape[1]
    count = batches * tokens
    high = block_rows(batches, cap)
    chip = lax.axis_index("expert") // 2

    def batch_of(index):
        return steps(index, tokens, batches)

    col = lax.broadcasted_iota(jnp.int32, (tokens, count), 1)
    spread = col - tokens * batch_of(col) == lax.broadcasted_iota(jnp.int32, (tokens, count), 0)
    spread = spread.astype(jnp.float32)
    own_lane = batch_of(lax.broadcasted_iota(jnp.int32, (batches, count), 1))
    own_lane = own_lane == lax.broadcasted_iota(jnp.int32, (batches, count), 0)

    def row_of(values):
        wide = jnp.dot(values.astype(jnp.float32), spread, preferred_element_type=jnp.float32)
        return jnp.sum(jnp.where(own_lane, wide, 0.0), axis=0, keepdims=True).astype(jnp.int32)

    ids = row_of(picks[:batches, :])
    reps = row_of(picks[batches:, :])
    target = jnp.zeros_like(ids)
    for expert in range(experts):
        target = jnp.where(ids == expert, table[0:1, expert : expert + 1], target)

    sub = lax.broadcasted_iota(jnp.int32, (8, count), 0)
    inside = (target == (sub ^ chip)) & (sub < SQUARE)
    before_from = lax.broadcasted_iota(jnp.int32, (count, count), 0)
    before_to = lax.broadcasted_iota(jnp.int32, (count, count), 1)
    before = (before_from < before_to) & (batch_of(before_from) == batch_of(before_to))
    earlier = jnp.dot(
        inside.astype(jnp.bfloat16),
        before.astype(jnp.bfloat16),
        preferred_element_type=jnp.float32,
    )
    position = jnp.sum(jnp.where(inside, earlier, 0.0), axis=0, keepdims=True).astype(jnp.int32)

    row = lax.broadcasted_iota(jnp.int32, (SQUARE * high, count), 0)
    peer = steps(row, high, SQUARE)
    left = row - high * peer
    group = steps(left, cap, batches + 1)
    left = left - cap * group
    lane = batch_of(lax.broadcasted_iota(jnp.int32, (SQUARE * high, count), 1))
    sel = ((target == (peer ^ chip)) & (position == left) & (group == lane)).astype(jnp.bfloat16)
    sel_ref[...] = sel
    meta_row = lax.broadcasted_iota(jnp.int32, (high, LANES), 0) == batches * cap
    meta_lane = lax.broadcasted_iota(jnp.int32, (high, LANES), 1)
    x = x()
    for q in range(SQUARE):
        part = jnp.dot(sel[q * high : (q + 1) * high], x, preferred_element_type=jnp.float32)
        meta = jnp.zeros((high, LANES), jnp.float32)
        for core in range(2):
            at = 2 * q + core
            hits = (ids == table[1:2, at : at + 1]) & (reps == table[2:3, at : at + 1])
            load = jnp.sum(hits.astype(jnp.float32), axis=1, keepdims=True)
            meta = jnp.where(meta_row & (meta_lane == core), load, meta)
        blocks[q][...] = part.astype(jnp.bfloat16)
        blocks[q][:, :LANES] = (part[:, :LANES] + meta).astype(jnp.bfloat16)


def pick_own_kernel(cap, home_hbm, new_hbm, x_hbm, ids_hbm, reps_hbm, *refs):
    blocks, (sel_ref, table_ref, picks_ref, zero_ref) = refs[:SQUARE], refs[SQUARE : SQUARE + 4]
    home_ref, new_ref, x_ref, ids_ref, reps_ref, sem = refs[SQUARE + 4 :]
    sources = (home_hbm, new_hbm, ids_hbm, reps_hbm, x_hbm)
    targets = (home_ref, new_ref, ids_ref, reps_ref, x_ref)
    copies = [
        pltpu.make_async_copy(source, target, sem.at[index])
        for index, (source, target) in enumerate(zip(sources, targets))
    ]
    for copy in copies:
        copy.start()
    zero_ref[...] = jnp.zeros(zero_ref.shape, zero_ref.dtype)
    chip = lax.axis_index("expert") // 2
    slots = new_ref.shape[0]
    experts = home_ref.shape[0]
    for copy in copies[:-1]:
        copy.wait()
    picks = jnp.concatenate([ids_ref[...], reps_ref[...]], axis=0)
    picks_ref[...] = picks
    row = lax.broadcasted_iota(jnp.int32, table_ref.shape, 0)
    lane = lax.broadcasted_iota(jnp.int32, table_ref.shape, 1)
    table = jnp.zeros(table_ref.shape, jnp.int32)
    for expert in range(experts):
        table = jnp.where((row == 0) & (lane == expert), home_ref[expert], table)
    for at in range(2 * SQUARE):
        slot = 2 * (chip ^ (at // 2)) + at % 2
        mine = new_ref[slot]
        rank = jnp.int32(0)
        for other in range(slots):
            rank = rank + ((new_ref[other] == mine) & (slot > other)).astype(jnp.int32)
        table = jnp.where((row == 1) & (lane == at), mine, table)
        table = jnp.where((row == 2) & (lane == at), rank, table)
    table_ref[...] = table

    def rows():
        copies[-1].wait()
        return x_ref[...]

    pick(cap, table, picks, rows, blocks, sel_ref, experts)


def pick_far_kernel(cap, experts, table_ref, x_ref, picks_ref, *refs):
    blocks, sel_ref = refs[:SQUARE], refs[SQUARE]
    pick(cap, table_ref[...], picks_ref[...], lambda: x_ref[...], blocks, sel_ref, experts)


def pick_shapes(cap, x, batches):
    high = block_rows(batches, cap)
    count, width = x.shape
    block = jax.ShapeDtypeStruct((high, width), jnp.bfloat16)
    sel = jax.ShapeDtypeStruct((SQUARE * high, count), jnp.bfloat16)
    cost = pl.CostEstimate(
        flops=2 * SQUARE * high * count * width,
        bytes_accessed=4 * SQUARE * high * width,
        transcendentals=0,
    )
    return [block] * SQUARE + [sel], cost


def pick_own(cap, home, new, x, ids, reps):
    batches, tokens = ids.shape
    shapes, cost = pick_shapes(cap, x, batches)
    shapes += [
        jax.ShapeDtypeStruct((8, LANES), jnp.int32),
        jax.ShapeDtypeStruct((2 * batches, tokens), jnp.int32),
        jax.ShapeDtypeStruct((8, LANES), jnp.float32),
    ]
    return pl.pallas_call(
        functools.partial(pick_own_kernel, cap),
        out_shape=shapes,
        in_specs=[pl.BlockSpec(memory_space=HBM)] * 5,
        out_specs=[pl.BlockSpec(memory_space=VMEM)] * len(shapes),
        scratch_shapes=[
            SMEM(home.shape, jnp.int32),
            SMEM(new.shape, jnp.int32),
            VMEM(x.shape, x.dtype),
            VMEM(ids.shape, ids.dtype),
            VMEM(reps.shape, reps.dtype),
            pltpu.SemaphoreType.DMA((5,)),
        ],
        cost_estimate=cost,
        compiler_params=pltpu.CompilerParams(vmem_limit_bytes=SMALL),
    )(*(pltpu.with_memory_space_constraint(value, HBM) for value in (home, new, x, ids, reps)))


def pick_far(cap, experts, table, x, picks):
    shapes, cost = pick_shapes(cap, x, picks.shape[0] // 2)
    return pl.pallas_call(
        functools.partial(pick_far_kernel, cap, experts),
        out_shape=shapes,
        in_specs=[pl.BlockSpec(memory_space=VMEM)] * 3,
        out_specs=[pl.BlockSpec(memory_space=VMEM)] * (SQUARE + 1),
        cost_estimate=cost,
        compiler_params=pltpu.CompilerParams(vmem_limit_bytes=SMALL),
    )(table, x, picks)


def fetch_kernel(*refs):
    count = len(refs) // 2
    sources, targets, sem = refs[:count], refs[count : 2 * count], refs[2 * count]
    copies = [
        pltpu.make_async_copy(source, target, sem.at[index])
        for index, (source, target) in enumerate(zip(sources, targets))
    ]
    for copy in copies:
        copy.start()
    for copy in copies:
        copy.wait()


def fetched(values):
    count = len(values)
    return pl.pallas_call(
        fetch_kernel,
        out_shape=[jax.ShapeDtypeStruct(value.shape, value.dtype) for value in values],
        in_specs=[pl.BlockSpec(memory_space=HBM)] * count,
        out_specs=[pl.BlockSpec(memory_space=VMEM)] * count,
        scratch_shapes=[pltpu.SemaphoreType.DMA((count,))],
        cost_estimate=pl.CostEstimate(
            flops=0, bytes_accessed=4 * sum(value.size for value in values), transcendentals=0
        ),
        compiler_params=pltpu.CompilerParams(vmem_limit_bytes=LARGE),
    )(*(pltpu.with_memory_space_constraint(value, HBM) for value in values))


def expert_kernel(meta, *refs):
    blocks, panels, prior_ref = refs[:SQUARE], refs[SQUARE : SQUARE + 6], refs[SQUARE + 6]
    outs, load_ref = refs[SQUARE + 7 : 2 * SQUARE + 7], refs[2 * SQUARE + 7]
    high = blocks[0].shape[0]
    x = jnp.concatenate([block[...] for block in blocks], axis=0)
    contract = (((1,), (1,)), ((), ()))
    start = meta - meta % 8
    load = prior_ref[...]
    for block in blocks:
        load = load + block[start : start + 8, :LANES].astype(jnp.float32)
    load_ref[...] = load
    total = None
    for gate_ref, up_ref, down_ref in (panels[:3], panels[3:]):
        gate = jnp.dot(x, gate_ref[0], preferred_element_type=jnp.float32)
        up = jnp.dot(x, up_ref[0], preferred_element_type=jnp.float32)
        hidden = (gate / (1.0 + jnp.exp(-gate)) * up).astype(jnp.bfloat16)
        part = lax.dot_general(hidden, down_ref[0], contract, preferred_element_type=jnp.float32)
        total = part if total is None else total + part
    total = total.astype(jnp.bfloat16)
    for q in range(SQUARE):
        outs[q][...] = total[q * high : (q + 1) * high]


def run_expert(meta, blocks, panels, panels_far, prior):
    high, width = blocks[0].shape
    half = panels[0].shape[2]
    rows = SQUARE * high
    return pl.pallas_call(
        functools.partial(expert_kernel, meta),
        out_shape=[jax.ShapeDtypeStruct((high, width), jnp.bfloat16)] * SQUARE
        + [jax.ShapeDtypeStruct(prior.shape, prior.dtype)],
        in_specs=[pl.BlockSpec(memory_space=VMEM)] * (SQUARE + 7),
        out_specs=[pl.BlockSpec(memory_space=VMEM)] * (SQUARE + 1),
        cost_estimate=pl.CostEstimate(
            flops=2 * rows * width * half * 6,
            bytes_accessed=6 * 2 * width * half + 4 * rows * width,
            transcendentals=2 * rows * half,
        ),
        compiler_params=pltpu.CompilerParams(vmem_limit_bytes=LARGE),
    )(*blocks, *panels, *panels_far, prior)


def chosen(sel_ref, blocks):
    y = jnp.concatenate([block[...] for block in blocks], axis=0)
    return lax.dot_general(
        sel_ref[...], y, (((0,), (0,)), ((), ())), preferred_element_type=jnp.float32
    )


def merge_kernel(sel_ref, *refs):
    refs[SQUARE][...] = chosen(sel_ref, refs[:SQUARE]).astype(jnp.bfloat16)


def final_kernel(meta, sel_ref, weight_ref, back_ref, load_ref, load_far_ref, *refs):
    out_ref, slot_ref = refs[SQUARE], refs[SQUARE + 1]
    core = lax.axis_index("expert") % 2
    both = load_ref[...] + load_far_ref[...]
    row = lax.broadcasted_iota(jnp.int32, both.shape, 0)
    lane = lax.broadcasted_iota(jnp.int32, both.shape, 1)
    slot_ref[0] = jnp.sum(jnp.where((row == meta % 8) & (lane == core), both, 0.0)).astype(
        jnp.int32
    )
    batches, tokens = weight_ref.shape
    total = chosen(sel_ref, refs[:SQUARE]) + back_ref[...].astype(jnp.float32)
    lane = lax.broadcasted_iota(jnp.int32, (tokens, tokens), 0)
    same = lane == lax.broadcasted_iota(jnp.int32, (tokens, tokens), 1)
    scale = jnp.concatenate(
        [
            jnp.sum(
                jnp.where(same, weight_ref[batch : batch + 1, :], 0.0), axis=1, keepdims=True
            )
            for batch in range(batches)
        ],
        axis=0,
    )
    out_ref[...] = (total * scale).astype(jnp.bfloat16)


def merge_rows(kernel, sel, others, blocks, loads):
    count = sel.shape[1]
    width = blocks[0].shape[1]
    shapes = [jax.ShapeDtypeStruct((count, width), jnp.bfloat16)]
    specs = [pl.BlockSpec(memory_space=VMEM)]
    if loads:
        shapes.append(jax.ShapeDtypeStruct((1,), jnp.int32))
        specs.append(pl.BlockSpec(memory_space=SMEM))
    return pl.pallas_call(
        kernel,
        out_shape=shapes,
        in_specs=[pl.BlockSpec(memory_space=VMEM)] * (SQUARE + 1 + len(others)),
        out_specs=specs,
        cost_estimate=pl.CostEstimate(
            flops=2 * sel.shape[0] * count * width,
            bytes_accessed=2 * (sel.shape[0] + count) * width,
            transcendentals=0,
        ),
        compiler_params=pltpu.CompilerParams(vmem_limit_bytes=SMALL),
    )(sel, *others, *blocks)


def swapped(size, bits):
    return [(index, index ^ bits) for index in range(size)]


def dispatched(
    activations,
    pick_weight,
    expert_ids,
    replica,
    old_home,
    new_expert,
    gate_panel,
    up_panel,
    down_panel,
):
    size = lax.axis_size("expert")
    batches, tokens, width = activations.shape
    rows = batches * tokens
    cap = min(CAP * REPL, tokens)
    meta = batches * cap
    distant = 2 * SQUARE

    def swap(value, bits):
        return lax.ppermute(value, "expert", swapped(size, bits))

    def around(blocks):
        return [blocks[0]] + [swap(blocks[q], 2 * q) for q in range(1, SQUARE)]

    x = activations.reshape(rows, width)
    x_far = swap(x, distant)
    panels = (gate_panel, up_panel, down_panel)
    panels_far = [swap(panel, 1) for panel in panels]
    *blocks, sel, table, picks, zero = pick_own(
        cap,
        old_home,
        new_expert,
        x,
        expert_ids.reshape(batches, tokens),
        replica.reshape(batches, tokens),
    )
    picks_far = swap(picks, distant)
    blocks = around(blocks)
    *blocks_far, sel_far = pick_far(cap, old_home.shape[0], table, x_far, picks_far)
    blocks_far = around(blocks_far)
    panels = fetched(panels)
    *results, load = run_expert(meta, blocks, panels, panels_far, zero)
    *results_far, load = run_expert(meta, blocks_far, panels, panels_far, load)
    results_far = around(results_far)
    results = around(results)
    load_far = swap(load, 1)
    (far,) = merge_rows(merge_kernel, sel_far, (), results_far, False)
    back = swap(far, distant)
    weight = pick_weight.reshape(batches, tokens)
    output, slot_load = merge_rows(
        functools.partial(final_kernel, meta),
        sel,
        (weight, back, load, load_far),
        results,
        True,
    )
    return output.reshape(batches, tokens, width), slot_load


def solution(mesh):
    chips = mesh.shape["expert"] // 2

    def per_device(*args):
        if direct(args):
            return dispatched(*args)
        return gathered(*args)

    def direct(args):
        return chips == 2 * SQUARE and args[2].shape[2] == 1

    return jax.shard_map(
        per_device,
        mesh=mesh,
        in_specs=(
            P(None, ("groups", "expert"), None),
            P(None, ("groups", "expert"), None),
            P(None, ("groups", "expert"), None),
            P(None, ("groups", "expert"), None),
            P(),
            P("groups"),
            P("expert", None, None),
            P("expert", None, None),
            P("expert", None, None),
        ),
        out_specs=(P(None, ("groups", "expert"), None), P(("groups", "expert"))),
        check_vma=False,
    )
```

```python
import functools

import jax
import jax.numpy as jnp
from jax import lax
from jax.experimental import pallas as pl
from jax.experimental.pallas import tpu as pltpu
from jax.sharding import PartitionSpec as P


CAP = 2
REPL = 5
LANES = 128
SQUARE = 4
SMALL = 4 << 20
LARGE = 20 << 20
VMEM = pltpu.VMEM
SMEM = pltpu.SMEM
HBM = pltpu.MemorySpace.HBM


def slot_rank(new_expert, me):
    positions = jnp.arange(new_expert.shape[0], dtype=jnp.int32)
    mine = jnp.sum(jnp.where(positions == me, new_expert, 0))
    rank = jnp.sum(((new_expert == mine) & (positions < me)).astype(jnp.int32))
    return mine, rank


def gathered(
    activations,
    pick_weight,
    expert_ids,
    replica,
    old_home,
    new_expert,
    gate_panel,
    up_panel,
    down_panel,
):
    me = lax.axis_index("expert")
    batches, tokens, width = activations.shape
    top = expert_ids.shape[2]
    rows = batches * tokens
    x = activations.reshape(rows, width)
    picks = jnp.concatenate([expert_ids.reshape(rows, top), replica.reshape(rows, top)], axis=1)
    weights = pick_weight.reshape(rows, top)
    picks_all = lax.all_gather(picks, "expert", axis=0, tiled=True)
    weights_all = lax.all_gather(weights, "expert", axis=0, tiled=True)
    x_all = lax.all_gather(x, "expert", axis=0, tiled=True)
    ids_all = picks_all[:, :top]
    rep_all = picks_all[:, top:]
    mine, rank = slot_rank(new_expert, me)
    load = jnp.sum(((ids_all == mine) & (rep_all == rank)).astype(jnp.int32))
    labels = jnp.arange(old_home.shape[0], dtype=jnp.int32)
    held = jnp.sum(jnp.where(old_home == me // 2, labels, 0))
    scale = jnp.sum(jnp.where(ids_all == held, weights_all, 0.0), axis=1, keepdims=True)
    gate = jnp.dot(x_all, gate_panel[0], preferred_element_type=jnp.float32)
    up = jnp.dot(x_all, up_panel[0], preferred_element_type=jnp.float32)
    hidden = (jax.nn.silu(gate) * up).astype(jnp.bfloat16)
    part = lax.dot_general(
        hidden, down_panel[0], (((1,), (1,)), ((), ())), preferred_element_type=jnp.float32
    )
    part = (part * scale).astype(jnp.bfloat16)
    total = lax.psum_scatter(part, "expert", scatter_dimension=0, tiled=True)
    return total.reshape(batches, tokens, width), load.reshape(1)


def steps(index, size, count):
    whole = jnp.zeros_like(index)
    for step in range(1, count):
        whole = whole + (index >= step * size).astype(jnp.int32)
    return whole


def block_rows(batches, cap):
    return -(-(batches * cap + 1) // 8) * 8


def pick(cap, table, picks, x, blocks, sel_ref, experts):
    batches, tokens = picks.shape[0] // 2, picks.shape[1]
    count = batches * tokens
    high = block_rows(batches, cap)
    chip = lax.axis_index("expert") // 2

    def batch_of(index):
        return steps(index, tokens, batches)

    col = lax.broadcasted_iota(jnp.int32, (tokens, count), 1)
    spread = col - tokens * batch_of(col) == lax.broadcasted_iota(jnp.int32, (tokens, count), 0)
    spread = spread.astype(jnp.float32)
    own_lane = batch_of(lax.broadcasted_iota(jnp.int32, (batches, count), 1))
    own_lane = own_lane == lax.broadcasted_iota(jnp.int32, (batches, count), 0)

    def row_of(values):
        wide = jnp.dot(values.astype(jnp.float32), spread, preferred_element_type=jnp.float32)
        return jnp.sum(jnp.where(own_lane, wide, 0.0), axis=0, keepdims=True).astype(jnp.int32)

    ids = row_of(picks[:batches, :])
    reps = row_of(picks[batches:, :])
    target = jnp.zeros_like(ids)
    for expert in range(experts):
        target = jnp.where(ids == expert, table[0:1, expert : expert + 1], target)

    sub = lax.broadcasted_iota(jnp.int32, (8, count), 0)
    inside = (target == (sub ^ chip)) & (sub < SQUARE)
    before_from = lax.broadcasted_iota(jnp.int32, (count, count), 0)
    before_to = lax.broadcasted_iota(jnp.int32, (count, count), 1)
    before = (before_from < before_to) & (batch_of(before_from) == batch_of(before_to))
    earlier = jnp.dot(
        inside.astype(jnp.bfloat16),
        before.astype(jnp.bfloat16),
        preferred_element_type=jnp.float32,
    )
    position = jnp.sum(jnp.where(inside, earlier, 0.0), axis=0, keepdims=True).astype(jnp.int32)

    row = lax.broadcasted_iota(jnp.int32, (SQUARE * high, count), 0)
    peer = steps(row, high, SQUARE)
    left = row - high * peer
    group = steps(left, cap, batches + 1)
    left = left - cap * group
    lane = batch_of(lax.broadcasted_iota(jnp.int32, (SQUARE * high, count), 1))
    sel = ((target == (peer ^ chip)) & (position == left) & (group == lane)).astype(jnp.bfloat16)
    sel_ref[...] = sel
    meta_row = lax.broadcasted_iota(jnp.int32, (high, LANES), 0) == batches * cap
    meta_lane = lax.broadcasted_iota(jnp.int32, (high, LANES), 1)
    x = x()
    for q in range(SQUARE):
        part = jnp.dot(sel[q * high : (q + 1) * high], x, preferred_element_type=jnp.float32)
        meta = jnp.zeros((high, LANES), jnp.float32)
        for core in range(2):
            at = 2 * q + core
            hits = (ids == table[1:2, at : at + 1]) & (reps == table[2:3, at : at + 1])
            load = jnp.sum(hits.astype(jnp.float32), axis=1, keepdims=True)
            meta = jnp.where(meta_row & (meta_lane == core), load, meta)
        blocks[q][...] = part.astype(jnp.bfloat16)
        blocks[q][:, :LANES] = (part[:, :LANES] + meta).astype(jnp.bfloat16)


def pick_own_kernel(cap, home_hbm, new_hbm, x_hbm, ids_hbm, reps_hbm, *refs):
    blocks, (sel_ref, table_ref, picks_ref, zero_ref) = refs[:SQUARE], refs[SQUARE : SQUARE + 4]
    home_ref, new_ref, x_ref, ids_ref, reps_ref, sem = refs[SQUARE + 4 :]
    sources = (home_hbm, new_hbm, ids_hbm, reps_hbm, x_hbm)
    targets = (home_ref, new_ref, ids_ref, reps_ref, x_ref)
    copies = [
        pltpu.make_async_copy(source, target, sem.at[index])
        for index, (source, target) in enumerate(zip(sources, targets))
    ]
    for copy in copies:
        copy.start()
    zero_ref[...] = jnp.zeros(zero_ref.shape, zero_ref.dtype)
    chip = lax.axis_index("expert") // 2
    slots = new_ref.shape[0]
    experts = home_ref.shape[0]
    for copy in copies[:-1]:
        copy.wait()
    picks = jnp.concatenate([ids_ref[...], reps_ref[...]], axis=0)
    picks_ref[...] = picks
    row = lax.broadcasted_iota(jnp.int32, table_ref.shape, 0)
    lane = lax.broadcasted_iota(jnp.int32, table_ref.shape, 1)
    table = jnp.zeros(table_ref.shape, jnp.int32)
    for expert in range(experts):
        table = jnp.where((row == 0) & (lane == expert), home_ref[expert], table)
    for at in range(2 * SQUARE):
        slot = 2 * (chip ^ (at // 2)) + at % 2
        mine = new_ref[slot]
        rank = jnp.int32(0)
        for other in range(slots):
            rank = rank + ((new_ref[other] == mine) & (slot > other)).astype(jnp.int32)
        table = jnp.where((row == 1) & (lane == at), mine, table)
        table = jnp.where((row == 2) & (lane == at), rank, table)
    table_ref[...] = table

    def rows():
        copies[-1].wait()
        return x_ref[...]

    pick(cap, table, picks, rows, blocks, sel_ref, experts)


def pick_far_kernel(cap, experts, table_ref, x_ref, picks_ref, *refs):
    blocks, sel_ref = refs[:SQUARE], refs[SQUARE]
    pick(cap, table_ref[...], picks_ref[...], lambda: x_ref[...], blocks, sel_ref, experts)


def pick_shapes(cap, x, batches):
    high = block_rows(batches, cap)
    count, width = x.shape
    block = jax.ShapeDtypeStruct((high, width), jnp.bfloat16)
    sel = jax.ShapeDtypeStruct((SQUARE * high, count), jnp.bfloat16)
    cost = pl.CostEstimate(
        flops=2 * SQUARE * high * count * width,
        bytes_accessed=4 * SQUARE * high * width,
        transcendentals=0,
    )
    return [block] * SQUARE + [sel], cost


def pick_own(cap, home, new, x, ids, reps):
    batches, tokens = ids.shape
    shapes, cost = pick_shapes(cap, x, batches)
    shapes += [
        jax.ShapeDtypeStruct((8, LANES), jnp.int32),
        jax.ShapeDtypeStruct((2 * batches, tokens), jnp.int32),
        jax.ShapeDtypeStruct((8, LANES), jnp.float32),
    ]
    return pl.pallas_call(
        functools.partial(pick_own_kernel, cap),
        out_shape=shapes,
        in_specs=[pl.BlockSpec(memory_space=HBM)] * 5,
        out_specs=[pl.BlockSpec(memory_space=VMEM)] * len(shapes),
        scratch_shapes=[
            SMEM(home.shape, jnp.int32),
            SMEM(new.shape, jnp.int32),
            VMEM(x.shape, x.dtype),
            VMEM(ids.shape, ids.dtype),
            VMEM(reps.shape, reps.dtype),
            pltpu.SemaphoreType.DMA((5,)),
        ],
        cost_estimate=cost,
        compiler_params=pltpu.CompilerParams(vmem_limit_bytes=SMALL),
    )(*(pltpu.with_memory_space_constraint(value, HBM) for value in (home, new, x, ids, reps)))


def pick_far(cap, experts, table, x, picks):
    shapes, cost = pick_shapes(cap, x, picks.shape[0] // 2)
    return pl.pallas_call(
        functools.partial(pick_far_kernel, cap, experts),
        out_shape=shapes,
        in_specs=[pl.BlockSpec(memory_space=VMEM)] * 3,
        out_specs=[pl.BlockSpec(memory_space=VMEM)] * (SQUARE + 1),
        cost_estimate=cost,
        compiler_params=pltpu.CompilerParams(vmem_limit_bytes=SMALL),
    )(table, x, picks)


def fetch_kernel(*refs):
    count = len(refs) // 2
    sources, targets, sem = refs[:count], refs[count : 2 * count], refs[2 * count]
    copies = [
        pltpu.make_async_copy(source, target, sem.at[index])
        for index, (source, target) in enumerate(zip(sources, targets))
    ]
    for copy in copies:
        copy.start()
    for copy in copies:
        copy.wait()


def fetched(values):
    count = len(values)
    return pl.pallas_call(
        fetch_kernel,
        out_shape=[jax.ShapeDtypeStruct(value.shape, value.dtype) for value in values],
        in_specs=[pl.BlockSpec(memory_space=HBM)] * count,
        out_specs=[pl.BlockSpec(memory_space=VMEM)] * count,
        scratch_shapes=[pltpu.SemaphoreType.DMA((count,))],
        cost_estimate=pl.CostEstimate(
            flops=0, bytes_accessed=4 * sum(value.size for value in values), transcendentals=0
        ),
        compiler_params=pltpu.CompilerParams(vmem_limit_bytes=LARGE),
    )(*(pltpu.with_memory_space_constraint(value, HBM) for value in values))


def expert_kernel(meta, *refs):
    blocks, panels, prior_ref = refs[:SQUARE], refs[SQUARE : SQUARE + 6], refs[SQUARE + 6]
    outs, load_ref = refs[SQUARE + 7 : 2 * SQUARE + 7], refs[2 * SQUARE + 7]
    high = blocks[0].shape[0]
    x = jnp.concatenate([block[...] for block in blocks], axis=0)
    contract = (((1,), (1,)), ((), ()))
    start = meta - meta % 8
    load = prior_ref[...]
    for block in blocks:
        load = load + block[start : start + 8, :LANES].astype(jnp.float32)
    load_ref[...] = load
    total = None
    for gate_ref, up_ref, down_ref in (panels[:3], panels[3:]):
        gate = jnp.dot(x, gate_ref[0], preferred_element_type=jnp.float32)
        up = jnp.dot(x, up_ref[0], preferred_element_type=jnp.float32)
        hidden = (gate / (1.0 + jnp.exp(-gate)) * up).astype(jnp.bfloat16)
        part = lax.dot_general(hidden, down_ref[0], contract, preferred_element_type=jnp.float32)
        total = part if total is None else total + part
    total = total.astype(jnp.bfloat16)
    for q in range(SQUARE):
        outs[q][...] = total[q * high : (q + 1) * high]


def run_expert(meta, blocks, panels, panels_far, prior):
    high, width = blocks[0].shape
    half = panels[0].shape[2]
    rows = SQUARE * high
    return pl.pallas_call(
        functools.partial(expert_kernel, meta),
        out_shape=[jax.ShapeDtypeStruct((high, width), jnp.bfloat16)] * SQUARE
        + [jax.ShapeDtypeStruct(prior.shape, prior.dtype)],
        in_specs=[pl.BlockSpec(memory_space=VMEM)] * (SQUARE + 7),
        out_specs=[pl.BlockSpec(memory_space=VMEM)] * (SQUARE + 1),
        cost_estimate=pl.CostEstimate(
            flops=2 * rows * width * half * 6,
            bytes_accessed=6 * 2 * width * half + 4 * rows * width,
            transcendentals=2 * rows * half,
        ),
        compiler_params=pltpu.CompilerParams(vmem_limit_bytes=LARGE),
    )(*blocks, *panels, *panels_far, prior)


def chosen(sel_ref, blocks):
    y = jnp.concatenate([block[...] for block in blocks], axis=0)
    return lax.dot_general(
        sel_ref[...], y, (((0,), (0,)), ((), ())), preferred_element_type=jnp.float32
    )


def merge_kernel(sel_ref, *refs):
    refs[SQUARE][...] = chosen(sel_ref, refs[:SQUARE]).astype(jnp.bfloat16)


def merge_own_kernel(sel_ref, weight_ref, *refs):
    out_ref, scale_ref = refs[SQUARE:]
    out_ref[...] = chosen(sel_ref, refs[:SQUARE]).astype(jnp.bfloat16)
    batches, tokens = weight_ref.shape
    lane = lax.broadcasted_iota(jnp.int32, (tokens, tokens), 0)
    same = lane == lax.broadcasted_iota(jnp.int32, (tokens, tokens), 1)
    for batch in range(batches):
        column = jnp.where(same, weight_ref[batch : batch + 1, :], 0.0)
        column = jnp.sum(column, axis=1, keepdims=True)
        scale_ref[batch * tokens : (batch + 1) * tokens, :] = jnp.broadcast_to(
            column, (tokens, LANES)
        )


def final_kernel(meta, own_ref, scale_ref, load_ref, load_far_ref, back_ref, out_ref, slot_ref):
    core = lax.axis_index("expert") % 2
    both = load_ref[...] + load_far_ref[...]
    row = lax.broadcasted_iota(jnp.int32, both.shape, 0)
    lane = lax.broadcasted_iota(jnp.int32, both.shape, 1)
    slot_ref[0] = jnp.sum(jnp.where((row == meta % 8) & (lane == core), both, 0.0)).astype(
        jnp.int32
    )
    total = own_ref[...].astype(jnp.float32) + back_ref[...].astype(jnp.float32)
    out_ref[...] = (total * scale_ref[:, :1]).astype(jnp.bfloat16)


def small_call(kernel, shapes, *operands, slot=False):
    specs = [pl.BlockSpec(memory_space=VMEM)] * len(shapes)
    if slot:
        shapes = shapes + [jax.ShapeDtypeStruct((1,), jnp.int32)]
        specs = specs + [pl.BlockSpec(memory_space=SMEM)]
    return pl.pallas_call(
        kernel,
        out_shape=shapes,
        in_specs=[pl.BlockSpec(memory_space=VMEM)] * len(operands),
        out_specs=specs,
        cost_estimate=pl.CostEstimate(
            flops=2 * sum(shape.size for shape in shapes) * LANES,
            bytes_accessed=2 * sum(operand.size for operand in operands),
            transcendentals=0,
        ),
        compiler_params=pltpu.CompilerParams(vmem_limit_bytes=SMALL),
    )(*operands)


def swapped(size, bits):
    return [(index, index ^ bits) for index in range(size)]


def dispatched(
    activations,
    pick_weight,
    expert_ids,
    replica,
    old_home,
    new_expert,
    gate_panel,
    up_panel,
    down_panel,
):
    size = lax.axis_size("expert")
    batches, tokens, width = activations.shape
    rows = batches * tokens
    cap = min(CAP * REPL, tokens)
    meta = batches * cap
    distant = 2 * SQUARE

    def swap(value, bits):
        return lax.ppermute(value, "expert", swapped(size, bits))

    def around(blocks):
        return [blocks[0]] + [swap(blocks[q], 2 * q) for q in range(1, SQUARE)]

    x = activations.reshape(rows, width)
    x_far = swap(x, distant)
    panels = (gate_panel, up_panel, down_panel)
    panels_far = [swap(panel, 1) for panel in panels]
    *blocks, sel, table, picks, zero = pick_own(
        cap,
        old_home,
        new_expert,
        x,
        expert_ids.reshape(batches, tokens),
        replica.reshape(batches, tokens),
    )
    picks_far = swap(picks, distant)
    blocks = around(blocks)
    *blocks_far, sel_far = pick_far(cap, old_home.shape[0], table, x_far, picks_far)
    blocks_far = around(blocks_far)
    panels = fetched(panels)
    *results, load = run_expert(meta, blocks, panels, panels_far, zero)
    *results_far, load = run_expert(meta, blocks_far, panels, panels_far, load)
    results_far = around(results_far)
    results = around(results)
    load_far = swap(load, 1)
    whole = jax.ShapeDtypeStruct((rows, width), jnp.bfloat16)
    (far,) = small_call(merge_kernel, [whole], sel_far, *results_far)
    back = swap(far, distant)
    weight = pick_weight.reshape(batches, tokens)
    own, scale = small_call(
        merge_own_kernel,
        [whole, jax.ShapeDtypeStruct((rows, LANES), jnp.float32)],
        sel,
        weight,
        *results,
    )
    output, slot_load = small_call(
        functools.partial(final_kernel, meta),
        [whole],
        own,
        scale,
        load,
        load_far,
        back,
        slot=True,
    )
    return output.reshape(batches, tokens, width), slot_load


def solution(mesh):
    chips = mesh.shape["expert"] // 2

    def per_device(*args):
        if direct(args):
            return dispatched(*args)
        return gathered(*args)

    def direct(args):
        return chips == 2 * SQUARE and args[2].shape[2] == 1

    return jax.shard_map(
        per_device,
        mesh=mesh,
        in_specs=(
            P(None, ("groups", "expert"), None),
            P(None, ("groups", "expert"), None),
            P(None, ("groups", "expert"), None),
            P(None, ("groups", "expert"), None),
            P(),
            P("groups"),
            P("expert", None, None),
            P("expert", None, None),
            P("expert", None, None),
        ),
        out_specs=(P(None, ("groups", "expert"), None), P(("groups", "expert"))),
        check_vma=False,
    )
```

```python
import functools

import jax
import jax.numpy as jnp
from jax import lax
from jax.experimental import pallas as pl
from jax.experimental.pallas import tpu as pltpu
from jax.sharding import PartitionSpec as P


CAP = 2
REPL = 5
LANES = 128
SQUARE = 4
TILE = 8
PANELS = 2
SMALL = 4 << 20
LARGE = 20 << 20
VMEM = pltpu.VMEM
SMEM = pltpu.SMEM
HBM = pltpu.MemorySpace.HBM


def slot_rank(new_expert, me):
    positions = jnp.arange(new_expert.shape[0], dtype=jnp.int32)
    mine = jnp.sum(jnp.where(positions == me, new_expert, 0))
    rank = jnp.sum(((new_expert == mine) & (positions < me)).astype(jnp.int32))
    return mine, rank


def gathered(
    activations,
    pick_weight,
    expert_ids,
    replica,
    old_home,
    new_expert,
    gate_panel,
    up_panel,
    down_panel,
):
    me = lax.axis_index("expert")
    batches, tokens, width = activations.shape
    top = expert_ids.shape[2]
    rows = batches * tokens
    x = activations.reshape(rows, width)
    picks = jnp.concatenate([expert_ids.reshape(rows, top), replica.reshape(rows, top)], axis=1)
    weights = pick_weight.reshape(rows, top)
    picks_all = lax.all_gather(picks, "expert", axis=0, tiled=True)
    weights_all = lax.all_gather(weights, "expert", axis=0, tiled=True)
    x_all = lax.all_gather(x, "expert", axis=0, tiled=True)
    ids_all = picks_all[:, :top]
    rep_all = picks_all[:, top:]
    mine, rank = slot_rank(new_expert, me)
    load = jnp.sum(((ids_all == mine) & (rep_all == rank)).astype(jnp.int32))
    labels = jnp.arange(old_home.shape[0], dtype=jnp.int32)
    held = jnp.sum(jnp.where(old_home == me // 2, labels, 0))
    scale = jnp.sum(jnp.where(ids_all == held, weights_all, 0.0), axis=1, keepdims=True)
    gate = jnp.dot(x_all, gate_panel[0], preferred_element_type=jnp.float32)
    up = jnp.dot(x_all, up_panel[0], preferred_element_type=jnp.float32)
    hidden = (jax.nn.silu(gate) * up).astype(jnp.bfloat16)
    part = lax.dot_general(
        hidden, down_panel[0], (((1,), (1,)), ((), ())), preferred_element_type=jnp.float32
    )
    part = (part * scale).astype(jnp.bfloat16)
    total = lax.psum_scatter(part, "expert", scatter_dimension=0, tiled=True)
    return total.reshape(batches, tokens, width), load.reshape(1)


def steps(index, size, count):
    whole = jnp.zeros_like(index)
    for step in range(1, count):
        whole = whole + (index >= step * size).astype(jnp.int32)
    return whole


def tiling(count):
    full, rest = divmod(count, TILE)
    fold = TILE // rest if rest and TILE % rest == 0 else 1
    if rest and fold == 1:
        full, rest = full + 1, 0
    return full, rest, fold


def block_rows(batches, cap):
    return -(-batches * cap // TILE) * TILE


def block_lanes(count, width):
    full, rest, fold = tiling(count)
    return full * width + (width // fold if rest else 0)


def packed(count, rows, ref):
    full, rest, fold = tiling(count)
    width = rows.shape[1]
    for tile in range(full):
        part = rows[tile * TILE : (tile + 1) * TILE]
        ref[:, tile * width : (tile + 1) * width] = part.astype(ref.dtype)
    if rest:
        tail = rows[full * TILE : (full + 1) * TILE]
        piece = width // fold
        turn = steps(lax.broadcasted_iota(jnp.int32, (TILE, piece), 0), rest, fold)
        value = tail[:, :piece]
        for index in range(1, fold):
            moved = pltpu.roll(tail[:, index * piece : (index + 1) * piece], index * rest, axis=0)
            value = jnp.where(turn == index, moved, value)
        ref[:, full * width : full * width + piece] = value.astype(ref.dtype)


def unpacked(count, width, ref):
    full, rest, fold = tiling(count)
    tiles = [ref[:, tile * width : (tile + 1) * width] for tile in range(full)]
    if rest:
        piece = width // fold
        tail = ref[:, full * width : full * width + piece].astype(jnp.float32)
        parts = [tail]
        for index in range(1, fold):
            parts.append(pltpu.roll(tail, TILE - index * rest, axis=0))
        tiles.append(jnp.concatenate(parts, axis=1).astype(ref.dtype))
    return tiles


def stacked(count, width, refs):
    tiles = [tile for ref in refs for tile in unpacked(count, width, ref)]
    return jnp.concatenate(tiles, axis=0)


def pick(cap, table, picks, x, blocks, sel_ref, experts):
    batches, tokens = picks.shape[0] // 2, picks.shape[1]
    count = batches * tokens
    high = block_rows(batches, cap)
    chip = lax.axis_index("expert") // 2

    def batch_of(index):
        return steps(index, tokens, batches)

    col = lax.broadcasted_iota(jnp.int32, (tokens, count), 1)
    spread = col - tokens * batch_of(col) == lax.broadcasted_iota(jnp.int32, (tokens, count), 0)
    spread = spread.astype(jnp.float32)
    own_lane = batch_of(lax.broadcasted_iota(jnp.int32, (batches, count), 1))
    own_lane = own_lane == lax.broadcasted_iota(jnp.int32, (batches, count), 0)

    def row_of(values):
        wide = jnp.dot(values.astype(jnp.float32), spread, preferred_element_type=jnp.float32)
        return jnp.sum(jnp.where(own_lane, wide, 0.0), axis=0, keepdims=True).astype(jnp.int32)

    ids = row_of(picks[:batches, :])
    reps = row_of(picks[batches:, :])
    target = jnp.zeros_like(ids)
    for expert in range(experts):
        target = jnp.where(ids == expert, table[0:1, expert : expert + 1], target)

    sub = lax.broadcasted_iota(jnp.int32, (8, count), 0)
    inside = (target == (sub ^ chip)) & (sub < SQUARE)
    before_from = lax.broadcasted_iota(jnp.int32, (count, count), 0)
    before_to = lax.broadcasted_iota(jnp.int32, (count, count), 1)
    before = (before_from < before_to) & (batch_of(before_from) == batch_of(before_to))
    earlier = jnp.dot(
        inside.astype(jnp.bfloat16),
        before.astype(jnp.bfloat16),
        preferred_element_type=jnp.float32,
    )
    position = jnp.sum(jnp.where(inside, earlier, 0.0), axis=0, keepdims=True).astype(jnp.int32)

    row = lax.broadcasted_iota(jnp.int32, (SQUARE * high, count), 0)
    peer = steps(row, high, SQUARE)
    left = row - high * peer
    group = steps(left, cap, batches + 1)
    left = left - cap * group
    lane = batch_of(lax.broadcasted_iota(jnp.int32, (SQUARE * high, count), 1))
    sel = ((target == (peer ^ chip)) & (position == left) & (group == lane)).astype(jnp.bfloat16)
    sel_ref[...] = sel
    meta_lane = lax.broadcasted_iota(jnp.int32, (TILE, LANES), 1)
    x = x()
    for q in range(SQUARE):
        part = jnp.dot(sel[q * high : (q + 1) * high], x, preferred_element_type=jnp.float32)
        meta = jnp.zeros((TILE, LANES), jnp.float32)
        for core in range(2):
            at = 2 * q + core
            hits = (ids == table[1:2, at : at + 1]) & (reps == table[2:3, at : at + 1])
            load = jnp.sum(hits.astype(jnp.float32), axis=1, keepdims=True)
            meta = jnp.where(meta_lane == core, load, meta)
        packed(batches * cap, part, blocks[q])
        blocks[q][:, blocks[q].shape[1] - LANES :] = meta.astype(jnp.bfloat16)


def pick_own_kernel(cap, home_hbm, new_hbm, x_hbm, ids_hbm, reps_hbm, *refs):
    panels_hbm, refs = refs[:PANELS], refs[PANELS:]
    blocks, (sel_ref, table_ref, picks_ref, zero_ref) = refs[:SQUARE], refs[SQUARE : SQUARE + 4]
    panels, refs = refs[SQUARE + 4 : SQUARE + 4 + PANELS], refs[SQUARE + 4 + PANELS :]
    home_ref, new_ref, x_ref, ids_ref, reps_ref, sem = refs
    sources = (home_hbm, new_hbm, ids_hbm, reps_hbm, x_hbm, *panels_hbm)
    targets = (home_ref, new_ref, ids_ref, reps_ref, x_ref, *panels)
    copies = [
        pltpu.make_async_copy(source, target, sem.at[index])
        for index, (source, target) in enumerate(zip(sources, targets))
    ]
    for copy in copies:
        copy.start()
    zero_ref[...] = jnp.zeros(zero_ref.shape, zero_ref.dtype)
    chip = lax.axis_index("expert") // 2
    slots = new_ref.shape[0]
    experts = home_ref.shape[0]
    for copy in copies[:4]:
        copy.wait()
    picks = jnp.concatenate([ids_ref[...], reps_ref[...]], axis=0)
    picks_ref[...] = picks
    row = lax.broadcasted_iota(jnp.int32, table_ref.shape, 0)
    lane = lax.broadcasted_iota(jnp.int32, table_ref.shape, 1)
    table = jnp.zeros(table_ref.shape, jnp.int32)
    for expert in range(experts):
        table = jnp.where((row == 0) & (lane == expert), home_ref[expert], table)
    for at in range(2 * SQUARE):
        slot = 2 * (chip ^ (at // 2)) + at % 2
        mine = new_ref[slot]
        rank = jnp.int32(0)
        for other in range(slots):
            rank = rank + ((new_ref[other] == mine) & (slot > other)).astype(jnp.int32)
        table = jnp.where((row == 1) & (lane == at), mine, table)
        table = jnp.where((row == 2) & (lane == at), rank, table)
    table_ref[...] = table

    def rows():
        copies[4].wait()
        return x_ref[...]

    pick(cap, table, picks, rows, blocks, sel_ref, experts)
    for copy in copies[5:]:
        copy.wait()


def pick_far_kernel(cap, experts, table_ref, x_ref, picks_ref, *refs):
    blocks, sel_ref = refs[:SQUARE], refs[SQUARE]
    pick(cap, table_ref[...], picks_ref[...], lambda: x_ref[...], blocks, sel_ref, experts)


def pick_shapes(cap, x, batches):
    high = block_rows(batches, cap)
    count, width = x.shape
    lanes = block_lanes(batches * cap, width) + LANES
    block = jax.ShapeDtypeStruct((TILE, lanes), jnp.bfloat16)
    sel = jax.ShapeDtypeStruct((SQUARE * high, count), jnp.bfloat16)
    cost = pl.CostEstimate(
        flops=2 * SQUARE * high * count * width,
        bytes_accessed=4 * SQUARE * high * width,
        transcendentals=0,
    )
    return [block] * SQUARE + [sel], cost


def pick_own(cap, home, new, x, ids, reps, panels):
    batches, tokens = ids.shape
    shapes, cost = pick_shapes(cap, x, batches)
    shapes += [
        jax.ShapeDtypeStruct((8, LANES), jnp.int32),
        jax.ShapeDtypeStruct((2 * batches, tokens), jnp.int32),
        jax.ShapeDtypeStruct((8, LANES), jnp.float32),
    ]
    shapes += [jax.ShapeDtypeStruct(panel.shape, panel.dtype) for panel in panels]
    return pl.pallas_call(
        functools.partial(pick_own_kernel, cap),
        out_shape=shapes,
        in_specs=[pl.BlockSpec(memory_space=HBM)] * (5 + len(panels)),
        out_specs=[pl.BlockSpec(memory_space=VMEM)] * len(shapes),
        scratch_shapes=[
            SMEM(home.shape, jnp.int32),
            SMEM(new.shape, jnp.int32),
            VMEM(x.shape, x.dtype),
            VMEM(ids.shape, ids.dtype),
            VMEM(reps.shape, reps.dtype),
            pltpu.SemaphoreType.DMA((5 + len(panels),)),
        ],
        cost_estimate=cost,
        compiler_params=pltpu.CompilerParams(vmem_limit_bytes=LARGE),
    )(*(pltpu.with_memory_space_constraint(value, HBM) for value in (home, new, x, ids, reps, *panels)))


def pick_far(cap, experts, table, x, picks):
    shapes, cost = pick_shapes(cap, x, picks.shape[0] // 2)
    return pl.pallas_call(
        functools.partial(pick_far_kernel, cap, experts),
        out_shape=shapes,
        in_specs=[pl.BlockSpec(memory_space=VMEM)] * 3,
        out_specs=[pl.BlockSpec(memory_space=VMEM)] * (SQUARE + 1),
        cost_estimate=cost,
        compiler_params=pltpu.CompilerParams(vmem_limit_bytes=SMALL),
    )(table, x, picks)


def fetch_kernel(*refs):
    count = len(refs) // 2
    sources, targets, sem = refs[:count], refs[count : 2 * count], refs[2 * count]
    copies = [
        pltpu.make_async_copy(source, target, sem.at[index])
        for index, (source, target) in enumerate(zip(sources, targets))
    ]
    for copy in copies:
        copy.start()
    for copy in copies:
        copy.wait()


def fetched(values):
    count = len(values)
    return pl.pallas_call(
        fetch_kernel,
        out_shape=[jax.ShapeDtypeStruct(value.shape, value.dtype) for value in values],
        in_specs=[pl.BlockSpec(memory_space=HBM)] * count,
        out_specs=[pl.BlockSpec(memory_space=VMEM)] * count,
        scratch_shapes=[pltpu.SemaphoreType.DMA((count,))],
        cost_estimate=pl.CostEstimate(
            flops=0, bytes_accessed=4 * sum(value.size for value in values), transcendentals=0
        ),
        compiler_params=pltpu.CompilerParams(vmem_limit_bytes=LARGE),
    )(*(pltpu.with_memory_space_constraint(value, HBM) for value in values))


def expert_kernel(count, *refs):
    blocks, panels, prior_ref = refs[:SQUARE], refs[SQUARE : SQUARE + 6], refs[SQUARE + 6]
    outs, load_ref = refs[SQUARE + 7 : 2 * SQUARE + 7], refs[2 * SQUARE + 7]
    x = stacked(count, panels[0].shape[1], blocks)
    high = x.shape[0] // SQUARE
    contract = (((1,), (1,)), ((), ()))
    load = prior_ref[...]
    for block in blocks:
        load = load + block[:, block.shape[1] - LANES :].astype(jnp.float32)
    load_ref[...] = load
    total = None
    for gate_ref, up_ref, down_ref in (panels[:3], panels[3:]):
        gate = jnp.dot(x, gate_ref[0], preferred_element_type=jnp.float32)
        up = jnp.dot(x, up_ref[0], preferred_element_type=jnp.float32)
        hidden = (gate / (1.0 + jnp.exp(-gate)) * up).astype(jnp.bfloat16)
        part = lax.dot_general(hidden, down_ref[0], contract, preferred_element_type=jnp.float32)
        total = part if total is None else total + part
    for q in range(SQUARE):
        packed(count, total[q * high : (q + 1) * high], outs[q])


def run_expert(count, blocks, panels, panels_far, prior):
    width, half = panels[0].shape[1:]
    rows = SQUARE * count
    block = jax.ShapeDtypeStruct((TILE, block_lanes(count, width)), jnp.bfloat16)
    return pl.pallas_call(
        functools.partial(expert_kernel, count),
        out_shape=[block] * SQUARE
        + [jax.ShapeDtypeStruct(prior.shape, prior.dtype)],
        in_specs=[pl.BlockSpec(memory_space=VMEM)] * (SQUARE + 7),
        out_specs=[pl.BlockSpec(memory_space=VMEM)] * (SQUARE + 1),
        cost_estimate=pl.CostEstimate(
            flops=2 * rows * width * half * 6,
            bytes_accessed=6 * 2 * width * half + 4 * rows * width,
            transcendentals=2 * rows * half,
        ),
        compiler_params=pltpu.CompilerParams(vmem_limit_bytes=LARGE),
    )(*blocks, *panels, *panels_far, prior)


def chosen(count, width, sel_ref, blocks):
    y = stacked(count, width, blocks)
    return lax.dot_general(
        sel_ref[...], y, (((0,), (0,)), ((), ())), preferred_element_type=jnp.float32
    )


def merge_kernel(count, sel_ref, *refs):
    width = refs[SQUARE].shape[1]
    refs[SQUARE][...] = chosen(count, width, sel_ref, refs[:SQUARE]).astype(jnp.bfloat16)


def merge_own_kernel(count, sel_ref, weight_ref, *refs):
    out_ref, scale_ref = refs[SQUARE:]
    width = out_ref.shape[1]
    out_ref[...] = chosen(count, width, sel_ref, refs[:SQUARE]).astype(jnp.bfloat16)
    batches, tokens = weight_ref.shape
    lane = lax.broadcasted_iota(jnp.int32, (tokens, tokens), 0)
    same = lane == lax.broadcasted_iota(jnp.int32, (tokens, tokens), 1)
    for batch in range(batches):
        column = jnp.where(same, weight_ref[batch : batch + 1, :], 0.0)
        column = jnp.sum(column, axis=1, keepdims=True)
        scale_ref[batch * tokens : (batch + 1) * tokens, :] = jnp.broadcast_to(
            column, (tokens, LANES)
        )


def final_kernel(own_ref, scale_ref, load_ref, load_far_ref, back_ref, out_ref, slot_ref):
    core = lax.axis_index("expert") % 2
    both = load_ref[...] + load_far_ref[...]
    row = lax.broadcasted_iota(jnp.int32, both.shape, 0)
    lane = lax.broadcasted_iota(jnp.int32, both.shape, 1)
    slot_ref[0] = jnp.sum(jnp.where((row == 0) & (lane == core), both, 0.0)).astype(
        jnp.int32
    )
    total = own_ref[...].astype(jnp.float32) + back_ref[...].astype(jnp.float32)
    out_ref[...] = (total * scale_ref[:, :1]).astype(jnp.bfloat16)


def small_call(kernel, shapes, *operands, slot=False):
    specs = [pl.BlockSpec(memory_space=VMEM)] * len(shapes)
    if slot:
        shapes = shapes + [jax.ShapeDtypeStruct((1,), jnp.int32)]
        specs = specs + [pl.BlockSpec(memory_space=SMEM)]
    return pl.pallas_call(
        kernel,
        out_shape=shapes,
        in_specs=[pl.BlockSpec(memory_space=VMEM)] * len(operands),
        out_specs=specs,
        cost_estimate=pl.CostEstimate(
            flops=2 * sum(shape.size for shape in shapes) * LANES,
            bytes_accessed=2 * sum(operand.size for operand in operands),
            transcendentals=0,
        ),
        compiler_params=pltpu.CompilerParams(vmem_limit_bytes=SMALL),
    )(*operands)


def swapped(size, bits):
    return [(index, index ^ bits) for index in range(size)]


def dispatched(
    activations,
    pick_weight,
    expert_ids,
    replica,
    old_home,
    new_expert,
    gate_panel,
    up_panel,
    down_panel,
):
    size = lax.axis_size("expert")
    batches, tokens, width = activations.shape
    rows = batches * tokens
    cap = min(CAP * REPL, tokens)
    count = batches * cap
    distant = 2 * SQUARE

    def swap(value, bits):
        return lax.ppermute(value, "expert", swapped(size, bits))

    def around(blocks):
        return [blocks[0]] + [swap(blocks[q], 2 * q) for q in range(1, SQUARE)]

    x = activations.reshape(rows, width)
    x_far = swap(x, distant)
    panels = (gate_panel, up_panel, down_panel)
    panels_far = [swap(panel, 1) for panel in panels]
    *blocks, sel, table, picks, zero, gate_own, up_own = pick_own(
        cap,
        old_home,
        new_expert,
        x,
        expert_ids.reshape(batches, tokens),
        replica.reshape(batches, tokens),
        panels[:PANELS],
    )
    picks_far = swap(picks, distant)
    blocks = around(blocks)
    *blocks_far, sel_far = pick_far(cap, old_home.shape[0], table, x_far, picks_far)
    blocks_far = around(blocks_far)
    panels = (gate_own, up_own, *fetched(panels[PANELS:]))
    *results, load = run_expert(count, blocks, panels, panels_far, zero)
    *results_far, load = run_expert(count, blocks_far, panels, panels_far, load)
    results_far = around(results_far)
    results = around(results)
    load_far = swap(load, 1)
    whole = jax.ShapeDtypeStruct((rows, width), jnp.bfloat16)
    (far,) = small_call(functools.partial(merge_kernel, count), [whole], sel_far, *results_far)
    back = swap(far, distant)
    weight = pick_weight.reshape(batches, tokens)
    own, scale = small_call(
        functools.partial(merge_own_kernel, count),
        [whole, jax.ShapeDtypeStruct((rows, LANES), jnp.float32)],
        sel,
        weight,
        *results,
    )
    output, slot_load = small_call(
        final_kernel,
        [whole],
        own,
        scale,
        load,
        load_far,
        back,
        slot=True,
    )
    return output.reshape(batches, tokens, width), slot_load


def solution(mesh):
    chips = mesh.shape["expert"] // 2

    def per_device(*args):
        if direct(args):
            return dispatched(*args)
        return gathered(*args)

    def direct(args):
        return chips == 2 * SQUARE and args[2].shape[2] == 1

    return jax.shard_map(
        per_device,
        mesh=mesh,
        in_specs=(
            P(None, ("groups", "expert"), None),
            P(None, ("groups", "expert"), None),
            P(None, ("groups", "expert"), None),
            P(None, ("groups", "expert"), None),
            P(),
            P("groups"),
            P("expert", None, None),
            P("expert", None, None),
            P("expert", None, None),
        ),
        out_specs=(P(None, ("groups", "expert"), None), P(("groups", "expert"))),
        check_vma=False,
    )
```

```python
import functools

import jax
import jax.numpy as jnp
from jax import lax
from jax.experimental import pallas as pl
from jax.experimental.pallas import tpu as pltpu
from jax.sharding import PartitionSpec as P


CAP = 2
REPL = 5
LANES = 128
SQUARE = 4
TILE = 8
PEERS = ((0, 1, 2, 3), (0, 3, 1, 2))
PANELS = 2
SMALL = 4 << 20
LARGE = 20 << 20
VMEM = pltpu.VMEM
SMEM = pltpu.SMEM
HBM = pltpu.MemorySpace.HBM


def slot_rank(new_expert, me):
    positions = jnp.arange(new_expert.shape[0], dtype=jnp.int32)
    mine = jnp.sum(jnp.where(positions == me, new_expert, 0))
    rank = jnp.sum(((new_expert == mine) & (positions < me)).astype(jnp.int32))
    return mine, rank


def gathered(
    activations,
    pick_weight,
    expert_ids,
    replica,
    old_home,
    new_expert,
    gate_panel,
    up_panel,
    down_panel,
):
    me = lax.axis_index("expert")
    batches, tokens, width = activations.shape
    top = expert_ids.shape[2]
    rows = batches * tokens
    x = activations.reshape(rows, width)
    picks = jnp.concatenate([expert_ids.reshape(rows, top), replica.reshape(rows, top)], axis=1)
    weights = pick_weight.reshape(rows, top)
    picks_all = lax.all_gather(picks, "expert", axis=0, tiled=True)
    weights_all = lax.all_gather(weights, "expert", axis=0, tiled=True)
    x_all = lax.all_gather(x, "expert", axis=0, tiled=True)
    ids_all = picks_all[:, :top]
    rep_all = picks_all[:, top:]
    mine, rank = slot_rank(new_expert, me)
    load = jnp.sum(((ids_all == mine) & (rep_all == rank)).astype(jnp.int32))
    labels = jnp.arange(old_home.shape[0], dtype=jnp.int32)
    held = jnp.sum(jnp.where(old_home == me // 2, labels, 0))
    scale = jnp.sum(jnp.where(ids_all == held, weights_all, 0.0), axis=1, keepdims=True)
    gate = jnp.dot(x_all, gate_panel[0], preferred_element_type=jnp.float32)
    up = jnp.dot(x_all, up_panel[0], preferred_element_type=jnp.float32)
    hidden = (jax.nn.silu(gate) * up).astype(jnp.bfloat16)
    part = lax.dot_general(
        hidden, down_panel[0], (((1,), (1,)), ((), ())), preferred_element_type=jnp.float32
    )
    part = (part * scale).astype(jnp.bfloat16)
    total = lax.psum_scatter(part, "expert", scatter_dimension=0, tiled=True)
    return total.reshape(batches, tokens, width), load.reshape(1)


def steps(index, size, count):
    whole = jnp.zeros_like(index)
    for step in range(1, count):
        whole = whole + (index >= step * size).astype(jnp.int32)
    return whole


def peer_of(slot, core):
    value = jnp.zeros_like(slot)
    for index in range(1, SQUARE):
        peer = jnp.where(core == 0, PEERS[0][index], PEERS[1][index])
        value = jnp.where(slot == index, peer, value)
    return value


def tiling(count):
    full, rest = divmod(count, TILE)
    fold = TILE // rest if rest and TILE % rest == 0 else 1
    if rest and fold == 1:
        full, rest = full + 1, 0
    return full, rest, fold


def block_rows(batches, cap):
    return -(-batches * cap // TILE) * TILE


def block_lanes(count, width):
    full, rest, fold = tiling(count)
    return full * width + (width // fold if rest else 0)


def packed(count, rows, ref):
    full, rest, fold = tiling(count)
    width = rows.shape[1]
    for tile in range(full):
        part = rows[tile * TILE : (tile + 1) * TILE]
        ref[:, tile * width : (tile + 1) * width] = part.astype(ref.dtype)
    if rest:
        tail = rows[full * TILE : (full + 1) * TILE]
        piece = width // fold
        turn = steps(lax.broadcasted_iota(jnp.int32, (TILE, piece), 0), rest, fold)
        value = tail[:, :piece]
        for index in range(1, fold):
            moved = pltpu.roll(tail[:, index * piece : (index + 1) * piece], index * rest, axis=0)
            value = jnp.where(turn == index, moved, value)
        ref[:, full * width : full * width + piece] = value.astype(ref.dtype)


def unpacked(count, width, ref):
    full, rest, fold = tiling(count)
    tiles = [ref[:, tile * width : (tile + 1) * width] for tile in range(full)]
    if rest:
        piece = width // fold
        tail = ref[:, full * width : full * width + piece].astype(jnp.float32)
        parts = [tail]
        for index in range(1, fold):
            parts.append(pltpu.roll(tail, TILE - index * rest, axis=0))
        tiles.append(jnp.concatenate(parts, axis=1).astype(ref.dtype))
    return tiles


def stacked(count, width, refs):
    tiles = [tile for ref in refs for tile in unpacked(count, width, ref)]
    return jnp.concatenate(tiles, axis=0)


def pick(cap, table, picks, x, blocks, sel_ref, experts):
    batches, tokens = picks.shape[0] // 2, picks.shape[1]
    count = batches * tokens
    high = block_rows(batches, cap)
    chip = lax.axis_index("expert") // 2
    side = lax.axis_index("expert") % 2

    def batch_of(index):
        return steps(index, tokens, batches)

    col = lax.broadcasted_iota(jnp.int32, (tokens, count), 1)
    spread = col - tokens * batch_of(col) == lax.broadcasted_iota(jnp.int32, (tokens, count), 0)
    spread = spread.astype(jnp.float32)
    own_lane = batch_of(lax.broadcasted_iota(jnp.int32, (batches, count), 1))
    own_lane = own_lane == lax.broadcasted_iota(jnp.int32, (batches, count), 0)

    def row_of(values):
        wide = jnp.dot(values.astype(jnp.float32), spread, preferred_element_type=jnp.float32)
        return jnp.sum(jnp.where(own_lane, wide, 0.0), axis=0, keepdims=True).astype(jnp.int32)

    ids = row_of(picks[:batches, :])
    reps = row_of(picks[batches:, :])
    target = jnp.zeros_like(ids)
    for expert in range(experts):
        target = jnp.where(ids == expert, table[0:1, expert : expert + 1], target)

    sub = lax.broadcasted_iota(jnp.int32, (8, count), 0)
    inside = (target == (sub ^ chip)) & (sub < SQUARE)
    before_from = lax.broadcasted_iota(jnp.int32, (count, count), 0)
    before_to = lax.broadcasted_iota(jnp.int32, (count, count), 1)
    before = (before_from < before_to) & (batch_of(before_from) == batch_of(before_to))
    earlier = jnp.dot(
        inside.astype(jnp.bfloat16),
        before.astype(jnp.bfloat16),
        preferred_element_type=jnp.float32,
    )
    position = jnp.sum(jnp.where(inside, earlier, 0.0), axis=0, keepdims=True).astype(jnp.int32)

    row = lax.broadcasted_iota(jnp.int32, (SQUARE * high, count), 0)
    peer = steps(row, high, SQUARE)
    left = row - high * peer
    peer = peer_of(peer, side)
    group = steps(left, cap, batches + 1)
    left = left - cap * group
    lane = batch_of(lax.broadcasted_iota(jnp.int32, (SQUARE * high, count), 1))
    sel = ((target == (peer ^ chip)) & (position == left) & (group == lane)).astype(jnp.bfloat16)
    sel_ref[...] = sel
    meta_lane = lax.broadcasted_iota(jnp.int32, (TILE, LANES), 1)
    x = x()
    for q in range(SQUARE):
        part = jnp.dot(sel[q * high : (q + 1) * high], x, preferred_element_type=jnp.float32)
        meta = jnp.zeros((TILE, LANES), jnp.float32)
        for core in range(2):
            at = 2 * q + core
            hits = (ids == table[1:2, at : at + 1]) & (reps == table[2:3, at : at + 1])
            load = jnp.sum(hits.astype(jnp.float32), axis=1, keepdims=True)
            meta = jnp.where(meta_lane == core, load, meta)
        packed(batches * cap, part, blocks[q])
        blocks[q][:, blocks[q].shape[1] - LANES :] = meta.astype(jnp.bfloat16)


def pick_own_kernel(cap, home_hbm, new_hbm, x_hbm, ids_hbm, reps_hbm, *refs):
    panels_hbm, refs = refs[:PANELS], refs[PANELS:]
    blocks, (sel_ref, table_ref, picks_ref, zero_ref) = refs[:SQUARE], refs[SQUARE : SQUARE + 4]
    panels, refs = refs[SQUARE + 4 : SQUARE + 4 + PANELS], refs[SQUARE + 4 + PANELS :]
    home_ref, new_ref, x_ref, ids_ref, reps_ref, sem = refs
    sources = (home_hbm, new_hbm, ids_hbm, reps_hbm, x_hbm, *panels_hbm)
    targets = (home_ref, new_ref, ids_ref, reps_ref, x_ref, *panels)
    copies = [
        pltpu.make_async_copy(source, target, sem.at[index])
        for index, (source, target) in enumerate(zip(sources, targets))
    ]
    for copy in copies:
        copy.start()
    zero_ref[...] = jnp.zeros(zero_ref.shape, zero_ref.dtype)
    chip = lax.axis_index("expert") // 2
    side = lax.axis_index("expert") % 2
    slots = new_ref.shape[0]
    experts = home_ref.shape[0]
    for copy in copies[:4]:
        copy.wait()
    picks = jnp.concatenate([ids_ref[...], reps_ref[...]], axis=0)
    picks_ref[...] = picks
    row = lax.broadcasted_iota(jnp.int32, table_ref.shape, 0)
    lane = lax.broadcasted_iota(jnp.int32, table_ref.shape, 1)
    table = jnp.zeros(table_ref.shape, jnp.int32)
    for expert in range(experts):
        table = jnp.where((row == 0) & (lane == expert), home_ref[expert], table)
    for at in range(2 * SQUARE):
        slot = 2 * (chip ^ peer_of(jnp.int32(at // 2), side)) + at % 2
        mine = new_ref[slot]
        rank = jnp.int32(0)
        for other in range(slots):
            rank = rank + ((new_ref[other] == mine) & (slot > other)).astype(jnp.int32)
        table = jnp.where((row == 1) & (lane == at), mine, table)
        table = jnp.where((row == 2) & (lane == at), rank, table)
    table_ref[...] = table

    def rows():
        copies[4].wait()
        return x_ref[...]

    pick(cap, table, picks, rows, blocks, sel_ref, experts)
    for copy in copies[5:]:
        copy.wait()


def pick_far_kernel(cap, experts, table_ref, x_ref, picks_ref, *refs):
    blocks, sel_ref = refs[:SQUARE], refs[SQUARE]
    pick(cap, table_ref[...], picks_ref[...], lambda: x_ref[...], blocks, sel_ref, experts)


def pick_shapes(cap, x, batches):
    high = block_rows(batches, cap)
    count, width = x.shape
    lanes = block_lanes(batches * cap, width) + LANES
    block = jax.ShapeDtypeStruct((TILE, lanes), jnp.bfloat16)
    sel = jax.ShapeDtypeStruct((SQUARE * high, count), jnp.bfloat16)
    cost = pl.CostEstimate(
        flops=2 * SQUARE * high * count * width,
        bytes_accessed=4 * SQUARE * high * width,
        transcendentals=0,
    )
    return [block] * SQUARE + [sel], cost


def pick_own(cap, home, new, x, ids, reps, panels):
    batches, tokens = ids.shape
    shapes, cost = pick_shapes(cap, x, batches)
    shapes += [
        jax.ShapeDtypeStruct((8, LANES), jnp.int32),
        jax.ShapeDtypeStruct((2 * batches, tokens), jnp.int32),
        jax.ShapeDtypeStruct((8, LANES), jnp.float32),
    ]
    shapes += [jax.ShapeDtypeStruct(panel.shape, panel.dtype) for panel in panels]
    return pl.pallas_call(
        functools.partial(pick_own_kernel, cap),
        out_shape=shapes,
        in_specs=[pl.BlockSpec(memory_space=HBM)] * (5 + len(panels)),
        out_specs=[pl.BlockSpec(memory_space=VMEM)] * len(shapes),
        scratch_shapes=[
            SMEM(home.shape, jnp.int32),
            SMEM(new.shape, jnp.int32),
            VMEM(x.shape, x.dtype),
            VMEM(ids.shape, ids.dtype),
            VMEM(reps.shape, reps.dtype),
            pltpu.SemaphoreType.DMA((5 + len(panels),)),
        ],
        cost_estimate=cost,
        compiler_params=pltpu.CompilerParams(vmem_limit_bytes=LARGE),
    )(*(pltpu.with_memory_space_constraint(value, HBM) for value in (home, new, x, ids, reps, *panels)))


def pick_far(cap, experts, table, x, picks):
    shapes, cost = pick_shapes(cap, x, picks.shape[0] // 2)
    return pl.pallas_call(
        functools.partial(pick_far_kernel, cap, experts),
        out_shape=shapes,
        in_specs=[pl.BlockSpec(memory_space=VMEM)] * 3,
        out_specs=[pl.BlockSpec(memory_space=VMEM)] * (SQUARE + 1),
        cost_estimate=cost,
        compiler_params=pltpu.CompilerParams(vmem_limit_bytes=SMALL),
    )(table, x, picks)


def fetch_kernel(*refs):
    count = len(refs) // 2
    sources, targets, sem = refs[:count], refs[count : 2 * count], refs[2 * count]
    copies = [
        pltpu.make_async_copy(source, target, sem.at[index])
        for index, (source, target) in enumerate(zip(sources, targets))
    ]
    for copy in copies:
        copy.start()
    for copy in copies:
        copy.wait()


def fetched(values):
    count = len(values)
    return pl.pallas_call(
        fetch_kernel,
        out_shape=[jax.ShapeDtypeStruct(value.shape, value.dtype) for value in values],
        in_specs=[pl.BlockSpec(memory_space=HBM)] * count,
        out_specs=[pl.BlockSpec(memory_space=VMEM)] * count,
        scratch_shapes=[pltpu.SemaphoreType.DMA((count,))],
        cost_estimate=pl.CostEstimate(
            flops=0, bytes_accessed=4 * sum(value.size for value in values), transcendentals=0
        ),
        compiler_params=pltpu.CompilerParams(vmem_limit_bytes=LARGE),
    )(*(pltpu.with_memory_space_constraint(value, HBM) for value in values))


def expert_kernel(count, *refs):
    blocks, panels, prior_ref = refs[:SQUARE], refs[SQUARE : SQUARE + 6], refs[SQUARE + 6]
    outs, load_ref = refs[SQUARE + 7 : 2 * SQUARE + 7], refs[2 * SQUARE + 7]
    x = stacked(count, panels[0].shape[1], blocks)
    high = x.shape[0] // SQUARE
    contract = (((1,), (1,)), ((), ()))
    load = prior_ref[...]
    for block in blocks:
        load = load + block[:, block.shape[1] - LANES :].astype(jnp.float32)
    load_ref[...] = load
    total = None
    for gate_ref, up_ref, down_ref in (panels[:3], panels[3:]):
        gate = jnp.dot(x, gate_ref[0], preferred_element_type=jnp.float32)
        up = jnp.dot(x, up_ref[0], preferred_element_type=jnp.float32)
        hidden = (gate / (1.0 + jnp.exp(-gate)) * up).astype(jnp.bfloat16)
        part = lax.dot_general(hidden, down_ref[0], contract, preferred_element_type=jnp.float32)
        total = part if total is None else total + part
    for q in range(SQUARE):
        packed(count, total[q * high : (q + 1) * high], outs[q])


def run_expert(count, blocks, panels, panels_far, prior):
    width, half = panels[0].shape[1:]
    rows = SQUARE * count
    block = jax.ShapeDtypeStruct((TILE, block_lanes(count, width)), jnp.bfloat16)
    return pl.pallas_call(
        functools.partial(expert_kernel, count),
        out_shape=[block] * SQUARE
        + [jax.ShapeDtypeStruct(prior.shape, prior.dtype)],
        in_specs=[pl.BlockSpec(memory_space=VMEM)] * (SQUARE + 7),
        out_specs=[pl.BlockSpec(memory_space=VMEM)] * (SQUARE + 1),
        cost_estimate=pl.CostEstimate(
            flops=2 * rows * width * half * 6,
            bytes_accessed=6 * 2 * width * half + 4 * rows * width,
            transcendentals=2 * rows * half,
        ),
        compiler_params=pltpu.CompilerParams(vmem_limit_bytes=LARGE),
    )(*blocks, *panels, *panels_far, prior)


def chosen(count, width, sel_ref, blocks):
    y = stacked(count, width, blocks)
    return lax.dot_general(
        sel_ref[...], y, (((0,), (0,)), ((), ())), preferred_element_type=jnp.float32
    )


def merge_kernel(count, sel_ref, *refs):
    width = refs[SQUARE].shape[1]
    refs[SQUARE][...] = chosen(count, width, sel_ref, refs[:SQUARE]).astype(jnp.bfloat16)


def merge_own_kernel(count, sel_ref, weight_ref, *refs):
    out_ref, scale_ref = refs[SQUARE:]
    width = out_ref.shape[1]
    out_ref[...] = chosen(count, width, sel_ref, refs[:SQUARE]).astype(jnp.bfloat16)
    batches, tokens = weight_ref.shape
    lane = lax.broadcasted_iota(jnp.int32, (tokens, tokens), 0)
    same = lane == lax.broadcasted_iota(jnp.int32, (tokens, tokens), 1)
    for batch in range(batches):
        column = jnp.where(same, weight_ref[batch : batch + 1, :], 0.0)
        column = jnp.sum(column, axis=1, keepdims=True)
        scale_ref[batch * tokens : (batch + 1) * tokens, :] = jnp.broadcast_to(
            column, (tokens, LANES)
        )


def final_kernel(own_ref, scale_ref, load_ref, load_far_ref, back_ref, out_ref, slot_ref):
    core = lax.axis_index("expert") % 2
    both = load_ref[...] + load_far_ref[...]
    row = lax.broadcasted_iota(jnp.int32, both.shape, 0)
    lane = lax.broadcasted_iota(jnp.int32, both.shape, 1)
    slot_ref[0] = jnp.sum(jnp.where((row == 0) & (lane == core), both, 0.0)).astype(
        jnp.int32
    )
    total = own_ref[...].astype(jnp.float32) + back_ref[...].astype(jnp.float32)
    out_ref[...] = (total * scale_ref[:, :1]).astype(jnp.bfloat16)


def small_call(kernel, shapes, *operands, slot=False):
    specs = [pl.BlockSpec(memory_space=VMEM)] * len(shapes)
    if slot:
        shapes = shapes + [jax.ShapeDtypeStruct((1,), jnp.int32)]
        specs = specs + [pl.BlockSpec(memory_space=SMEM)]
    return pl.pallas_call(
        kernel,
        out_shape=shapes,
        in_specs=[pl.BlockSpec(memory_space=VMEM)] * len(operands),
        out_specs=specs,
        cost_estimate=pl.CostEstimate(
            flops=2 * sum(shape.size for shape in shapes) * LANES,
            bytes_accessed=2 * sum(operand.size for operand in operands),
            transcendentals=0,
        ),
        compiler_params=pltpu.CompilerParams(vmem_limit_bytes=SMALL),
    )(*operands)


def swapped(size, bits):
    return [(index, index ^ bits[index % 2]) for index in range(size)]


def dispatched(
    activations,
    pick_weight,
    expert_ids,
    replica,
    old_home,
    new_expert,
    gate_panel,
    up_panel,
    down_panel,
):
    size = lax.axis_size("expert")
    batches, tokens, width = activations.shape
    rows = batches * tokens
    cap = min(CAP * REPL, tokens)
    count = batches * cap
    distant = (2 * SQUARE, 2 * SQUARE)
    beside = (1, 1)

    def swap(value, bits):
        return lax.ppermute(value, "expert", swapped(size, bits))

    def around(blocks):
        return [blocks[0]] + [
            swap(blocks[q], [2 * order[q] for order in PEERS])
            for q in range(1, SQUARE)
        ]

    x = activations.reshape(rows, width)
    x_far = swap(x, distant)
    panels = (gate_panel, up_panel, down_panel)
    panels_far = [swap(panel, beside) for panel in panels]
    *blocks, sel, table, picks, zero, gate_own, up_own = pick_own(
        cap,
        old_home,
        new_expert,
        x,
        expert_ids.reshape(batches, tokens),
        replica.reshape(batches, tokens),
        panels[:PANELS],
    )
    picks_far = swap(picks, distant)
    blocks = around(blocks)
    *blocks_far, sel_far = pick_far(cap, old_home.shape[0], table, x_far, picks_far)
    blocks_far = around(blocks_far)
    panels = (gate_own, up_own, *fetched(panels[PANELS:]))
    *results, load = run_expert(count, blocks, panels, panels_far, zero)
    *results_far, load = run_expert(count, blocks_far, panels, panels_far, load)
    results_far = around(results_far)
    results = around(results)
    load_far = swap(load, beside)
    whole = jax.ShapeDtypeStruct((rows, width), jnp.bfloat16)
    (far,) = small_call(functools.partial(merge_kernel, count), [whole], sel_far, *results_far)
    back = swap(far, distant)
    weight = pick_weight.reshape(batches, tokens)
    own, scale = small_call(
        functools.partial(merge_own_kernel, count),
        [whole, jax.ShapeDtypeStruct((rows, LANES), jnp.float32)],
        sel,
        weight,
        *results,
    )
    output, slot_load = small_call(
        final_kernel,
        [whole],
        own,
        scale,
        load,
        load_far,
        back,
        slot=True,
    )
    return output.reshape(batches, tokens, width), slot_load


def solution(mesh):
    chips = mesh.shape["expert"] // 2

    def per_device(*args):
        if direct(args):
            return dispatched(*args)
        return gathered(*args)

    def direct(args):
        return chips == 2 * SQUARE and args[2].shape[2] == 1

    return jax.shard_map(
        per_device,
        mesh=mesh,
        in_specs=(
            P(None, ("groups", "expert"), None),
            P(None, ("groups", "expert"), None),
            P(None, ("groups", "expert"), None),
            P(None, ("groups", "expert"), None),
            P(),
            P("groups"),
            P("expert", None, None),
            P("expert", None, None),
            P("expert", None, None),
        ),
        out_specs=(P(None, ("groups", "expert"), None), P(("groups", "expert"))),
        check_vma=False,
    )
```

```python
import functools

import jax
import jax.numpy as jnp
from jax import lax
from jax.experimental import pallas as pl
from jax.experimental.pallas import tpu as pltpu
from jax.sharding import PartitionSpec as P


CAP = 2
REPL = 5
LANES = 128
SQUARE = 4
TILE = 8
PEERS = ((0, 1, 2, 3), (0, 3, 1, 2))
SMALL = 4 << 20
LARGE = 20 << 20
VMEM = pltpu.VMEM
SMEM = pltpu.SMEM
HBM = pltpu.MemorySpace.HBM


def slot_rank(new_expert, me):
    positions = jnp.arange(new_expert.shape[0], dtype=jnp.int32)
    mine = jnp.sum(jnp.where(positions == me, new_expert, 0))
    rank = jnp.sum(((new_expert == mine) & (positions < me)).astype(jnp.int32))
    return mine, rank


def gathered(
    activations,
    pick_weight,
    expert_ids,
    replica,
    old_home,
    new_expert,
    gate_panel,
    up_panel,
    down_panel,
):
    me = lax.axis_index("expert")
    batches, tokens, width = activations.shape
    top = expert_ids.shape[2]
    rows = batches * tokens
    x = activations.reshape(rows, width)
    picks = jnp.concatenate([expert_ids.reshape(rows, top), replica.reshape(rows, top)], axis=1)
    weights = pick_weight.reshape(rows, top)
    picks_all = lax.all_gather(picks, "expert", axis=0, tiled=True)
    weights_all = lax.all_gather(weights, "expert", axis=0, tiled=True)
    x_all = lax.all_gather(x, "expert", axis=0, tiled=True)
    ids_all = picks_all[:, :top]
    rep_all = picks_all[:, top:]
    mine, rank = slot_rank(new_expert, me)
    load = jnp.sum(((ids_all == mine) & (rep_all == rank)).astype(jnp.int32))
    labels = jnp.arange(old_home.shape[0], dtype=jnp.int32)
    held = jnp.sum(jnp.where(old_home == me // 2, labels, 0))
    scale = jnp.sum(jnp.where(ids_all == held, weights_all, 0.0), axis=1, keepdims=True)
    gate = jnp.dot(x_all, gate_panel[0], preferred_element_type=jnp.float32)
    up = jnp.dot(x_all, up_panel[0], preferred_element_type=jnp.float32)
    hidden = (jax.nn.silu(gate) * up).astype(jnp.bfloat16)
    part = lax.dot_general(
        hidden, down_panel[0], (((1,), (1,)), ((), ())), preferred_element_type=jnp.float32
    )
    part = (part * scale).astype(jnp.bfloat16)
    total = lax.psum_scatter(part, "expert", scatter_dimension=0, tiled=True)
    return total.reshape(batches, tokens, width), load.reshape(1)


def steps(index, size, count):
    whole = jnp.zeros_like(index)
    for step in range(1, count):
        whole = whole + (index >= step * size).astype(jnp.int32)
    return whole


def peer_of(slot, core):
    value = jnp.zeros_like(slot)
    for index in range(1, SQUARE):
        peer = jnp.where(core == 0, PEERS[0][index], PEERS[1][index])
        value = jnp.where(slot == index, peer, value)
    return value


def tiling(count):
    full, rest = divmod(count, TILE)
    fold = TILE // rest if rest and TILE % rest == 0 else 1
    if rest and fold == 1:
        full, rest = full + 1, 0
    return full, rest, fold


def block_rows(batches, cap):
    return -(-batches * cap // TILE) * TILE


def block_lanes(count, width):
    full, rest, fold = tiling(count)
    return full * width + (width // fold if rest else 0)


def packed(count, rows, ref):
    full, rest, fold = tiling(count)
    width = rows.shape[1]
    for tile in range(full):
        part = rows[tile * TILE : (tile + 1) * TILE]
        ref[:, tile * width : (tile + 1) * width] = part.astype(ref.dtype)
    if rest:
        tail = rows[full * TILE : (full + 1) * TILE]
        piece = width // fold
        turn = steps(lax.broadcasted_iota(jnp.int32, (TILE, piece), 0), rest, fold)
        value = tail[:, :piece]
        for index in range(1, fold):
            moved = pltpu.roll(tail[:, index * piece : (index + 1) * piece], index * rest, axis=0)
            value = jnp.where(turn == index, moved, value)
        ref[:, full * width : full * width + piece] = value.astype(ref.dtype)


def unpacked(count, width, ref):
    full, rest, fold = tiling(count)
    tiles = [ref[:, tile * width : (tile + 1) * width] for tile in range(full)]
    if rest:
        piece = width // fold
        tail = ref[:, full * width : full * width + piece].astype(jnp.float32)
        parts = [tail]
        for index in range(1, fold):
            parts.append(pltpu.roll(tail, TILE - index * rest, axis=0))
        tiles.append(jnp.concatenate(parts, axis=1).astype(ref.dtype))
    return tiles


def stacked(count, width, refs):
    tiles = [tile for ref in refs for tile in unpacked(count, width, ref)]
    return jnp.concatenate(tiles, axis=0)


def pick(cap, table, picks, x, blocks, sel_ref, experts):
    batches, tokens = picks.shape[0] // 2, picks.shape[1]
    count = batches * tokens
    high = block_rows(batches, cap)
    chip = lax.axis_index("expert") // 2
    side = lax.axis_index("expert") % 2

    def batch_of(index):
        return steps(index, tokens, batches)

    col = lax.broadcasted_iota(jnp.int32, (tokens, count), 1)
    spread = col - tokens * batch_of(col) == lax.broadcasted_iota(jnp.int32, (tokens, count), 0)
    spread = spread.astype(jnp.float32)
    own_lane = batch_of(lax.broadcasted_iota(jnp.int32, (batches, count), 1))
    own_lane = own_lane == lax.broadcasted_iota(jnp.int32, (batches, count), 0)

    def row_of(values):
        wide = jnp.dot(values.astype(jnp.float32), spread, preferred_element_type=jnp.float32)
        return jnp.sum(jnp.where(own_lane, wide, 0.0), axis=0, keepdims=True).astype(jnp.int32)

    ids = row_of(picks[:batches, :])
    reps = row_of(picks[batches:, :])
    target = jnp.zeros_like(ids)
    for expert in range(experts):
        target = jnp.where(ids == expert, table[0:1, expert : expert + 1], target)

    sub = lax.broadcasted_iota(jnp.int32, (8, count), 0)
    inside = (target == (sub ^ chip)) & (sub < SQUARE)
    before_from = lax.broadcasted_iota(jnp.int32, (count, count), 0)
    before_to = lax.broadcasted_iota(jnp.int32, (count, count), 1)
    before = (before_from < before_to) & (batch_of(before_from) == batch_of(before_to))
    earlier = jnp.dot(
        inside.astype(jnp.bfloat16),
        before.astype(jnp.bfloat16),
        preferred_element_type=jnp.float32,
    )
    position = jnp.sum(jnp.where(inside, earlier, 0.0), axis=0, keepdims=True).astype(jnp.int32)

    row = lax.broadcasted_iota(jnp.int32, (SQUARE * high, count), 0)
    peer = steps(row, high, SQUARE)
    left = row - high * peer
    peer = peer_of(peer, side)
    group = steps(left, cap, batches + 1)
    left = left - cap * group
    lane = batch_of(lax.broadcasted_iota(jnp.int32, (SQUARE * high, count), 1))
    sel = ((target == (peer ^ chip)) & (position == left) & (group == lane)).astype(jnp.bfloat16)
    sel_ref[...] = sel
    meta_lane = lax.broadcasted_iota(jnp.int32, (TILE, LANES), 1)
    x = x()
    for q in range(SQUARE):
        part = jnp.dot(sel[q * high : (q + 1) * high], x, preferred_element_type=jnp.float32)
        meta = jnp.zeros((TILE, LANES), jnp.float32)
        for core in range(2):
            at = 2 * q + core
            hits = (ids == table[1:2, at : at + 1]) & (reps == table[2:3, at : at + 1])
            load = jnp.sum(hits.astype(jnp.float32), axis=1, keepdims=True)
            meta = jnp.where(meta_lane == core, load, meta)
        packed(batches * cap, part, blocks[q])
        blocks[q][:, blocks[q].shape[1] - LANES :] = meta.astype(jnp.bfloat16)


def pick_own_kernel(cap, home_hbm, new_hbm, x_hbm, ids_hbm, reps_hbm, *refs):
    blocks, (sel_ref, table_ref, picks_ref, zero_ref) = refs[:SQUARE], refs[SQUARE : SQUARE + 4]
    home_ref, new_ref, x_ref, ids_ref, reps_ref, sem = refs[SQUARE + 4 :]
    sources = (home_hbm, new_hbm, ids_hbm, reps_hbm, x_hbm)
    targets = (home_ref, new_ref, ids_ref, reps_ref, x_ref)
    copies = [
        pltpu.make_async_copy(source, target, sem.at[index])
        for index, (source, target) in enumerate(zip(sources, targets))
    ]
    for copy in copies:
        copy.start()
    zero_ref[...] = jnp.zeros(zero_ref.shape, zero_ref.dtype)
    chip = lax.axis_index("expert") // 2
    side = lax.axis_index("expert") % 2
    slots = new_ref.shape[0]
    experts = home_ref.shape[0]
    for copy in copies[:-1]:
        copy.wait()
    picks = jnp.concatenate([ids_ref[...], reps_ref[...]], axis=0)
    picks_ref[...] = picks
    row = lax.broadcasted_iota(jnp.int32, table_ref.shape, 0)
    lane = lax.broadcasted_iota(jnp.int32, table_ref.shape, 1)
    table = jnp.zeros(table_ref.shape, jnp.int32)
    for expert in range(experts):
        table = jnp.where((row == 0) & (lane == expert), home_ref[expert], table)
    for at in range(2 * SQUARE):
        slot = 2 * (chip ^ peer_of(jnp.int32(at // 2), side)) + at % 2
        mine = new_ref[slot]
        rank = jnp.int32(0)
        for other in range(slots):
            rank = rank + ((new_ref[other] == mine) & (slot > other)).astype(jnp.int32)
        table = jnp.where((row == 1) & (lane == at), mine, table)
        table = jnp.where((row == 2) & (lane == at), rank, table)
    table_ref[...] = table

    def rows():
        copies[-1].wait()
        return x_ref[...]

    pick(cap, table, picks, rows, blocks, sel_ref, experts)


def pick_far_kernel(cap, experts, table_ref, x_ref, picks_ref, *refs):
    blocks, sel_ref = refs[:SQUARE], refs[SQUARE]
    pick(cap, table_ref[...], picks_ref[...], lambda: x_ref[...], blocks, sel_ref, experts)


def pick_shapes(cap, x, batches):
    high = block_rows(batches, cap)
    count, width = x.shape
    lanes = block_lanes(batches * cap, width) + LANES
    block = jax.ShapeDtypeStruct((TILE, lanes), jnp.bfloat16)
    sel = jax.ShapeDtypeStruct((SQUARE * high, count), jnp.bfloat16)
    cost = pl.CostEstimate(
        flops=2 * SQUARE * high * count * width,
        bytes_accessed=4 * SQUARE * high * width,
        transcendentals=0,
    )
    return [block] * SQUARE + [sel], cost


def pick_own(cap, home, new, x, ids, reps):
    batches, tokens = ids.shape
    shapes, cost = pick_shapes(cap, x, batches)
    shapes += [
        jax.ShapeDtypeStruct((8, LANES), jnp.int32),
        jax.ShapeDtypeStruct((2 * batches, tokens), jnp.int32),
        jax.ShapeDtypeStruct((8, LANES), jnp.float32),
    ]
    return pl.pallas_call(
        functools.partial(pick_own_kernel, cap),
        out_shape=shapes,
        in_specs=[pl.BlockSpec(memory_space=HBM)] * 5,
        out_specs=[pl.BlockSpec(memory_space=VMEM)] * len(shapes),
        scratch_shapes=[
            SMEM(home.shape, jnp.int32),
            SMEM(new.shape, jnp.int32),
            VMEM(x.shape, x.dtype),
            VMEM(ids.shape, ids.dtype),
            VMEM(reps.shape, reps.dtype),
            pltpu.SemaphoreType.DMA((5,)),
        ],
        cost_estimate=cost,
        compiler_params=pltpu.CompilerParams(vmem_limit_bytes=SMALL),
    )(*(pltpu.with_memory_space_constraint(value, HBM) for value in (home, new, x, ids, reps)))


def pick_far(cap, experts, table, x, picks):
    shapes, cost = pick_shapes(cap, x, picks.shape[0] // 2)
    return pl.pallas_call(
        functools.partial(pick_far_kernel, cap, experts),
        out_shape=shapes,
        in_specs=[pl.BlockSpec(memory_space=VMEM)] * 3,
        out_specs=[pl.BlockSpec(memory_space=VMEM)] * (SQUARE + 1),
        cost_estimate=cost,
        compiler_params=pltpu.CompilerParams(vmem_limit_bytes=SMALL),
    )(table, x, picks)


def expert_kernel(count, stream, *refs):
    blocks, panels, prior_ref = refs[:SQUARE], refs[SQUARE : SQUARE + 6], refs[SQUARE + 6]
    outs, load_ref = refs[SQUARE + 7 : 2 * SQUARE + 7], refs[2 * SQUARE + 7]
    own, copies = list(panels[:3]), {}
    if stream:
        *held, sem = refs[2 * SQUARE + 8 :]
        for index, target in enumerate(held):
            own[index] = target
            copies[index] = pltpu.make_async_copy(panels[index], target, sem.at[index])
            copies[index].start()

    def ready(own_half, place):
        if own_half and place in copies:
            copies[place].wait()

    x = stacked(count, panels[0].shape[1], blocks)
    high = x.shape[0] // SQUARE
    contract = (((1,), (1,)), ((), ()))
    load = prior_ref[...]
    for block in blocks:
        load = load + block[:, block.shape[1] - LANES :].astype(jnp.float32)
    load_ref[...] = load
    total = None
    for own_half, (gate_ref, up_ref, down_ref) in enumerate((panels[3:], own)):
        ready(own_half, 0)
        gate = jnp.dot(x, gate_ref[0], preferred_element_type=jnp.float32)
        ready(own_half, 1)
        up = jnp.dot(x, up_ref[0], preferred_element_type=jnp.float32)
        hidden = (gate / (1.0 + jnp.exp(-gate)) * up).astype(jnp.bfloat16)
        ready(own_half, 2)
        part = lax.dot_general(hidden, down_ref[0], contract, preferred_element_type=jnp.float32)
        total = part if total is None else total + part
    for q in range(SQUARE):
        packed(count, total[q * high : (q + 1) * high], outs[q])


def run_expert(count, stream, blocks, panels, panels_far, prior):
    width, half = panels[0].shape[1:]
    rows = SQUARE * count
    block = jax.ShapeDtypeStruct((TILE, block_lanes(count, width)), jnp.bfloat16)
    shapes = [block] * SQUARE + [jax.ShapeDtypeStruct(prior.shape, prior.dtype)]
    places = [VMEM] * (SQUARE + 7)
    scratch = []
    if stream:
        panels = [pltpu.with_memory_space_constraint(panel, HBM) for panel in panels]
        shapes += [jax.ShapeDtypeStruct(panel.shape, panel.dtype) for panel in panels]
        places[SQUARE : SQUARE + 3] = [HBM] * len(panels)
        scratch.append(pltpu.SemaphoreType.DMA((len(panels),)))
    return pl.pallas_call(
        functools.partial(expert_kernel, count, stream),
        out_shape=shapes,
        in_specs=[pl.BlockSpec(memory_space=place) for place in places],
        out_specs=[pl.BlockSpec(memory_space=VMEM)] * len(shapes),
        scratch_shapes=scratch,
        cost_estimate=pl.CostEstimate(
            flops=2 * rows * width * half * 6,
            bytes_accessed=6 * 2 * width * half + 4 * rows * width,
            transcendentals=2 * rows * half,
        ),
        compiler_params=pltpu.CompilerParams(vmem_limit_bytes=LARGE),
    )(*blocks, *panels, *panels_far, prior)


def chosen(count, width, sel_ref, blocks):
    y = stacked(count, width, blocks)
    return lax.dot_general(
        sel_ref[...], y, (((0,), (0,)), ((), ())), preferred_element_type=jnp.float32
    )


def merge_kernel(count, sel_ref, *refs):
    width = refs[SQUARE].shape[1]
    refs[SQUARE][...] = chosen(count, width, sel_ref, refs[:SQUARE]).astype(jnp.bfloat16)


def merge_own_kernel(count, sel_ref, weight_ref, *refs):
    out_ref, scale_ref = refs[SQUARE:]
    width = out_ref.shape[1]
    out_ref[...] = chosen(count, width, sel_ref, refs[:SQUARE]).astype(jnp.bfloat16)
    batches, tokens = weight_ref.shape
    lane = lax.broadcasted_iota(jnp.int32, (tokens, tokens), 0)
    same = lane == lax.broadcasted_iota(jnp.int32, (tokens, tokens), 1)
    for batch in range(batches):
        column = jnp.where(same, weight_ref[batch : batch + 1, :], 0.0)
        column = jnp.sum(column, axis=1, keepdims=True)
        scale_ref[batch * tokens : (batch + 1) * tokens, :] = jnp.broadcast_to(
            column, (tokens, LANES)
        )


def final_kernel(own_ref, scale_ref, load_ref, load_far_ref, back_ref, out_ref, slot_ref):
    core = lax.axis_index("expert") % 2
    both = load_ref[...] + load_far_ref[...]
    row = lax.broadcasted_iota(jnp.int32, both.shape, 0)
    lane = lax.broadcasted_iota(jnp.int32, both.shape, 1)
    slot_ref[0] = jnp.sum(jnp.where((row == 0) & (lane == core), both, 0.0)).astype(
        jnp.int32
    )
    total = own_ref[...].astype(jnp.float32) + back_ref[...].astype(jnp.float32)
    out_ref[...] = (total * scale_ref[:, :1]).astype(jnp.bfloat16)


def small_call(kernel, shapes, *operands, slot=False):
    specs = [pl.BlockSpec(memory_space=VMEM)] * len(shapes)
    if slot:
        shapes = shapes + [jax.ShapeDtypeStruct((1,), jnp.int32)]
        specs = specs + [pl.BlockSpec(memory_space=SMEM)]
    return pl.pallas_call(
        kernel,
        out_shape=shapes,
        in_specs=[pl.BlockSpec(memory_space=VMEM)] * len(operands),
        out_specs=specs,
        cost_estimate=pl.CostEstimate(
            flops=2 * sum(shape.size for shape in shapes) * LANES,
            bytes_accessed=2 * sum(operand.size for operand in operands),
            transcendentals=0,
        ),
        compiler_params=pltpu.CompilerParams(vmem_limit_bytes=SMALL),
    )(*operands)


def swapped(size, bits):
    return [(index, index ^ bits[index % 2]) for index in range(size)]


def dispatched(
    activations,
    pick_weight,
    expert_ids,
    replica,
    old_home,
    new_expert,
    gate_panel,
    up_panel,
    down_panel,
):
    size = lax.axis_size("expert")
    batches, tokens, width = activations.shape
    rows = batches * tokens
    cap = min(CAP * REPL, tokens)
    count = batches * cap
    distant = (2 * SQUARE, 2 * SQUARE)
    beside = (1, 1)

    def swap(value, bits):
        return lax.ppermute(value, "expert", swapped(size, bits))

    def around(blocks):
        return [blocks[0]] + [
            swap(blocks[q], [2 * order[q] for order in PEERS])
            for q in range(1, SQUARE)
        ]

    x = activations.reshape(rows, width)
    x_far = swap(x, distant)
    panels = (gate_panel, up_panel, down_panel)
    panels_far = [swap(panel, beside) for panel in panels]
    *blocks, sel, table, picks, zero = pick_own(
        cap,
        old_home,
        new_expert,
        x,
        expert_ids.reshape(batches, tokens),
        replica.reshape(batches, tokens),
    )
    picks_far = swap(picks, distant)
    blocks = around(blocks)
    *blocks_far, sel_far = pick_far(cap, old_home.shape[0], table, x_far, picks_far)
    blocks_far = around(blocks_far)
    made = run_expert(count, True, blocks, panels, panels_far, zero)
    results, load, panels = made[:SQUARE], made[SQUARE], made[SQUARE + 1 :]
    *results_far, load = run_expert(count, False, blocks_far, panels, panels_far, load)
    results_far = around(results_far)
    results = around(results)
    load_far = swap(load, beside)
    whole = jax.ShapeDtypeStruct((rows, width), jnp.bfloat16)
    (far,) = small_call(functools.partial(merge_kernel, count), [whole], sel_far, *results_far)
    back = swap(far, distant)
    weight = pick_weight.reshape(batches, tokens)
    own, scale = small_call(
        functools.partial(merge_own_kernel, count),
        [whole, jax.ShapeDtypeStruct((rows, LANES), jnp.float32)],
        sel,
        weight,
        *results,
    )
    output, slot_load = small_call(
        final_kernel,
        [whole],
        own,
        scale,
        load,
        load_far,
        back,
        slot=True,
    )
    return output.reshape(batches, tokens, width), slot_load


def solution(mesh):
    chips = mesh.shape["expert"] // 2

    def per_device(*args):
        if direct(args):
            return dispatched(*args)
        return gathered(*args)

    def direct(args):
        return chips == 2 * SQUARE and args[2].shape[2] == 1

    return jax.shard_map(
        per_device,
        mesh=mesh,
        in_specs=(
            P(None, ("groups", "expert"), None),
            P(None, ("groups", "expert"), None),
            P(None, ("groups", "expert"), None),
            P(None, ("groups", "expert"), None),
            P(),
            P("groups"),
            P("expert", None, None),
            P("expert", None, None),
            P("expert", None, None),
        ),
        out_specs=(P(None, ("groups", "expert"), None), P(("groups", "expert"))),
        check_vma=False,
    )
```

```python
import functools

import jax
import jax.numpy as jnp
from jax import lax
from jax.experimental import pallas as pl
from jax.experimental.pallas import tpu as pltpu
from jax.sharding import PartitionSpec as P


CAP = 2
REPL = 5
LANES = 128
SQUARE = 4
TILE = 8
PEERS = ((0, 1, 2, 3), (0, 3, 1, 2))
SMALL = 4 << 20
LARGE = 20 << 20
VMEM = pltpu.VMEM
SMEM = pltpu.SMEM
HBM = pltpu.MemorySpace.HBM


def slot_rank(new_expert, me):
    positions = jnp.arange(new_expert.shape[0], dtype=jnp.int32)
    mine = jnp.sum(jnp.where(positions == me, new_expert, 0))
    rank = jnp.sum(((new_expert == mine) & (positions < me)).astype(jnp.int32))
    return mine, rank


def gathered(
    activations,
    pick_weight,
    expert_ids,
    replica,
    old_home,
    new_expert,
    gate_panel,
    up_panel,
    down_panel,
):
    me = lax.axis_index("expert")
    batches, tokens, width = activations.shape
    top = expert_ids.shape[2]
    rows = batches * tokens
    x = activations.reshape(rows, width)
    picks = jnp.concatenate([expert_ids.reshape(rows, top), replica.reshape(rows, top)], axis=1)
    weights = pick_weight.reshape(rows, top)
    picks_all = lax.all_gather(picks, "expert", axis=0, tiled=True)
    weights_all = lax.all_gather(weights, "expert", axis=0, tiled=True)
    x_all = lax.all_gather(x, "expert", axis=0, tiled=True)
    ids_all = picks_all[:, :top]
    rep_all = picks_all[:, top:]
    mine, rank = slot_rank(new_expert, me)
    load = jnp.sum(((ids_all == mine) & (rep_all == rank)).astype(jnp.int32))
    labels = jnp.arange(old_home.shape[0], dtype=jnp.int32)
    held = jnp.sum(jnp.where(old_home == me // 2, labels, 0))
    scale = jnp.sum(jnp.where(ids_all == held, weights_all, 0.0), axis=1, keepdims=True)
    gate = jnp.dot(x_all, gate_panel[0], preferred_element_type=jnp.float32)
    up = jnp.dot(x_all, up_panel[0], preferred_element_type=jnp.float32)
    hidden = (jax.nn.silu(gate) * up).astype(jnp.bfloat16)
    part = lax.dot_general(
        hidden, down_panel[0], (((1,), (1,)), ((), ())), preferred_element_type=jnp.float32
    )
    part = (part * scale).astype(jnp.bfloat16)
    total = lax.psum_scatter(part, "expert", scatter_dimension=0, tiled=True)
    return total.reshape(batches, tokens, width), load.reshape(1)


def steps(index, size, count):
    whole = jnp.zeros_like(index)
    for step in range(1, count):
        whole = whole + (index >= step * size).astype(jnp.int32)
    return whole


def peer_of(slot, core):
    value = jnp.zeros_like(slot)
    for index in range(1, SQUARE):
        peer = jnp.where(core == 0, PEERS[0][index], PEERS[1][index])
        value = jnp.where(slot == index, peer, value)
    return value


def tiling(count):
    full, rest = divmod(count, TILE)
    fold = TILE // rest if rest and TILE % rest == 0 else 1
    if rest and fold == 1:
        full, rest = full + 1, 0
    return full, rest, fold


def block_rows(batches, cap):
    return -(-batches * cap // TILE) * TILE


def block_lanes(count, width):
    full, rest, fold = tiling(count)
    return full * width + (width // fold if rest else 0)


def packed(count, rows, ref):
    full, rest, fold = tiling(count)
    width = rows.shape[1]
    for tile in range(full):
        part = rows[tile * TILE : (tile + 1) * TILE]
        ref[:, tile * width : (tile + 1) * width] = part.astype(ref.dtype)
    if rest:
        tail = rows[full * TILE : (full + 1) * TILE]
        piece = width // fold
        turn = steps(lax.broadcasted_iota(jnp.int32, (TILE, piece), 0), rest, fold)
        value = tail[:, :piece]
        for index in range(1, fold):
            moved = pltpu.roll(tail[:, index * piece : (index + 1) * piece], index * rest, axis=0)
            value = jnp.where(turn == index, moved, value)
        ref[:, full * width : full * width + piece] = value.astype(ref.dtype)


def unpacked(count, width, ref):
    full, rest, fold = tiling(count)
    tiles = [ref[:, tile * width : (tile + 1) * width] for tile in range(full)]
    if rest:
        piece = width // fold
        tail = ref[:, full * width : full * width + piece].astype(jnp.float32)
        parts = [tail]
        for index in range(1, fold):
            parts.append(pltpu.roll(tail, TILE - index * rest, axis=0))
        tiles.append(jnp.concatenate(parts, axis=1).astype(ref.dtype))
    return tiles


def stacked(count, width, refs):
    tiles = [tile for ref in refs for tile in unpacked(count, width, ref)]
    return jnp.concatenate(tiles, axis=0)


def pick(cap, table, picks, x, blocks, sel_ref, experts):
    batches, tokens = picks.shape[0] // 2, picks.shape[1]
    count = batches * tokens
    high = block_rows(batches, cap)
    chip = lax.axis_index("expert") // 2
    side = lax.axis_index("expert") % 2

    def batch_of(index):
        return steps(index, tokens, batches)

    col = lax.broadcasted_iota(jnp.int32, (tokens, count), 1)
    spread = col - tokens * batch_of(col) == lax.broadcasted_iota(jnp.int32, (tokens, count), 0)
    spread = spread.astype(jnp.float32)
    own_lane = batch_of(lax.broadcasted_iota(jnp.int32, (batches, count), 1))
    own_lane = own_lane == lax.broadcasted_iota(jnp.int32, (batches, count), 0)

    def row_of(values):
        wide = jnp.dot(values.astype(jnp.float32), spread, preferred_element_type=jnp.float32)
        return jnp.sum(jnp.where(own_lane, wide, 0.0), axis=0, keepdims=True).astype(jnp.int32)

    ids = row_of(picks[:batches, :])
    reps = row_of(picks[batches:, :])
    target = jnp.zeros_like(ids)
    for expert in range(experts):
        target = jnp.where(ids == expert, table[0:1, expert : expert + 1], target)

    sub = lax.broadcasted_iota(jnp.int32, (8, count), 0)
    inside = (target == (sub ^ chip)) & (sub < SQUARE)
    before_from = lax.broadcasted_iota(jnp.int32, (count, count), 0)
    before_to = lax.broadcasted_iota(jnp.int32, (count, count), 1)
    before = (before_from < before_to) & (batch_of(before_from) == batch_of(before_to))
    earlier = jnp.dot(
        inside.astype(jnp.bfloat16),
        before.astype(jnp.bfloat16),
        preferred_element_type=jnp.float32,
    )
    position = jnp.sum(jnp.where(inside, earlier, 0.0), axis=0, keepdims=True).astype(jnp.int32)

    row = lax.broadcasted_iota(jnp.int32, (SQUARE * high, count), 0)
    peer = steps(row, high, SQUARE)
    left = row - high * peer
    peer = peer_of(peer, side)
    group = steps(left, cap, batches + 1)
    left = left - cap * group
    lane = batch_of(lax.broadcasted_iota(jnp.int32, (SQUARE * high, count), 1))
    sel = ((target == (peer ^ chip)) & (position == left) & (group == lane)).astype(jnp.bfloat16)
    sel_ref[...] = sel
    meta_lane = lax.broadcasted_iota(jnp.int32, (TILE, LANES), 1)
    x = x()
    for q in range(SQUARE):
        part = jnp.dot(sel[q * high : (q + 1) * high], x, preferred_element_type=jnp.float32)
        meta = jnp.zeros((TILE, LANES), jnp.float32)
        for core in range(2):
            at = 2 * q + core
            hits = (ids == table[1:2, at : at + 1]) & (reps == table[2:3, at : at + 1])
            load = jnp.sum(hits.astype(jnp.float32), axis=1, keepdims=True)
            meta = jnp.where(meta_lane == core, load, meta)
        packed(batches * cap, part, blocks[q])
        blocks[q][:, blocks[q].shape[1] - LANES :] = meta.astype(jnp.bfloat16)


def pick_own_kernel(cap, home_hbm, new_hbm, x_hbm, ids_hbm, reps_hbm, *refs):
    blocks, (sel_ref, table_ref, picks_ref, zero_ref) = refs[:SQUARE], refs[SQUARE : SQUARE + 4]
    home_ref, new_ref, x_ref, ids_ref, reps_ref, sem = refs[SQUARE + 4 :]
    sources = (home_hbm, new_hbm, ids_hbm, reps_hbm, x_hbm)
    targets = (home_ref, new_ref, ids_ref, reps_ref, x_ref)
    copies = [
        pltpu.make_async_copy(source, target, sem.at[index])
        for index, (source, target) in enumerate(zip(sources, targets))
    ]
    for copy in copies:
        copy.start()
    zero_ref[...] = jnp.zeros(zero_ref.shape, zero_ref.dtype)
    chip = lax.axis_index("expert") // 2
    side = lax.axis_index("expert") % 2
    slots = new_ref.shape[0]
    experts = home_ref.shape[0]
    for copy in copies[:-1]:
        copy.wait()
    picks = jnp.concatenate([ids_ref[...], reps_ref[...]], axis=0)
    picks_ref[...] = picks
    row = lax.broadcasted_iota(jnp.int32, table_ref.shape, 0)
    lane = lax.broadcasted_iota(jnp.int32, table_ref.shape, 1)
    table = jnp.zeros(table_ref.shape, jnp.int32)
    for expert in range(experts):
        table = jnp.where((row == 0) & (lane == expert), home_ref[expert], table)
    pair = peer_of(steps(lane, 2, SQUARE), side)
    slot = 2 * (chip ^ pair) + lane % 2
    mine = jnp.zeros(table_ref.shape, jnp.int32)
    for other in range(slots):
        mine = jnp.where(slot == other, new_ref[other], mine)
    rank = jnp.zeros(table_ref.shape, jnp.int32)
    for other in range(slots):
        rank = rank + ((new_ref[other] == mine) & (slot > other)).astype(jnp.int32)
    table = jnp.where((row == 1) & (lane < 2 * SQUARE), mine, table)
    table = jnp.where((row == 2) & (lane < 2 * SQUARE), rank, table)
    table_ref[...] = table

    def rows():
        copies[-1].wait()
        return x_ref[...]

    pick(cap, table, picks, rows, blocks, sel_ref, experts)


def pick_far_kernel(cap, experts, table_ref, x_ref, picks_ref, *refs):
    blocks, sel_ref = refs[:SQUARE], refs[SQUARE]
    pick(cap, table_ref[...], picks_ref[...], lambda: x_ref[...], blocks, sel_ref, experts)


def pick_shapes(cap, x, batches):
    high = block_rows(batches, cap)
    count, width = x.shape
    lanes = block_lanes(batches * cap, width) + LANES
    block = jax.ShapeDtypeStruct((TILE, lanes), jnp.bfloat16)
    sel = jax.ShapeDtypeStruct((SQUARE * high, count), jnp.bfloat16)
    cost = pl.CostEstimate(
        flops=2 * SQUARE * high * count * width,
        bytes_accessed=4 * SQUARE * high * width,
        transcendentals=0,
    )
    return [block] * SQUARE + [sel], cost


def pick_own(cap, home, new, x, ids, reps):
    batches, tokens = ids.shape
    shapes, cost = pick_shapes(cap, x, batches)
    shapes += [
        jax.ShapeDtypeStruct((8, LANES), jnp.int32),
        jax.ShapeDtypeStruct((2 * batches, tokens), jnp.int32),
        jax.ShapeDtypeStruct((8, LANES), jnp.float32),
    ]
    return pl.pallas_call(
        functools.partial(pick_own_kernel, cap),
        out_shape=shapes,
        in_specs=[pl.BlockSpec(memory_space=HBM)] * 5,
        out_specs=[pl.BlockSpec(memory_space=VMEM)] * len(shapes),
        scratch_shapes=[
            SMEM(home.shape, jnp.int32),
            SMEM(new.shape, jnp.int32),
            VMEM(x.shape, x.dtype),
            VMEM(ids.shape, ids.dtype),
            VMEM(reps.shape, reps.dtype),
            pltpu.SemaphoreType.DMA((5,)),
        ],
        cost_estimate=cost,
        compiler_params=pltpu.CompilerParams(vmem_limit_bytes=SMALL),
    )(*(pltpu.with_memory_space_constraint(value, HBM) for value in (home, new, x, ids, reps)))


def pick_far(cap, experts, table, x, picks):
    shapes, cost = pick_shapes(cap, x, picks.shape[0] // 2)
    return pl.pallas_call(
        functools.partial(pick_far_kernel, cap, experts),
        out_shape=shapes,
        in_specs=[pl.BlockSpec(memory_space=VMEM)] * 3,
        out_specs=[pl.BlockSpec(memory_space=VMEM)] * (SQUARE + 1),
        cost_estimate=cost,
        compiler_params=pltpu.CompilerParams(vmem_limit_bytes=SMALL),
    )(table, x, picks)


def expert_kernel(count, stream, *refs):
    blocks, panels, prior_ref = refs[:SQUARE], refs[SQUARE : SQUARE + 6], refs[SQUARE + 6]
    outs, load_ref = refs[SQUARE + 7 : 2 * SQUARE + 7], refs[2 * SQUARE + 7]
    own, copies = list(panels[:3]), {}
    if stream:
        *held, sem = refs[2 * SQUARE + 8 :]
        for index, target in enumerate(held):
            own[index] = target
            copies[index] = pltpu.make_async_copy(panels[index], target, sem.at[index])
            copies[index].start()

    def ready(own_half, place):
        if own_half and place in copies:
            copies[place].wait()

    x = stacked(count, panels[0].shape[1], blocks)
    high = x.shape[0] // SQUARE
    contract = (((1,), (1,)), ((), ()))
    load = prior_ref[...]
    for block in blocks:
        load = load + block[:, block.shape[1] - LANES :].astype(jnp.float32)
    load_ref[...] = load
    total = None
    for own_half, (gate_ref, up_ref, down_ref) in enumerate((panels[3:], own)):
        ready(own_half, 0)
        gate = jnp.dot(x, gate_ref[0], preferred_element_type=jnp.float32)
        ready(own_half, 1)
        up = jnp.dot(x, up_ref[0], preferred_element_type=jnp.float32)
        hidden = (gate / (1.0 + jnp.exp(-gate)) * up).astype(jnp.bfloat16)
        ready(own_half, 2)
        part = lax.dot_general(hidden, down_ref[0], contract, preferred_element_type=jnp.float32)
        total = part if total is None else total + part
    for q in range(SQUARE):
        packed(count, total[q * high : (q + 1) * high], outs[q])


def run_expert(count, stream, blocks, panels, panels_far, prior):
    width, half = panels[0].shape[1:]
    rows = SQUARE * count
    block = jax.ShapeDtypeStruct((TILE, block_lanes(count, width)), jnp.bfloat16)
    shapes = [block] * SQUARE + [jax.ShapeDtypeStruct(prior.shape, prior.dtype)]
    places = [VMEM] * (SQUARE + 7)
    scratch = []
    if stream:
        panels = [pltpu.with_memory_space_constraint(panel, HBM) for panel in panels]
        shapes += [jax.ShapeDtypeStruct(panel.shape, panel.dtype) for panel in panels]
        places[SQUARE : SQUARE + 3] = [HBM] * len(panels)
        scratch.append(pltpu.SemaphoreType.DMA((len(panels),)))
    return pl.pallas_call(
        functools.partial(expert_kernel, count, stream),
        out_shape=shapes,
        in_specs=[pl.BlockSpec(memory_space=place) for place in places],
        out_specs=[pl.BlockSpec(memory_space=VMEM)] * len(shapes),
        scratch_shapes=scratch,
        cost_estimate=pl.CostEstimate(
            flops=2 * rows * width * half * 6,
            bytes_accessed=6 * 2 * width * half + 4 * rows * width,
            transcendentals=2 * rows * half,
        ),
        compiler_params=pltpu.CompilerParams(vmem_limit_bytes=LARGE),
    )(*blocks, *panels, *panels_far, prior)


def chosen(count, width, sel_ref, blocks):
    y = stacked(count, width, blocks)
    return lax.dot_general(
        sel_ref[...], y, (((0,), (0,)), ((), ())), preferred_element_type=jnp.float32
    )


def merge_kernel(count, sel_ref, *refs):
    width = refs[SQUARE].shape[1]
    refs[SQUARE][...] = chosen(count, width, sel_ref, refs[:SQUARE]).astype(jnp.bfloat16)


def merge_own_kernel(count, sel_ref, weight_ref, *refs):
    out_ref, scale_ref = refs[SQUARE:]
    width = out_ref.shape[1]
    out_ref[...] = chosen(count, width, sel_ref, refs[:SQUARE]).astype(jnp.bfloat16)
    batches, tokens = weight_ref.shape
    lane = lax.broadcasted_iota(jnp.int32, (tokens, tokens), 0)
    same = lane == lax.broadcasted_iota(jnp.int32, (tokens, tokens), 1)
    for batch in range(batches):
        column = jnp.where(same, weight_ref[batch : batch + 1, :], 0.0)
        column = jnp.sum(column, axis=1, keepdims=True)
        scale_ref[batch * tokens : (batch + 1) * tokens, :] = jnp.broadcast_to(
            column, (tokens, LANES)
        )


def final_kernel(own_ref, scale_ref, load_ref, load_far_ref, back_ref, out_ref, slot_ref):
    core = lax.axis_index("expert") % 2
    both = load_ref[...] + load_far_ref[...]
    row = lax.broadcasted_iota(jnp.int32, both.shape, 0)
    lane = lax.broadcasted_iota(jnp.int32, both.shape, 1)
    slot_ref[0] = jnp.sum(jnp.where((row == 0) & (lane == core), both, 0.0)).astype(
        jnp.int32
    )
    total = own_ref[...].astype(jnp.float32) + back_ref[...].astype(jnp.float32)
    out_ref[...] = (total * scale_ref[:, :1]).astype(jnp.bfloat16)


def small_call(kernel, shapes, *operands, slot=False):
    specs = [pl.BlockSpec(memory_space=VMEM)] * len(shapes)
    if slot:
        shapes = shapes + [jax.ShapeDtypeStruct((1,), jnp.int32)]
        specs = specs + [pl.BlockSpec(memory_space=SMEM)]
    return pl.pallas_call(
        kernel,
        out_shape=shapes,
        in_specs=[pl.BlockSpec(memory_space=VMEM)] * len(operands),
        out_specs=specs,
        cost_estimate=pl.CostEstimate(
            flops=2 * sum(shape.size for shape in shapes) * LANES,
            bytes_accessed=2 * sum(operand.size for operand in operands),
            transcendentals=0,
        ),
        compiler_params=pltpu.CompilerParams(vmem_limit_bytes=SMALL),
    )(*operands)


def swapped(size, bits):
    return [(index, index ^ bits[index % 2]) for index in range(size)]


def dispatched(
    activations,
    pick_weight,
    expert_ids,
    replica,
    old_home,
    new_expert,
    gate_panel,
    up_panel,
    down_panel,
):
    size = lax.axis_size("expert")
    batches, tokens, width = activations.shape
    rows = batches * tokens
    cap = min(CAP * REPL, tokens)
    count = batches * cap
    distant = (2 * SQUARE, 2 * SQUARE)
    beside = (1, 1)

    def swap(value, bits):
        return lax.ppermute(value, "expert", swapped(size, bits))

    def around(blocks):
        return [blocks[0]] + [
            swap(blocks[q], [2 * order[q] for order in PEERS])
            for q in range(1, SQUARE)
        ]

    x = activations.reshape(rows, width)
    x_far = swap(x, distant)
    panels = (gate_panel, up_panel, down_panel)
    panels_far = [swap(panel, beside) for panel in panels]
    *blocks, sel, table, picks, zero = pick_own(
        cap,
        old_home,
        new_expert,
        x,
        expert_ids.reshape(batches, tokens),
        replica.reshape(batches, tokens),
    )
    picks_far = swap(picks, distant)
    blocks = around(blocks)
    *blocks_far, sel_far = pick_far(cap, old_home.shape[0], table, x_far, picks_far)
    blocks_far = around(blocks_far)
    made = run_expert(count, True, blocks, panels, panels_far, zero)
    results, load, panels = made[:SQUARE], made[SQUARE], made[SQUARE + 1 :]
    *results_far, load = run_expert(count, False, blocks_far, panels, panels_far, load)
    results_far = around(results_far)
    results = around(results)
    load_far = swap(load, beside)
    whole = jax.ShapeDtypeStruct((rows, width), jnp.bfloat16)
    (far,) = small_call(functools.partial(merge_kernel, count), [whole], sel_far, *results_far)
    back = swap(far, distant)
    weight = pick_weight.reshape(batches, tokens)
    own, scale = small_call(
        functools.partial(merge_own_kernel, count),
        [whole, jax.ShapeDtypeStruct((rows, LANES), jnp.float32)],
        sel,
        weight,
        *results,
    )
    output, slot_load = small_call(
        final_kernel,
        [whole],
        own,
        scale,
        load,
        load_far,
        back,
        slot=True,
    )
    return output.reshape(batches, tokens, width), slot_load


def solution(mesh):
    chips = mesh.shape["expert"] // 2

    def per_device(*args):
        if direct(args):
            return dispatched(*args)
        return gathered(*args)

    def direct(args):
        return chips == 2 * SQUARE and args[2].shape[2] == 1

    return jax.shard_map(
        per_device,
        mesh=mesh,
        in_specs=(
            P(None, ("groups", "expert"), None),
            P(None, ("groups", "expert"), None),
            P(None, ("groups", "expert"), None),
            P(None, ("groups", "expert"), None),
            P(),
            P("groups"),
            P("expert", None, None),
            P("expert", None, None),
            P("expert", None, None),
        ),
        out_specs=(P(None, ("groups", "expert"), None), P(("groups", "expert"))),
        check_vma=False,
    )
```
